256 devices in a mesh: gx: 16 (over z, core), gy: 16 (over y, x).
Axes of the slice: x: 4, y: 4, z: 8, core: 2. Of those that a mesh axis runs over, the one named last changes fastest.
Arguments:
- latent_noise: float32 [1024, 65536], P('gx', 'gy'), may hold values from -6 to 6
- kappa_sq: float32 [1024, 1024], P('gx', 'gy'), may hold values from 0.25 to 4
- obs_cell: int32 [65536], P(('gx', 'gy')), may hold values from 0 to 4095
- obs_value: float32 [65536], P(('gx', 'gy')), may hold values from -6 to 6
- obs_var: float32 [65536], P(('gx', 'gy')), may hold values from 0.1 to 1
Outputs:
- latent_new: float32 [1024, 65536], P('gx', 'gy')
- prior_field: float32 [1024, 65536], P('gx', 'gy')
The draws below stay inside these ranges and needn't reach their ends.
Inputs may be any that keep to these rules, and one draw needn't show every extreme that they name: obs_cell[j] is a cell of the block held by device j // 256 in the order of gx+gy (gx slowest), written as row * 64 + column within that block.
All inputs are finite; a program needn't handle non-finite values.
Results may differ from the reference program's by a relative error of at most 0.0001.
Values sent between devices are 32-bit elements; how exact they have to be, the bound alone decides.
No kernel may reach another device: no remote copies, remote signals or barrier semaphores. Data moves between devices by JAX's collectives and lax.ppermute only.
A program may use at most 64 MiB of HBM per device.

```python
import math
import jax
import jax.numpy as jnp
import numpy as np
from jax import lax

CX = 64
CY = 64
MEMBERS = 64
SWEEPS = 4
OBS_DEV = 256
NX = 1024
NY = 1024
NOBS = 65536
N_GY = 16


def touch_ends(array, key, low, largest):
    shape = array.shape
    index_at = [jax.random.randint(jax.random.fold_in(key, axis), (), 0, shape[axis]) for axis in range(len(shape))]
    array = array.at[tuple(index_at)].set(low)
    longest = shape.index(max(shape))
    index_at[longest] = (index_at[longest] + 1) % shape[longest]
    return array.at[tuple(index_at)].set(largest)


def block_scale(key, dims, shards, smallest, top_value):
    level = 1.0
    for dim, shards_of in shards:
        steps = jax.random.uniform(jax.random.fold_in(jax.random.fold_in(key, 6), dim), (shards_of,), jnp.float32, smallest / len(shards), top_value / len(shards))
        level = level * jnp.repeat(jnp.exp(steps), dims[dim] // shards_of).reshape((-1,) + (1,) * (len(dims) - 1 - dim))
    return level


def scatter_about(key, dims, width, reach, pieces=(), kind=jnp.bfloat16):
    entries = jax.random.normal(key, dims, jnp.float32) * width
    if len(pieces) > 0:
        entries = block_scale(key, dims, pieces, -0.22, 0.18) * entries
    return jnp.clip(entries, min=-reach, max=reach).astype(kind)


def setup_inputs(seed: int = 0) -> dict:
    keys = jax.random.split(jax.random.key(seed), 6)
    return {
        "latent_noise": scatter_about(keys[0], (NX, NY * MEMBERS), 1.0, 6.0, ((0, 16), (1, 16)), jnp.float32),
        "kappa_sq": jnp.clip(jnp.exp(math.log(4.0) - 2.7725887 * jax.random.uniform(keys[1], (NX, NY), jnp.float32) ** block_scale(keys[1], (NX, NY), ((0, 16), (1, 16)), -0.2, 0.2)), 0.25, 4.0),
        "obs_cell": touch_ends(jax.random.randint(keys[2], (NOBS,), 0, CX * CY), jax.random.fold_in(keys[2], 1), 0, (CX * CY) - 1).astype(jnp.int32),
        "obs_value": scatter_about(keys[3], (NOBS,), 1.0, 6.0, ((0, 256),), jnp.float32),
        "obs_var": jnp.clip(jnp.exp(math.log(1.0) - 2.3025851 * jax.random.uniform(keys[4], (NOBS,), jnp.float32) ** block_scale(keys[4], (NOBS,), ((0, 256),), -0.2, 0.2)), 0.1, 1.0),
    }


LOWER_EDGE = 0.25
UPPER_EDGE = 12.0

def cheb_coeffs(terms):
    angles = np.pi * (np.arange(64) + 0.5) / 64.0
    nodes = 0.5 * (UPPER_EDGE + LOWER_EDGE) + 0.5 * (UPPER_EDGE - LOWER_EDGE) * np.cos(angles)
    values = []
    for order in range(terms):
        coeff = 2.0 / 64.0 * np.sum(np.cos(order * angles) / nodes)
        if order == 0:
            coeff = 0.5 * coeff
        values.append(float(coeff))
    return values

def chol_solve(factor, rhs):
    lower_sol = lax.linalg.triangular_solve(factor, rhs, left_side=True, lower=True)
    return lax.linalg.triangular_solve(factor, lower_sol, left_side=True, lower=True, transpose_a=True)

def scaled_apply(field, diagonal):
    padded = jnp.pad(field, ((1, 1), (1, 1), (0, 0)))
    beside = padded[2:, 1:-1] + padded[:-2, 1:-1] + padded[1:-1, 2:] + padded[1:-1, :-2]
    applied = diagonal[:, :, None] * field - beside
    return (2.0 * applied - (UPPER_EDGE + LOWER_EDGE) * field) / (UPPER_EDGE - LOWER_EDGE)

def prior_block(block, diagonal):
    coeffs = cheb_coeffs(SWEEPS + 1)
    earlier = block
    current = scaled_apply(block, diagonal)
    total = coeffs[0] * block + coeffs[1] * current
    for order in range(2, SWEEPS + 1):
        following = 2.0 * scaled_apply(current, diagonal) - earlier
        total = total + coeffs[order] * following
        earlier, current = (current, following)
    return total

def reference(latent_noise, kappa_sq, obs_cell, obs_value, obs_var):
    diagonal = kappa_sq + 4.0
    groups = MEMBERS // 8
    noise3 = latent_noise.reshape(NX, NY, MEMBERS)
    blocks = jnp.moveaxis(noise3.reshape(NX, NY, 8, groups), 2, 0)
    fields = lax.map(lambda piece: prior_block(piece, diagonal), blocks)
    field3 = jnp.moveaxis(fields, 0, 2).reshape(NX, NY, MEMBERS)
    prior_field = field3.reshape(NX, NY * MEMBERS)
    index = jnp.arange(NOBS, dtype=jnp.int32)
    owner = index // OBS_DEV
    global_x = owner // N_GY * CX + obs_cell // CY
    global_y = owner % N_GY * CY + obs_cell % CY
    predicted = field3[global_x, global_y]
    weight = 1.0 / obs_var
    misfits = obs_value[:, None] - predicted
    misfit_total = jnp.sum(misfits * misfits * weight[:, None])
    inflation = 1.0 + misfit_total / (MEMBERS * (MEMBERS - 1))
    spread = predicted - jnp.mean(predicted, axis=1, keepdims=True)
    scaled = spread * (weight / inflation)[:, None]
    gram = jnp.dot(scaled.T.astype(jnp.float32), spread.astype(jnp.float32), precision=lax.Precision.HIGHEST, preferred_element_type=jnp.float32)
    cross = jnp.dot(scaled.T.astype(jnp.float32), misfits.astype(jnp.float32), precision=lax.Precision.HIGHEST, preferred_element_type=jnp.float32)
    system = (MEMBERS - 1) * jnp.eye(MEMBERS, dtype=jnp.float32) + gram
    factor = jnp.linalg.cholesky(system)
    gain = chol_solve(factor, cross)
    latent_cells = latent_noise.reshape(NX * NY, MEMBERS)
    deviation = latent_cells - jnp.mean(latent_cells, axis=1, keepdims=True)
    update = jnp.dot(deviation.astype(jnp.float32), gain.astype(jnp.float32), precision=lax.Precision.HIGHEST, preferred_element_type=jnp.float32)
    latent_new = (latent_cells + update).reshape(NX, NY * MEMBERS)
    return (latent_new, prior_field)
```

```python
import jax
import jax.numpy as jnp
import numpy as np
from jax import lax
from jax.experimental import pallas as pl
from jax.experimental.pallas import tpu as pltpu
from jax.sharding import PartitionSpec as P

MEMBERS = 64
SWEEPS = 4
LOWER_EDGE = 0.25
UPPER_EDGE = 12.0
HALO = SWEEPS
CX = 64
CY = 64
OBS = 256
EXT_ROWS = CX + 16
EXT_LANES = (CY + 2 * HALO) * MEMBERS
BLOCKS = EXT_LANES // 128
LEFT = HALO * MEMBERS
WIDTH = CY * MEMBERS
STAT_ROWS = 40
VMEM = pltpu.MemorySpace.VMEM
SMEM = pltpu.MemorySpace.SMEM


def power_coeffs():
    angles = np.pi * (np.arange(64) + 0.5) / 64.0
    centre, half = 0.5 * (UPPER_EDGE + LOWER_EDGE), 0.5 * (UPPER_EDGE - LOWER_EDGE)
    nodes = centre + half * np.cos(angles)
    cheb = [2.0 / 64.0 * np.sum(np.cos(k * angles) / nodes) for k in range(SWEEPS + 1)]
    cheb[0] *= 0.5
    mono = np.polynomial.chebyshev.cheb2poly(cheb)
    return [float(v / half**k) for k, v in enumerate(mono)]


def split3(a):
    hi = a.astype(jnp.bfloat16)
    lo = (a - hi.astype(jnp.float32)).astype(jnp.bfloat16)
    return hi, lo


def field_kernel(flags, cell, lat, kap, xlo, xhi, ylo, yhi, val, var, prior, stat, ext, alp, ua, ub, tall, kext, pbuf):
    fx0, fx1, fy0, fy1 = flags[0], flags[1], flags[2], flags[3]
    right = LEFT + WIDTH
    zero4 = jnp.zeros((4, EXT_LANES), jnp.float32)
    ext[0:4, :] = zero4
    ext[EXT_ROWS - 4 : EXT_ROWS, :] = zero4
    ext[8 : 8 + CX, LEFT:right] = lat[...]
    ext[4:8, LEFT:right] = xlo[:, 0:WIDTH] * fx0
    ext[8 + CX : 12 + CX, LEFT:right] = xhi[:, 0:WIDTH] * fx1
    for ref, flag, at in ((ylo, fy0, 0), (yhi, fy1, right)):
        ext[8 : 8 + CX, at : at + LEFT] = ref[0:CX, 0:LEFT] * flag
        ext[4:8, at : at + LEFT] = ref[CX : CX + 4, 0:LEFT] * (flag * fx0)
        ext[8 + CX : 12 + CX, at : at + LEFT] = ref[CX + 4 : CX + 8, 0:LEFT] * (flag * fx1)
    kext[...] = jnp.zeros((EXT_ROWS, 128), jnp.float32)
    kext[8 : 8 + CX, HALO : HALO + CY] = kap[...]
    kext[4:8, HALO : HALO + CY] = xlo[:, WIDTH : WIDTH + CY]
    kext[8 + CX : 12 + CX, HALO : HALO + CY] = xhi[:, WIDTH : WIDTH + CY]
    for ref, at in ((ylo, 0), (yhi, HALO + CY)):
        kext[8 : 8 + CX, at : at + HALO] = ref[0:CX, LEFT : LEFT + HALO]
        kext[4:8, at : at + HALO] = ref[CX : CX + 4, LEFT : LEFT + HALO]
        kext[8 + CX : 12 + CX, at : at + HALO] = ref[CX + 4 : CX + 8, LEFT : LEFT + HALO]
    shifted = kext[...] - (0.5 * (UPPER_EDGE + LOWER_EDGE) - 4.0)
    lane = lax.broadcasted_iota(jnp.int32, (EXT_ROWS, 128), 1)
    upper = lane // MEMBERS
    low_half = upper == 0
    for c in range(BLOCKS):
        alp[:, c * 128 : (c + 1) * 128] = jnp.take_along_axis(shifted, upper + 2 * c, axis=1)

    coeffs = power_coeffs()

    def block(ref, c):
        c = min(max(c, 0), BLOCKS - 1)
        return ref[:, c * 128 : (c + 1) * 128]

    def sweep(src, first, last, coeff, scale, store):
        turned = [None] * (BLOCKS + 2)

        def turn(c):
            return pltpu.roll(block(src, c), 64, 1)

        before, here = turn(first - 1), turn(first)
        for c in range(first, last + 1):
            after = turn(c + 1)
            v = block(src, c)
            beside = here + jnp.where(low_half, before, after)
            beside = beside + pltpu.roll(v, 1, 0) + pltpu.roll(v, EXT_ROWS - 1, 0)
            applied = block(alp, c) * v - beside
            if scale != 1.0:
                applied = applied * scale
            store(c, coeff * block(ext, c) + applied)
            before, here = here, after

    def keep(dst):
        def store(c, new):
            flag = fy0 if c < LEFT // 128 else fy1 if c >= right // 128 else None
            if flag is not None:
                new = new * flag
            at = slice(c * 128, (c + 1) * 128)
            dst[0:8, at] = new[0:8] * fx0
            dst[8 : 8 + CX, at] = new[8 : 8 + CX]
            dst[8 + CX : EXT_ROWS, at] = new[8 + CX : EXT_ROWS] * fx1

        return store

    def finish(c, new):
        prior[:, c * 128 - LEFT : (c + 1) * 128 - LEFT] = new[8 : 8 + CX]
        at = (c - LEFT // 128) * CX
        tall[at : at + CX, :] = new[8 : 8 + CX]

    sweep(ext, 0, BLOCKS - 1, coeffs[3], coeffs[4], keep(ua))
    sweep(ua, 1, BLOCKS - 2, coeffs[2], 1.0, keep(ub))
    sweep(ub, 1, BLOCKS - 2, coeffs[1], 1.0, keep(ua))
    sweep(ua, 2, BLOCKS - 3, coeffs[0], 1.0, finish)

    for j in range(OBS):
        at = cell[j]
        pair = lax.bitwise_and(at, CY - 2) * (CX // 2)
        pbuf[j : j + 1, :] = tall[pl.ds(pair + lax.shift_right_logical(at, 6), 1), :]

    def column(row):
        pieces = [jnp.transpose(jnp.broadcast_to(row[i : i + 1, :], (128, 128))) for i in range(OBS // 128)]
        return jnp.concatenate(pieces, axis=0)

    value = column(val[0:2, :])
    weight = 1.0 / column(var[0:2, :])
    odd = column(val[2:4, :]) > 0.5
    both = pbuf[...]
    plane = lax.broadcasted_iota(jnp.int32, (OBS, 128), 1)
    member = plane < MEMBERS
    predicted = jnp.where(odd, pltpu.roll(both, 64, 1), both)
    predicted = jnp.where(member, predicted, 0.0)
    mean = jnp.sum(predicted, axis=1, keepdims=True) * (1.0 / MEMBERS)
    spread = jnp.where(member, predicted - mean, jnp.where(plane == MEMBERS, value - mean, 0.0))
    full = lax.dot_general(
        spread * weight,
        spread,
        (((0,), (0,)), ((), ())),
        precision=lax.Precision.HIGHEST,
        preferred_element_type=jnp.float32,
    )
    half = MEMBERS // 2
    tile = lax.broadcasted_iota(jnp.int32, (half, 128), 1)
    stat[0:half, :] = jnp.where(tile < MEMBERS, full[0:half], pltpu.roll(full[half:MEMBERS], 64, 1))
    stat[half:STAT_ROWS, :] = full[MEMBERS : MEMBERS + 8]


def update_kernel(parts, lat, out):
    total = parts[0]
    for i in range(1, parts.shape[0]):
        total = total + parts[i]
    half = MEMBERS // 2
    packed = total[0:half]
    gram = jnp.concatenate([packed, pltpu.roll(packed, 64, 1)], axis=0)
    last = total[half : half + 1]
    shape = (MEMBERS, 128)
    row = lax.broadcasted_iota(jnp.int32, shape, 0)
    lane = lax.broadcasted_iota(jnp.int32, shape, 1)
    eye = row == lane
    low = lane < MEMBERS
    square = jnp.sum(jnp.where(lane[0:1] == MEMBERS, last, 0.0), axis=1, keepdims=True)
    trace = jnp.sum(jnp.sum(jnp.where(eye, gram, 0.0), axis=0, keepdims=True), axis=1, keepdims=True)
    inflation = 1.0 + (MEMBERS * square + trace) / float(MEMBERS * (MEMBERS - 1))
    shift = (MEMBERS - 1) * inflation
    towards = jnp.transpose(jnp.broadcast_to(last, (128, 128)))[0:MEMBERS]
    aug = jnp.where(low, gram + jnp.where(eye, shift, 0.0), towards - pltpu.roll(gram, 64, 1))
    for k in range(MEMBERS):
        pivot_row = aug[k : k + 1, :]
        scaled = pivot_row / pivot_row[:, k : k + 1]
        aug = jnp.where(row == k, scaled, aug - aug[:, k : k + 1] * scaled)
    gain = aug - jnp.sum(aug, axis=0, keepdims=True) * (1.0 / MEMBERS)
    weights = jnp.concatenate(
        [jnp.where(low, pltpu.roll(gain, 64, 1), 0.0), jnp.where(low, 0.0, gain)], axis=0
    )
    w_hi, w_lo = split3(weights)
    for c in range(WIDTH // 128):
        x = lat[:, c * 128 : (c + 1) * 128]
        x_hi, x_lo = split3(x)
        dot = lambda a, b: jnp.dot(a, b, preferred_element_type=jnp.float32)
        out[:, c * 128 : (c + 1) * 128] = x + ((dot(x_lo, w_hi) + dot(x_hi, w_lo)) + dot(x_hi, w_hi))


def ring(axis, step):
    count = lax.axis_size(axis)
    return [(i, (i + step) % count) for i in range(count)]


def per_device(latent, kappa, obs_cell, obs_value, obs_var):
    gx, gy = lax.axis_index("gx"), lax.axis_index("gy")
    last_x, last_y = lax.axis_size("gx") - 1, lax.axis_size("gy") - 1
    flags = jnp.stack([gx > 0, gx < last_x, gy > 0, gy < last_y]).astype(jnp.float32)

    rows = jnp.concatenate([latent, jnp.pad(kappa, ((0, 0), (0, 128 - CY)))], axis=1)
    xlo = lax.ppermute(rows[CX - HALO :], "gx", ring("gx", 1))
    xhi = lax.ppermute(rows[:HALO], "gx", ring("gx", -1))

    def cols(at):
        tall = jnp.concatenate(
            [a[:, at * MEMBERS : (at + HALO) * MEMBERS] for a in (latent, xlo, xhi)], axis=0
        )
        thin = jnp.concatenate(
            [kappa[:, at : at + HALO], xlo[:, WIDTH + at : WIDTH + at + HALO], xhi[:, WIDTH + at : WIDTH + at + HALO]], axis=0
        )
        return jnp.concatenate([tall, jnp.pad(thin, ((0, 0), (0, 128 - HALO)))], axis=1)

    ylo = lax.ppermute(cols(CY - HALO), "gy", ring("gy", 1))
    yhi = lax.ppermute(cols(0), "gy", ring("gy", -1))

    odd = (obs_cell % 2).astype(jnp.float32)
    val = jnp.concatenate([obs_value.reshape(2, 128), odd.reshape(2, 128)], axis=0)
    var = obs_var.reshape(2, 128)
    vmem, smem = pl.BlockSpec(memory_space=VMEM), pl.BlockSpec(memory_space=SMEM)
    wide = pltpu.VMEM((EXT_ROWS, EXT_LANES), jnp.float32)
    prior, stat = pl.pallas_call(
        field_kernel,
        out_shape=(
            jax.ShapeDtypeStruct((CX, WIDTH), jnp.float32),
            jax.ShapeDtypeStruct((STAT_ROWS, 128), jnp.float32),
        ),
        in_specs=[smem, smem] + [vmem] * 8,
        out_specs=(vmem, vmem),
        scratch_shapes=[wide] * 4
        + [pltpu.VMEM((r, 128), jnp.float32) for r in (CX * CY // 2, EXT_ROWS, OBS)],
        name="field",
    )(flags, obs_cell, latent, kappa, xlo, xhi, ylo, yhi, val, var)

    for axis in ("gy", "gx"):
        count = lax.axis_size(axis)
        parts = lax.all_to_all(jnp.broadcast_to(stat[None], (count,) + stat.shape), axis, 0, 0)
        if axis == "gy":
            stat = jnp.sum(parts, axis=0)

    latent_new = pl.pallas_call(
        update_kernel,
        out_shape=jax.ShapeDtypeStruct((CX, WIDTH), jnp.float32),
        in_specs=[vmem] * 2,
        out_specs=vmem,
        name="update",
    )(parts, latent)
    return (latent_new, prior)


def solution(mesh):
    placed = (P("gx", "gy"), P("gx", "gy"), P(("gx", "gy")), P(("gx", "gy")), P(("gx", "gy")))
    return jax.shard_map(
        per_device,
        mesh=mesh,
        in_specs=placed,
        out_specs=(P("gx", "gy"), P("gx", "gy")),
        check_vma=False,
    )
```

```python
import jax
import jax.numpy as jnp
import numpy as np
from jax import lax
from jax.experimental import pallas as pl
from jax.experimental.pallas import tpu as pltpu
from jax.sharding import PartitionSpec as P

MEMBERS = 64
SWEEPS = 4
LOWER_EDGE = 0.25
UPPER_EDGE = 12.0
HALO = SWEEPS
CX = 64
CY = 64
OBS = 256
TALL = CX + 16
WIDTH = CY * MEMBERS
BLOCKS = WIDTH // 128
EDGE = HALO * MEMBERS
RIM = 6
STAT = 17
HALF = MEMBERS // 2
VMEM = pltpu.MemorySpace.VMEM
SMEM = pltpu.MemorySpace.SMEM
F32 = jnp.float32


def power_coeffs():
    angles = np.pi * (np.arange(64) + 0.5) / 64.0
    centre, half = 0.5 * (UPPER_EDGE + LOWER_EDGE), 0.5 * (UPPER_EDGE - LOWER_EDGE)
    nodes = centre + half * np.cos(angles)
    cheb = [2.0 / 64.0 * np.sum(np.cos(k * angles) / nodes) for k in range(SWEEPS + 1)]
    cheb[0] *= 0.5
    mono = np.polynomial.chebyshev.cheb2poly(cheb)
    return [float(v / half**k) for k, v in enumerate(mono)]


COEFFS = power_coeffs()
CENTRE = 0.5 * (UPPER_EDGE + LOWER_EDGE) - 4.0


def lanes(c):
    return slice(c * 128, (c + 1) * 128)


def sweep(src, xi, alpha, first, last, coeff, scale, store):
    top = src.shape[1] // 128 - 1
    low_half = lax.broadcasted_iota(jnp.int32, (TALL, 128), 1) < MEMBERS

    def turn(c):
        return pltpu.roll(src[:, lanes(min(max(c, 0), top))], 64, 1)

    before, here = turn(first - 1), turn(first)
    for c in range(first, last + 1):
        after = turn(c + 1)
        v = src[:, lanes(c)]
        beside = here + jnp.where(low_half, before, after)
        beside = beside + pltpu.roll(v, 1, 0) + pltpu.roll(v, TALL - 1, 0)
        applied = alpha[:, lanes(c)] * v - beside
        if scale != 1.0:
            applied = applied * scale
        store(c, coeff * xi[:, lanes(c)] + applied)
        before, here = here, after


def spread_kappa(alpha, shifted, count, start):
    upper = (lax.broadcasted_iota(jnp.int32, (TALL, 128), 1) >= MEMBERS).astype(jnp.int32)
    for c in range(count):
        alpha[:, lanes(c)] = jnp.take_along_axis(shifted, upper + (2 * c + start), axis=1)


def rows_kernel(lat_hbm, kap_hbm, to_lo, to_hi, first, last, kap, sems):
    copies = [
        pltpu.make_async_copy(lat_hbm.at[0:8, :], first, sems.at[0]),
        pltpu.make_async_copy(lat_hbm.at[CX - 8 : CX, :], last, sems.at[1]),
        pltpu.make_async_copy(kap_hbm, kap, sems.at[2]),
    ]
    for copy in copies:
        copy.start()
    for copy in copies:
        copy.wait()
    to_lo[:, 0:WIDTH] = first[0:HALO, :]
    to_hi[:, 0:WIDTH] = last[8 - HALO : 8, :]
    blank = jnp.zeros((HALO, 128 - CY), F32)
    to_lo[:, WIDTH:] = jnp.concatenate([kap[0:HALO, :], blank], axis=1)
    to_hi[:, WIDTH:] = jnp.concatenate([kap[CX - HALO : CX, :], blank], axis=1)


def kappa_rows(dst, kap, xlo, xhi):
    dst[...] = jnp.zeros(dst.shape, F32)
    dst[8 : 8 + CX, 0:CY] = kap[...]
    dst[4:8, :] = xlo[:, WIDTH:]
    dst[8 + CX : 12 + CX, :] = xhi[:, WIDTH:]


def cols_kernel(first, last, kap, xlo, xhi, to_lo, to_hi, kext):
    kappa_rows(kext, kap, xlo, xhi)
    turned = jnp.transpose(kext[...])
    for dst, src, at in ((to_lo, first, 0), (to_hi, last, CY - HALO)):
        dst[0:CX, :] = src[...]
        dst[CX : CX + 4, :] = xlo[:, at * MEMBERS : at * MEMBERS + EDGE]
        dst[CX + 4 : CX + 8, :] = xhi[:, at * MEMBERS : at * MEMBERS + EDGE]
        dst[CX + 8 : CX + 16, 128:256] = jnp.zeros((8, 128), F32)
        dst[CX + 12 : CX + 16, 0:128] = jnp.zeros((4, 128), F32)
        dst[CX + 8 : CX + 12, 0:128] = turned[at : at + HALO, :]


def keep_rows(dst, flags):
    def store(c, new):
        dst[0:8, lanes(c)] = new[0:8] * flags[0:1, :]
        dst[8 : 8 + CX, lanes(c)] = new[8 : 8 + CX]
        dst[8 + CX : TALL, lanes(c)] = new[8 + CX : TALL] * flags[1:2, :]

    return store


def into_tiles(tiles, c, new):
    for t in range(CX // 8):
        at = (t * BLOCKS + c) * 8
        tiles[at : at + 8, :] = new[8 + 8 * t : 16 + 8 * t]


def fill_rows(ext, flags, at, body, xlo, xhi, extra=None):
    to = slice(at, at + body.shape[1])
    zero4 = jnp.zeros((4, body.shape[1]), F32)
    reps = body.shape[1] // 128
    low, high = (jnp.concatenate([flags[i : i + 1, :]] * reps, axis=1) for i in (0, 1))
    if extra is not None:
        side = jnp.concatenate([extra] * reps, axis=1)
        body, low, high = body * side, low * side, high * side
    ext[0:4, to] = zero4
    ext[TALL - 4 : TALL, to] = zero4
    ext[8 : 8 + CX, to] = body
    ext[4:8, to] = xlo * low
    ext[8 + CX : 12 + CX, to] = xhi * high


def inner_kernel(flags, lat, kap, xlo, xhi, val, var, tiles, value, weight, odd, ext, alpha, ua, ub, kext):
    for c in range(BLOCKS):
        fill_rows(ext, flags, c * 128, lat[:, lanes(c)], xlo[:, lanes(c)], xhi[:, lanes(c)])
    kappa_rows(kext, kap, xlo, xhi)
    spread_kappa(alpha, kext[0:TALL, :] - CENTRE, BLOCKS, 0)
    top = BLOCKS - 1
    sweep(ext, ext, alpha, 0, top, COEFFS[3], COEFFS[4], keep_rows(ua, flags))
    sweep(ua, ext, alpha, 1, top - 1, COEFFS[2], 1.0, keep_rows(ub, flags))
    sweep(ub, ext, alpha, 1, top - 1, COEFFS[1], 1.0, keep_rows(ua, flags))
    sweep(ua, ext, alpha, 2, top - 2, COEFFS[0], 1.0, lambda c, new: into_tiles(tiles, c, new))

    def column(row):
        pieces = [jnp.transpose(jnp.broadcast_to(row[i : i + 1, :], (128, 128))) for i in range(OBS // 128)]
        return jnp.concatenate(pieces, axis=0)

    value[...] = column(val[0:2, :])
    odd[...] = column(val[2:4, :])
    weight[...] = 1.0 / column(var[0:2, :])


def rim_kernel(
    flags, cell_hbm, lat0, lat1, kap, xlo, xhi, ylo, yhi, value, weight, odd, held,
    tiles, stat, cell, sems, ext, alpha, ua, ub, kext, pbuf,
):
    copies = [pltpu.make_async_copy(cell_hbm, cell, sems.at[CX // 8])]
    for t in range(CX // 8):
        at = pl.ds((t * BLOCKS + 2) * 8, (BLOCKS - 4) * 8)
        copies.append(pltpu.make_async_copy(held.at[at, :], tiles.at[at, :], sems.at[t]))
    for copy in copies:
        copy.start()
    kappa_rows(kext, kap, xlo, xhi)
    own = jnp.transpose(kext[...])
    near = RIM * 128 - EDGE
    for side, (lat, msg) in enumerate(((lat0, ylo), (lat1, yhi))):
        flag = flags[2 + side : 3 + side, :]
        at = 0 if side == 0 else WIDTH - near
        here, there = (EDGE, 0) if side == 0 else (0, near)
        fill_rows(ext, flags, here, lat[...], xlo[:, at : at + near], xhi[:, at : at + near])
        fill_rows(ext, flags, there, msg[0:CX, :], msg[CX : CX + 4, :], msg[CX + 4 : CX + 8, :], flag)
        if side == 0:
            kext[0:4, :] = msg[CX + 8 : CX + 12, 0:128]
            kext[4:16, :] = own[0:12, :]
        else:
            kext[0:8, :] = own[CY - 8 : CY, :]
            kext[8:12, :] = msg[CX + 8 : CX + 12, 0:128]
        shifted = jnp.transpose(kext[...])[0:TALL, :] - CENTRE
        spread_kappa(alpha, shifted, RIM, 0)

        def keep(dst):
            plain = keep_rows(dst, flags)
            outside = (0, 1) if side == 0 else (RIM - 2, RIM - 1)
            return lambda c, new: plain(c, new * flag if c in outside else new)

        def finish(c, new):
            into_tiles(tiles, c - 2 if side == 0 else c + BLOCKS - RIM + 2, new)

        sweep(ext, ext, alpha, 0, RIM - 1, COEFFS[3], COEFFS[4], keep(ua))
        sweep(ua, ext, alpha, 1, RIM - 2, COEFFS[2], 1.0, keep(ub))
        sweep(ub, ext, alpha, 1, RIM - 2, COEFFS[1], 1.0, keep(ua))
        sweep(ua, ext, alpha, 2, RIM - 3, COEFFS[0], 1.0, finish)

    for copy in copies:
        copy.wait()
    for j in range(OBS):
        at = cell[j]
        x, y = lax.shift_right_logical(at, 6), lax.bitwise_and(at, CY - 1)
        row = lax.bitwise_and(x, 56) * BLOCKS + lax.bitwise_and(y, CY - 2) * 4 + lax.bitwise_and(x, 7)
        pbuf[j : j + 1, :] = tiles[pl.ds(row, 1), :]
    both = pbuf[...]
    lane = lax.broadcasted_iota(jnp.int32, (OBS, 128), 1)
    member = lane < MEMBERS
    predicted = jnp.where(odd[...] > 0.5, pltpu.roll(both, 64, 1), both)
    predicted = jnp.where(member, predicted, 0.0)
    mean = jnp.sum(predicted, axis=1, keepdims=True) * (1.0 / MEMBERS)
    spread = jnp.where(member, predicted - mean, jnp.where(lane == MEMBERS, value[...] - mean, 0.0))
    full = lax.dot_general(
        spread * weight[...],
        spread,
        (((0,), (0,)), ((), ())),
        precision=lax.Precision.HIGHEST,
        preferred_element_type=F32,
    )
    lane = lax.broadcasted_iota(jnp.int32, (HALF, 128), 1)
    row = lax.broadcasted_iota(jnp.int32, (HALF, 128), 0)
    first, second = full[0:HALF], full[HALF:MEMBERS]
    packed = jnp.where(lane >= row, first, pltpu.roll(second, 96, 1))
    folded = jnp.where(lane[0:16] < MEMBERS, packed[0:16], pltpu.roll(packed[16:32], 64, 1))
    diagonal = jnp.sum(jnp.where(lane == row + 96, pltpu.roll(second, 64, 1), 0.0), axis=0, keepdims=True)
    last = jnp.where(lane[0:1] < 96, full[MEMBERS : MEMBERS + 1], diagonal)
    stat[0 : STAT - 1, :] = folded
    stat[STAT - 1 : STAT, :] = last


def eliminate(aug):
    size = MEMBERS
    row = lax.broadcasted_iota(jnp.int32, (size, 128), 0)
    for start in range(0, size, 4):
        columns = [jnp.broadcast_to(aug[:, k : k + 1], (size, 128)) for k in range(start, start + 4)]
        for i in range(4):
            k = start + i
            here = row == k
            inverse = 1.0 / columns[i][k : k + 1, :]
            for j in range(i + 1, 4):
                scaled = columns[j][k : k + 1, :] * inverse
                columns[j] = jnp.where(here, scaled, columns[j] - columns[i] * scaled)
            scaled = aug[k : k + 1, :] * inverse
            aug = jnp.where(here, scaled, aug - columns[i] * scaled)
    return aug


def update_kernel(parts, lat, tiles, out_hbm, prior_hbm, total, out, sems):
    copies = [pltpu.make_async_copy(tiles, prior_hbm, sems.at[CX // 8])]
    copies[0].start()
    for i in range(STAT):
        row = parts[0, i]
        for d in range(1, parts.shape[0]):
            row = row + parts[d, i]
        total[i : i + 1, :] = row
    folded, last = total[0:16, :], total[16:17, :]
    packed = jnp.concatenate([folded, pltpu.roll(folded, 64, 1)], axis=0)
    tall = jnp.concatenate([packed, jnp.zeros((32, 128), F32), jnp.broadcast_to(last, (64, 128))], axis=0)
    turned = jnp.transpose(tall)
    lane = lax.broadcasted_iota(jnp.int32, (HALF, 128), 1)
    row = lax.broadcasted_iota(jnp.int32, (HALF, 128), 0)
    first = jnp.where(lane >= row, packed, turned[0:HALF])
    corner = jnp.where(lane < row + HALF, pltpu.roll(packed, 32, 1), pltpu.roll(turned[0:HALF], 32, 1))
    corner = jnp.where(lane == row + HALF, pltpu.roll(last, 64, 1), corner)
    second = jnp.where(lane < HALF, turned[HALF:MEMBERS], corner)
    gram = jnp.concatenate([first, second], axis=0)

    shape = (MEMBERS, 128)
    row = lax.broadcasted_iota(jnp.int32, shape, 0)
    lane = lax.broadcasted_iota(jnp.int32, shape, 1)
    eye = row == lane
    low = lane < MEMBERS
    square = jnp.where(lane[0:1] == MEMBERS, last, 0.0) * float(MEMBERS)
    trace = jnp.sum(jnp.where(eye, gram, 0.0), axis=0, keepdims=True)
    misfit = jnp.sum(square + trace, axis=1, keepdims=True)
    inflation = 1.0 + misfit / float(MEMBERS * (MEMBERS - 1))
    shift = (MEMBERS - 1) * inflation
    right = turned[0:MEMBERS] - pltpu.roll(gram, 64, 1)
    aug = eliminate(jnp.where(low, gram + jnp.where(eye, shift, 0.0), right))
    gain = aug - jnp.sum(aug, axis=0, keepdims=True) * (1.0 / MEMBERS)
    weights = jnp.concatenate(
        [jnp.where(low, pltpu.roll(gain, 64, 1), 0.0), jnp.where(low, 0.0, gain)], axis=0
    )

    def split(a):
        hi = a.astype(jnp.bfloat16)
        return hi, (a - hi.astype(F32)).astype(jnp.bfloat16)

    def dot(a, b):
        return jnp.dot(a, b, preferred_element_type=F32)

    w_hi, w_lo = split(weights)
    for t in range(CX // 8):
        at = slice(t * 256, (t + 1) * 256)
        x = lat[at, :]
        x_hi, x_lo = split(x)
        out[at, :] = x + ((dot(x_lo, w_hi) + dot(x_hi, w_lo)) + dot(x_hi, w_hi))
        copies.append(pltpu.make_async_copy(out.at[at, :], out_hbm.at[at, :], sems.at[t]))
        copies[-1].start()
    for copy in copies:
        copy.wait()


def ring(axis, step):
    count = lax.axis_size(axis)
    return [(i, (i + step) % count) for i in range(count)]


def arr(*shape):
    return jax.ShapeDtypeStruct(shape, F32)


def buf(*shape):
    return pltpu.VMEM(shape, F32)


def params(mib):
    return pltpu.CompilerParams(vmem_limit_bytes=mib << 20)


def cost(flops, moved):
    return pl.CostEstimate(flops=flops, bytes_accessed=moved, transcendentals=0)


def to_tiles(a):
    return a.reshape(CX // 8, 8, BLOCKS, 128).transpose(0, 2, 1, 3).reshape(CX * BLOCKS, 128)


def from_tiles(a):
    return a.reshape(CX // 8, BLOCKS, 8, 128).transpose(0, 2, 1, 3).reshape(CX, WIDTH)


def per_device(latent, kappa, obs_cell, obs_value, obs_var):
    gx, gy = lax.axis_index("gx"), lax.axis_index("gy")
    last_x, last_y = lax.axis_size("gx") - 1, lax.axis_size("gy") - 1
    inside = jnp.stack([gx > 0, gx < last_x, gy > 0, gy < last_y] * 2).astype(F32)
    flags = jnp.broadcast_to(inside[:, None], (8, 128))
    odd = (obs_cell % 2).astype(F32)
    val = jnp.concatenate([obs_value.reshape(2, 128), odd.reshape(2, 128)], axis=0)
    var = obs_var.reshape(2, 128)
    vmem, anywhere = pl.BlockSpec(memory_space=VMEM), pl.BlockSpec(memory_space=pl.ANY)
    hbm = pl.BlockSpec(memory_space=pltpu.MemorySpace.HBM)

    def part(shape, *at):
        return pl.BlockSpec(shape, lambda i: at)

    to_lo, to_hi = pl.pallas_call(
        rows_kernel,
        out_shape=(arr(HALO, WIDTH + 128),) * 2,
        in_specs=[hbm, hbm],
        out_specs=(vmem, vmem),
        scratch_shapes=[buf(8, WIDTH), buf(8, WIDTH), buf(CX, CY), pltpu.SemaphoreType.DMA((3,))],
        compiler_params=params(4),
        name="rows",
    )(latent, kappa)
    xlo = lax.ppermute(to_hi, "gx", ring("gx", 1))
    xhi = lax.ppermute(to_lo, "gx", ring("gx", -1))

    whole = part((HALO, WIDTH + 128), 0, 0)
    to_lo, to_hi = pl.pallas_call(
        cols_kernel,
        grid=(1,),
        out_shape=(arr(CX + 16, EDGE),) * 2,
        in_specs=[part((CX, EDGE), 0, 0), part((CX, EDGE), 0, WIDTH // EDGE - 1), part((CX, CY), 0, 0), whole, whole],
        out_specs=(part((CX + 16, EDGE), 0, 0),) * 2,
        scratch_shapes=[buf(128, 128)],
        compiler_params=params(4),
        name="cols",
    )(latent, latent, kappa, xlo, xhi)
    ylo = lax.ppermute(to_hi, "gy", ring("gy", 1))
    yhi = lax.ppermute(to_lo, "gy", ring("gy", -1))

    tiles, value, weight, odd = pl.pallas_call(
        inner_kernel,
        out_shape=(arr(CX * BLOCKS, 128), arr(OBS, 128), arr(OBS, 128), arr(OBS, 128)),
        in_specs=[vmem] * 7,
        out_specs=(vmem,) * 4,
        scratch_shapes=[buf(TALL, WIDTH)] * 4 + [buf(128, 128)],
        compiler_params=params(12),
        cost_estimate=cost(20_000_000, 12_000_000),
        name="inner",
    )(flags, latent, kappa, xlo, xhi, val, var)

    near = RIM * 128 - EDGE
    whole_of = lambda a: part(a.shape, *([0] * a.ndim))
    operands = (kappa, xlo, xhi, ylo, yhi, value, weight, odd, tiles)
    tiles, stat = pl.pallas_call(
        rim_kernel,
        grid=(1,),
        out_shape=(arr(CX * BLOCKS, 128), arr(STAT, 128)),
        in_specs=[
            whole_of(flags),
            anywhere,
            part((CX, near), 0, 0),
            part((CX, near), 0, WIDTH // near - 1),
            *(whole_of(a) for a in operands[:-1]),
            vmem,
        ],
        out_specs=(vmem, part((STAT, 128), 0, 0)),
        scratch_shapes=[pltpu.SMEM((OBS,), jnp.int32), pltpu.SemaphoreType.DMA((CX // 8 + 1,))]
        + [buf(TALL, RIM * 128)] * 4
        + [buf(128, 128), buf(OBS, 128)],
        compiler_params=params(12),
        name="rim",
    )(flags, obs_cell, latent, latent, *operands)

    stat = stat[:, None, :]
    for axis in ("gy", "gx"):
        count = lax.axis_size(axis)
        parts = lax.all_to_all(jnp.broadcast_to(stat[None], (count,) + stat.shape), axis, 0, 0)
        if axis == "gy":
            stat = jnp.sum(parts, axis=0)

    latent_new, prior = pl.pallas_call(
        update_kernel,
        out_shape=(arr(CX * BLOCKS, 128),) * 2,
        in_specs=[vmem] * 3,
        out_specs=(anywhere,) * 2,
        scratch_shapes=[buf(24, 128), buf(CX * BLOCKS, 128), pltpu.SemaphoreType.DMA((CX // 8 + 1,))],
        compiler_params=params(12),
        name="update",
    )(parts, to_tiles(latent), tiles)
    return (from_tiles(latent_new), from_tiles(prior))


def solution(mesh):
    placed = (P("gx", "gy"), P("gx", "gy"), P(("gx", "gy")), P(("gx", "gy")), P(("gx", "gy")))
    return jax.shard_map(
        per_device,
        mesh=mesh,
        in_specs=placed,
        out_specs=(P("gx", "gy"), P("gx", "gy")),
        check_vma=False,
    )
```

```python
import jax
import jax.numpy as jnp
import numpy as np
from jax import lax
from jax.experimental import pallas as pl
from jax.experimental.pallas import tpu as pltpu
from jax.sharding import PartitionSpec as P

MEMBERS = 64
SWEEPS = 4
LOWER_EDGE = 0.25
UPPER_EDGE = 12.0
HALO = SWEEPS
CX = 64
CY = 64
OBS = 256
TALL = CX + 16
WIDTH = CY * MEMBERS
BLOCKS = WIDTH // 128
EDGE = HALO * MEMBERS
RIM = 6
STAT = 17
HALF = MEMBERS // 2
VMEM = pltpu.MemorySpace.VMEM
SMEM = pltpu.MemorySpace.SMEM
F32 = jnp.float32


def power_coeffs():
    angles = np.pi * (np.arange(64) + 0.5) / 64.0
    centre, half = 0.5 * (UPPER_EDGE + LOWER_EDGE), 0.5 * (UPPER_EDGE - LOWER_EDGE)
    nodes = centre + half * np.cos(angles)
    cheb = [2.0 / 64.0 * np.sum(np.cos(k * angles) / nodes) for k in range(SWEEPS + 1)]
    cheb[0] *= 0.5
    mono = np.polynomial.chebyshev.cheb2poly(cheb)
    return [float(v / half**k) for k, v in enumerate(mono)]


COEFFS = power_coeffs()
CENTRE = 0.5 * (UPPER_EDGE + LOWER_EDGE) - 4.0


PAD = 8


def lanes(c):
    return slice(c * 128, (c + 1) * 128)


def stencil_buf(blocks):
    return pltpu.VMEM((blocks * TALL + 2 * PAD, 128), F32)


def rows_of(c, first=0, count=TALL):
    at = PAD + c * TALL + first
    return slice(at, at + count)


def sweep(src, xi, alpha, blocks, first, last, coeff, scale, store, tiles=(0, TALL)):
    at, count = tiles[0], tiles[1] - tiles[0]
    low_half = lax.broadcasted_iota(jnp.int32, (count, 128), 1) < MEMBERS

    def turn(c):
        return pltpu.roll(src[rows_of(min(max(c, 0), blocks - 1), at, count), :], 64, 1)

    before, here = turn(first - 1), turn(first)
    for c in range(first, last + 1):
        after = turn(c + 1)
        here_rows = rows_of(c, at, count)
        beside = here + jnp.where(low_half, before, after)
        beside = beside + (src[rows_of(c, at - 1, count), :] + src[rows_of(c, at + 1, count), :])
        applied = alpha[here_rows, :] * src[here_rows, :] - beside
        if scale != 1.0:
            applied = applied * scale
        store(c, coeff * xi[here_rows, :] + applied)
        before, here = here, after


def spread_kappa(alpha, shifted, count, start):
    upper = (lax.broadcasted_iota(jnp.int32, (TALL, 128), 1) >= MEMBERS).astype(jnp.int32)
    for c in range(count):
        alpha[rows_of(c), :] = jnp.take_along_axis(shifted, upper + (2 * c + start), axis=1)


def rows_kernel(lat_hbm, kap_hbm, to_lo, to_hi, kap, sems):
    copies = [
        pltpu.make_async_copy(kap_hbm.at[0:8, :], kap.at[0:8, :], sems.at[0]),
        pltpu.make_async_copy(kap_hbm.at[CX - 8 : CX, :], kap.at[8:16, :], sems.at[1]),
        pltpu.make_async_copy(lat_hbm.at[0:HALO, :], to_lo.at[:, 0:WIDTH], sems.at[2]),
        pltpu.make_async_copy(lat_hbm.at[CX - HALO : CX, :], to_hi.at[:, 0:WIDTH], sems.at[3]),
    ]
    for copy in copies:
        copy.start()
    copies[0].wait()
    copies[1].wait()
    blank = jnp.zeros((HALO, 128 - CY), F32)
    to_lo[:, WIDTH:] = jnp.concatenate([kap[0:HALO, :], blank], axis=1)
    to_hi[:, WIDTH:] = jnp.concatenate([kap[16 - HALO : 16, :], blank], axis=1)
    copies[2].wait()
    copies[3].wait()


def kappa_rows(dst, kap, xlo, xhi):
    dst[...] = jnp.zeros(dst.shape, F32)
    dst[8 : 8 + CX, 0:CY] = kap[...]
    dst[4:8, :] = xlo[:, WIDTH:]
    dst[8 + CX : 12 + CX, :] = xhi[:, WIDTH:]


def cols_kernel(first, last, kap, xlo, xhi, to_lo, to_hi, kext):
    kappa_rows(kext, kap, xlo, xhi)
    turned = jnp.transpose(kext[...])
    for dst, src, at in ((to_lo, first, 0), (to_hi, last, CY - HALO)):
        dst[0:CX, :] = src[...]
        dst[CX : CX + 4, :] = xlo[:, at * MEMBERS : at * MEMBERS + EDGE]
        dst[CX + 4 : CX + 8, :] = xhi[:, at * MEMBERS : at * MEMBERS + EDGE]
        dst[CX + 8 : CX + 16, 128:256] = jnp.zeros((8, 128), F32)
        dst[CX + 12 : CX + 16, 0:128] = jnp.zeros((4, 128), F32)
        dst[CX + 8 : CX + 12, 0:128] = turned[at : at + HALO, :]


def keep_rows(dst, flags):
    def store(c, new):
        dst[rows_of(c, 0, 8), :] = new[0:8] * flags[0:1, :]
        dst[rows_of(c, 8, CX), :] = new[8 : 8 + CX]
        dst[rows_of(c, 8 + CX, 8), :] = new[8 + CX : TALL] * flags[1:2, :]

    return store


def into_tiles(tiles, c, new):
    for t in range(CX // 8):
        at = (t * BLOCKS + c) * 8
        tiles[at : at + 8, :] = new[8 * t : 8 * t + 8]


def fill(ext, c, body, xlo, xhi, low, high):
    zero4 = jnp.zeros((4, 128), F32)
    ext[rows_of(c, 0, 4), :] = zero4
    ext[rows_of(c, 4, 4), :] = xlo * low
    ext[rows_of(c, 8, CX), :] = body
    ext[rows_of(c, 8 + CX, 4), :] = xhi * high
    ext[rows_of(c, 12 + CX, 4), :] = zero4


def inner_kernel(flags, lat, kap, xlo, xhi, val, var, tiles, value, weight, odd, ext, alpha, ua, ub, kext):
    for c in range(BLOCKS):
        fill(ext, c, lat[:, lanes(c)], xlo[:, lanes(c)], xhi[:, lanes(c)], flags[0:1, :], flags[1:2, :])
    kappa_rows(kext, kap, xlo, xhi)
    spread_kappa(alpha, kext[0:TALL, :] - CENTRE, BLOCKS, 0)
    top, inside = BLOCKS - 1, (8, 8 + CX)
    sweep(ext, ext, alpha, BLOCKS, 0, top, COEFFS[3], COEFFS[4], keep_rows(ua, flags))
    sweep(ua, ext, alpha, BLOCKS, 1, top - 1, COEFFS[2], 1.0, keep_rows(ub, flags))
    sweep(ub, ext, alpha, BLOCKS, 1, top - 1, COEFFS[1], 1.0, keep_rows(ua, flags))
    sweep(ua, ext, alpha, BLOCKS, 2, top - 2, COEFFS[0], 1.0, lambda c, new: into_tiles(tiles, c, new), inside)

    def column(row):
        pieces = [jnp.transpose(jnp.broadcast_to(row[i : i + 1, :], (128, 128))) for i in range(OBS // 128)]
        return jnp.concatenate(pieces, axis=0)

    value[...] = column(val[0:2, :])
    odd[...] = column(val[2:4, :])
    weight[...] = 1.0 / column(var[0:2, :])


def rim_kernel(
    flags, cell_vmem, lat0, lat1, kap, xlo, xhi, ylo, yhi, value, weight, odd, held,
    tiles, stat, cell, sem, ext, alpha, ua, ub, kext, pbuf,
):
    fetch = pltpu.make_async_copy(cell_vmem, cell, sem)
    fetch.start()
    kappa_rows(kext, kap, xlo, xhi)
    own = jnp.transpose(kext[...])
    near = RIM - 2
    for side, (lat, msg) in enumerate(((lat0, ylo), (lat1, yhi))):
        flag = flags[2 + side : 3 + side, :]
        low, high = flags[0:1, :], flags[1:2, :]
        for i in range(near):
            at = lanes(i if side == 0 else BLOCKS - near + i)
            fill(ext, i + 2 if side == 0 else i, lat[:, lanes(i)], xlo[:, at], xhi[:, at], low, high)
        for i in range(2):
            body = msg[0:CX, lanes(i)] * flag
            halo = msg[CX : CX + 4, lanes(i)], msg[CX + 4 : CX + 8, lanes(i)]
            fill(ext, i if side == 0 else near + i, body, *halo, low * flag, high * flag)
        if side == 0:
            kext[0:4, :] = msg[CX + 8 : CX + 12, 0:128]
            kext[4:16, :] = own[0:12, :]
        else:
            kext[0:8, :] = own[CY - 8 : CY, :]
            kext[8:12, :] = msg[CX + 8 : CX + 12, 0:128]
        spread_kappa(alpha, jnp.transpose(kext[...])[0:TALL, :] - CENTRE, RIM, 0)

        def keep(dst):
            plain = keep_rows(dst, flags)
            outside = (0, 1) if side == 0 else (RIM - 2, RIM - 1)
            return lambda c, new: plain(c, new * flag if c in outside else new)

        def finish(c, new):
            into_tiles(tiles, c - 2 if side == 0 else c + BLOCKS - RIM + 2, new)

        sweep(ext, ext, alpha, RIM, 0, RIM - 1, COEFFS[3], COEFFS[4], keep(ua))
        sweep(ua, ext, alpha, RIM, 1, RIM - 2, COEFFS[2], 1.0, keep(ub))
        sweep(ub, ext, alpha, RIM, 1, RIM - 2, COEFFS[1], 1.0, keep(ua))
        sweep(ua, ext, alpha, RIM, 2, RIM - 3, COEFFS[0], 1.0, finish, (8, 8 + CX))

    fetch.wait()
    for j in range(OBS):
        pbuf[j : j + 1, :] = tiles[pl.ds(cell[j], 1), :]
    both = pbuf[...]
    lane = lax.broadcasted_iota(jnp.int32, (OBS, 128), 1)
    member = lane < MEMBERS
    predicted = jnp.where(odd[...] > 0.5, pltpu.roll(both, 64, 1), both)
    predicted = jnp.where(member, predicted, 0.0)
    mean = jnp.sum(predicted, axis=1, keepdims=True) * (1.0 / MEMBERS)
    spread = jnp.where(member, predicted - mean, jnp.where(lane == MEMBERS, value[...] - mean, 0.0))
    full = lax.dot_general(
        spread * weight[...],
        spread,
        (((0,), (0,)), ((), ())),
        precision=lax.Precision.HIGHEST,
        preferred_element_type=F32,
    )
    lane = lax.broadcasted_iota(jnp.int32, (HALF, 128), 1)
    row = lax.broadcasted_iota(jnp.int32, (HALF, 128), 0)
    first, second = full[0:HALF], full[HALF:MEMBERS]
    packed = jnp.where(lane >= row, first, pltpu.roll(second, 96, 1))
    folded = jnp.where(lane[0:16] < MEMBERS, packed[0:16], pltpu.roll(packed[16:32], 64, 1))
    diagonal = jnp.sum(jnp.where(lane == row + 96, pltpu.roll(second, 64, 1), 0.0), axis=0, keepdims=True)
    last = jnp.where(lane[0:1] < 96, full[MEMBERS : MEMBERS + 1], diagonal)
    stat[0 : STAT - 1, :] = folded
    stat[STAT - 1 : STAT, :] = last


def eliminate(aug):
    size = 8
    row = lax.broadcasted_iota(jnp.int32, (size, 128), 0)
    for start in range(0, MEMBERS, size):
        columns = [jnp.broadcast_to(aug[:, k : k + 1], (MEMBERS, 128)) for k in range(start, start + size)]
        block = [column[start : start + size] for column in columns]
        pivot_rows = aug[start : start + size]
        for i in range(size):
            here = row == i
            inverse = 1.0 / block[i][i : i + 1]

            def clear(a):
                scaled = a[i : i + 1] * inverse
                return jnp.where(here, scaled, a - block[i] * scaled)

            block = block[: i + 1] + [clear(a) for a in block[i + 1 :]]
            pivot_rows = clear(pivot_rows)
        pieces = []
        for at in range(0, MEMBERS, size):
            if at == start:
                pieces.append(pivot_rows)
                continue
            terms = [column[at : at + size] * pivot_rows[i : i + 1] for i, column in enumerate(columns)]
            while len(terms) > 1:
                terms = [a + b for a, b in zip(terms[0::2], terms[1::2])]
            pieces.append(aug[at : at + size] - terms[0])
        aug = jnp.concatenate(pieces, axis=0)
    return aug


def update_kernel(parts, lat, tiles, out_hbm, prior_hbm, total, out, sems):
    copies = [pltpu.make_async_copy(tiles, prior_hbm, sems.at[CX // 8])]
    copies[0].start()
    for i in range(STAT):
        row = parts[0, i]
        for d in range(1, parts.shape[0]):
            row = row + parts[d, i]
        total[i : i + 1, :] = row
    folded, last = total[0:16, :], total[16:17, :]
    packed = jnp.concatenate([folded, pltpu.roll(folded, 64, 1)], axis=0)
    tall = jnp.concatenate([packed, jnp.zeros((32, 128), F32), jnp.broadcast_to(last, (64, 128))], axis=0)
    turned = jnp.transpose(tall)
    lane = lax.broadcasted_iota(jnp.int32, (HALF, 128), 1)
    row = lax.broadcasted_iota(jnp.int32, (HALF, 128), 0)
    first = jnp.where(lane >= row, packed, turned[0:HALF])
    corner = jnp.where(lane < row + HALF, pltpu.roll(packed, 32, 1), pltpu.roll(turned[0:HALF], 32, 1))
    corner = jnp.where(lane == row + HALF, pltpu.roll(last, 64, 1), corner)
    second = jnp.where(lane < HALF, turned[HALF:MEMBERS], corner)
    gram = jnp.concatenate([first, second], axis=0)

    shape = (MEMBERS, 128)
    row = lax.broadcasted_iota(jnp.int32, shape, 0)
    lane = lax.broadcasted_iota(jnp.int32, shape, 1)
    eye = row == lane
    low = lane < MEMBERS
    square = jnp.where(lane[0:1] == MEMBERS, last, 0.0) * float(MEMBERS)
    trace = jnp.sum(jnp.where(eye, gram, 0.0), axis=0, keepdims=True)
    misfit = jnp.sum(square + trace, axis=1, keepdims=True)
    inflation = 1.0 + misfit / float(MEMBERS * (MEMBERS - 1))
    shift = (MEMBERS - 1) * inflation
    right = turned[0:MEMBERS] - pltpu.roll(gram, 64, 1)
    aug = eliminate(jnp.where(low, gram + jnp.where(eye, shift, 0.0), right))
    gain = aug - jnp.sum(aug, axis=0, keepdims=True) * (1.0 / MEMBERS)
    weights = jnp.concatenate(
        [jnp.where(low, pltpu.roll(gain, 64, 1), 0.0), jnp.where(low, 0.0, gain)], axis=0
    )

    def split(a):
        hi = a.astype(jnp.bfloat16)
        return hi, (a - hi.astype(F32)).astype(jnp.bfloat16)

    def dot(a, b):
        return jnp.dot(a, b, preferred_element_type=F32)

    w_hi, w_lo = split(weights)
    for t in range(CX // 8):
        at = slice(t * 256, (t + 1) * 256)
        x = lat[at, :]
        x_hi, x_lo = split(x)
        out[at, :] = x + ((dot(x_lo, w_hi) + dot(x_hi, w_lo)) + dot(x_hi, w_hi))
        copies.append(pltpu.make_async_copy(out.at[at, :], out_hbm.at[at, :], sems.at[t]))
        copies[-1].start()
    for copy in copies:
        copy.wait()


def ring(axis, step):
    count = lax.axis_size(axis)
    return [(i, (i + step) % count) for i in range(count)]


def arr(*shape):
    return jax.ShapeDtypeStruct(shape, F32)


def buf(*shape):
    return pltpu.VMEM(shape, F32)


def params(mib):
    return pltpu.CompilerParams(vmem_limit_bytes=mib << 20)


def cost(flops, moved):
    return pl.CostEstimate(flops=flops, bytes_accessed=moved, transcendentals=0)


def to_tiles(a):
    return a.reshape(CX // 8, 8, BLOCKS, 128).transpose(0, 2, 1, 3).reshape(CX * BLOCKS, 128)


def from_tiles(a):
    return a.reshape(CX // 8, BLOCKS, 8, 128).transpose(0, 2, 1, 3).reshape(CX, WIDTH)


def per_device(latent, kappa, obs_cell, obs_value, obs_var):
    gx, gy = lax.axis_index("gx"), lax.axis_index("gy")
    last_x, last_y = lax.axis_size("gx") - 1, lax.axis_size("gy") - 1
    inside = jnp.stack([gx > 0, gx < last_x, gy > 0, gy < last_y] * 2).astype(F32)
    flags = jnp.broadcast_to(inside[:, None], (8, 128))
    odd = (obs_cell & 1).astype(F32)
    obs_x, obs_y = obs_cell >> 6, obs_cell & (CY - 1)
    obs_row = (obs_x & 56) * BLOCKS + (obs_y >> 1) * 8 + (obs_x & 7)
    val = jnp.concatenate([obs_value.reshape(2, 128), odd.reshape(2, 128)], axis=0)
    var = obs_var.reshape(2, 128)
    vmem, anywhere = pl.BlockSpec(memory_space=VMEM), pl.BlockSpec(memory_space=pl.ANY)
    hbm = pl.BlockSpec(memory_space=pltpu.MemorySpace.HBM)

    def part(shape, *at):
        return pl.BlockSpec(shape, lambda i: at)

    to_lo, to_hi = pl.pallas_call(
        rows_kernel,
        out_shape=(arr(HALO, WIDTH + 128),) * 2,
        in_specs=[hbm, hbm],
        out_specs=(vmem, vmem),
        scratch_shapes=[buf(16, CY), pltpu.SemaphoreType.DMA((4,))],
        compiler_params=params(4),
        name="rows",
    )(*(pltpu.with_memory_space_constraint(a, pltpu.MemorySpace.HBM) for a in (latent, kappa)))
    xlo = lax.ppermute(to_hi, "gx", ring("gx", 1))
    xhi = lax.ppermute(to_lo, "gx", ring("gx", -1))

    whole = part((HALO, WIDTH + 128), 0, 0)
    to_lo, to_hi = pl.pallas_call(
        cols_kernel,
        grid=(1,),
        out_shape=(arr(CX + 16, EDGE),) * 2,
        in_specs=[part((CX, EDGE), 0, 0), part((CX, EDGE), 0, WIDTH // EDGE - 1), part((CX, CY), 0, 0), whole, whole],
        out_specs=(part((CX + 16, EDGE), 0, 0),) * 2,
        scratch_shapes=[buf(128, 128)],
        compiler_params=params(4),
        name="cols",
    )(latent, latent, kappa, xlo, xhi)
    ylo = lax.ppermute(to_hi, "gy", ring("gy", 1))
    yhi = lax.ppermute(to_lo, "gy", ring("gy", -1))

    tiles, value, weight, odd = pl.pallas_call(
        inner_kernel,
        out_shape=(arr(CX * BLOCKS, 128), arr(OBS, 128), arr(OBS, 128), arr(OBS, 128)),
        in_specs=[vmem] * 7,
        out_specs=(vmem,) * 4,
        scratch_shapes=[stencil_buf(BLOCKS)] * 4 + [buf(128, 128)],
        compiler_params=params(12),
        cost_estimate=cost(20_000_000, 12_000_000),
        name="inner",
    )(flags, latent, kappa, xlo, xhi, val, var)

    near = RIM * 128 - EDGE
    obs_row = obs_row.astype(jnp.int32)
    whole_of = lambda a: part(a.shape, *([0] * a.ndim))
    operands = (kappa, xlo, xhi, ylo, yhi, value, weight, odd, tiles)
    tiles, stat = pl.pallas_call(
        rim_kernel,
        grid=(1,),
        out_shape=(arr(CX * BLOCKS, 128), arr(STAT, 128)),
        in_specs=[
            whole_of(flags),
            anywhere,
            part((CX, near), 0, 0),
            part((CX, near), 0, WIDTH // near - 1),
            *(whole_of(a) for a in operands[:-1]),
            vmem,
        ],
        out_specs=(vmem, part((STAT, 128), 0, 0)),
        scratch_shapes=[pltpu.SMEM((OBS,), jnp.int32), pltpu.SemaphoreType.DMA]
        + [stencil_buf(RIM)] * 4
        + [buf(128, 128), buf(OBS, 128)],
        input_output_aliases={12: 0},
        compiler_params=params(12),
        name="rim",
    )(flags, obs_row, latent, latent, *operands)

    stat = stat[:, None, :]
    for axis in ("gy", "gx"):
        count = lax.axis_size(axis)
        parts = lax.all_to_all(jnp.broadcast_to(stat[None], (count,) + stat.shape), axis, 0, 0)
        if axis == "gy":
            stat = jnp.sum(parts, axis=0)

    latent_new, prior = pl.pallas_call(
        update_kernel,
        out_shape=(arr(CX * BLOCKS, 128),) * 2,
        in_specs=[vmem] * 3,
        out_specs=(anywhere,) * 2,
        scratch_shapes=[buf(24, 128), buf(CX * BLOCKS, 128), pltpu.SemaphoreType.DMA((CX // 8 + 1,))],
        compiler_params=params(12),
        name="update",
    )(parts, to_tiles(latent), tiles)
    return (from_tiles(latent_new), from_tiles(prior))


def solution(mesh):
    placed = (P("gx", "gy"), P("gx", "gy"), P(("gx", "gy")), P(("gx", "gy")), P(("gx", "gy")))
    return jax.shard_map(
        per_device,
        mesh=mesh,
        in_specs=placed,
        out_specs=(P("gx", "gy"), P("gx", "gy")),
        check_vma=False,
    )
```

```python
import jax
import jax.numpy as jnp
import numpy as np
from jax import lax
from jax.experimental import pallas as pl
from jax.experimental.pallas import tpu as pltpu
from jax.sharding import PartitionSpec as P

MEMBERS = 64
SWEEPS = 4
LOWER_EDGE = 0.25
UPPER_EDGE = 12.0
HALO = SWEEPS
CX = 64
CY = 64
OBS = 256
TALL = CX + 16
WIDTH = CY * MEMBERS
BLOCKS = WIDTH // 128
EDGE = HALO * MEMBERS
STAT = 17
HALF = MEMBERS // 2
VMEM = pltpu.MemorySpace.VMEM
SMEM = pltpu.MemorySpace.SMEM
F32 = jnp.float32


def power_coeffs():
    angles = np.pi * (np.arange(64) + 0.5) / 64.0
    centre, half = 0.5 * (UPPER_EDGE + LOWER_EDGE), 0.5 * (UPPER_EDGE - LOWER_EDGE)
    nodes = centre + half * np.cos(angles)
    cheb = [2.0 / 64.0 * np.sum(np.cos(k * angles) / nodes) for k in range(SWEEPS + 1)]
    cheb[0] *= 0.5
    mono = np.polynomial.chebyshev.cheb2poly(cheb)
    return [float(v / half**k) for k, v in enumerate(mono)]


COEFFS = power_coeffs()
CENTRE = 0.5 * (UPPER_EDGE + LOWER_EDGE) - 4.0


PAD = 8


def lanes(c):
    return slice(c * 128, (c + 1) * 128)


def stencil_buf(blocks):
    return pltpu.VMEM((blocks * TALL + 2 * PAD, 128), F32)


def rows_of(c, first=0, count=TALL):
    at = PAD + c * TALL + first
    return slice(at, at + count)


def sweep(get, xi, alpha, order, coeff, scale, store, at=0, count=TALL):
    low_half = lax.broadcasted_iota(jnp.int32, (count, 128), 1) < MEMBERS
    turned = {}

    def turn(c):
        if c not in turned:
            turned[c] = pltpu.roll(get(c, at), 64, 1)
        return turned[c]

    for c, lower, upper in order:
        beside = turn(c) + jnp.where(low_half, turn(lower), turn(upper))
        beside = beside + (get(c, at - 1) + get(c, at + 1))
        applied = alpha(c) * get(c, at) - beside
        if scale != 1.0:
            applied = applied * scale
        store(c, coeff * xi(c) + applied)


def spread_kappa(alpha, shifted, count, start):
    upper = (lax.broadcasted_iota(jnp.int32, (TALL, 128), 1) >= MEMBERS).astype(jnp.int32)
    for c in range(count):
        alpha[rows_of(c), :] = jnp.take_along_axis(shifted, upper + (2 * c + start), axis=1)


def rows_kernel(lat_hbm, kap_hbm, to_lo, to_hi, kap, sems):
    copies = [
        pltpu.make_async_copy(kap_hbm.at[0:8, :], kap.at[0:8, :], sems.at[0]),
        pltpu.make_async_copy(kap_hbm.at[CX - 8 : CX, :], kap.at[8:16, :], sems.at[1]),
        pltpu.make_async_copy(lat_hbm.at[0:HALO, :], to_lo.at[:, 0:WIDTH], sems.at[2]),
        pltpu.make_async_copy(lat_hbm.at[CX - HALO : CX, :], to_hi.at[:, 0:WIDTH], sems.at[3]),
    ]
    for copy in copies:
        copy.start()
    copies[0].wait()
    copies[1].wait()
    blank = jnp.zeros((HALO, 128 - CY), F32)
    to_lo[:, WIDTH:] = jnp.concatenate([kap[0:HALO, :], blank], axis=1)
    to_hi[:, WIDTH:] = jnp.concatenate([kap[16 - HALO : 16, :], blank], axis=1)
    copies[2].wait()
    copies[3].wait()


def kappa_rows(dst, kap, xlo, xhi):
    dst[...] = jnp.zeros(dst.shape, F32)
    dst[8 : 8 + CX, 0:CY] = kap[...]
    dst[4:8, :] = xlo[:, WIDTH:]
    dst[8 + CX : 12 + CX, :] = xhi[:, WIDTH:]


def cols_kernel(first, last, kap, xlo, xhi, to_lo, to_hi, kext):
    kappa_rows(kext, kap, xlo, xhi)
    turned = jnp.transpose(kext[...])
    for dst, src, at in ((to_lo, first, 0), (to_hi, last, CY - HALO)):
        dst[0:CX, :] = src[...]
        dst[CX : CX + 4, :] = xlo[:, at * MEMBERS : at * MEMBERS + EDGE]
        dst[CX + 4 : CX + 8, :] = xhi[:, at * MEMBERS : at * MEMBERS + EDGE]
        dst[CX + 8 : CX + 16, 128:256] = jnp.zeros((8, 128), F32)
        dst[CX + 12 : CX + 16, 0:128] = jnp.zeros((4, 128), F32)
        dst[CX + 8 : CX + 12, 0:128] = turned[at : at + HALO, :]


def keep_rows(dst, flags):
    def store(c, new):
        dst[rows_of(c, 0, 8), :] = new[0:8] * flags[0:1, :]
        dst[rows_of(c, 8, CX), :] = new[8 : 8 + CX]
        dst[rows_of(c, 8 + CX, 8), :] = new[8 + CX : TALL] * flags[1:2, :]

    return store


def into_tiles(tiles, c, new):
    for t in range(CX // 8):
        at = (t * BLOCKS + c) * 8
        tiles[at : at + 8, :] = new[8 * t : 8 * t + 8]


def fill(ext, c, body, xlo, xhi, low, high):
    zero4 = jnp.zeros((4, 128), F32)
    ext[rows_of(c, 0, 4), :] = zero4
    ext[rows_of(c, 4, 4), :] = xlo * low
    ext[rows_of(c, 8, CX), :] = body
    ext[rows_of(c, 8 + CX, 4), :] = xhi * high
    ext[rows_of(c, 12 + CX, 4), :] = zero4


def inner_kernel(flags, lat, kap, xlo, xhi, val, var, tiles, value, weight, odd, ext, alpha, u3, u2, u1, kext):
    for c in range(BLOCKS):
        fill(ext, c, lat[:, lanes(c)], xlo[:, lanes(c)], xhi[:, lanes(c)], flags[0:1, :], flags[1:2, :])
    kappa_rows(kext, kap, xlo, xhi)
    spread_kappa(alpha, kext[0:TALL, :] - CENTRE, BLOCKS, 0)

    def run(src, depth, step, scale, store, at=0, count=TALL):
        order = [(c, max(c - 1, 0), min(c + 1, BLOCKS - 1)) for c in range(depth, BLOCKS - depth)]
        get = lambda c, shift: src[rows_of(c, shift, count), :]
        xi = lambda c: ext[rows_of(c, at, count), :]
        diag = lambda c: alpha[rows_of(c, at, count), :]
        sweep(get, xi, diag, order, COEFFS[step], scale, store, at, count)

    run(ext, 0, 3, COEFFS[4], keep_rows(u3, flags))
    run(u3, 1, 2, 1.0, keep_rows(u2, flags))
    run(u2, 1, 1, 1.0, keep_rows(u1, flags))
    run(u1, 2, 0, 1.0, lambda c, new: into_tiles(tiles, c, new), 8, CX)

    def column(row):
        pieces = [jnp.transpose(jnp.broadcast_to(row[i : i + 1, :], (128, 128))) for i in range(OBS // 128)]
        return jnp.concatenate(pieces, axis=0)

    value[...] = column(val[0:2, :])
    odd[...] = column(val[2:4, :])
    weight[...] = 1.0 / column(var[0:2, :])


def rim_kernel(
    flags, cell_vmem, ylo, yhi, value, weight, odd, ext, alpha, u3, u2, u1, held,
    tiles, stat, cell, sem, ext_out, alpha_out, v3, v2, v1, kext, pbuf,
):
    fetch = pltpu.make_async_copy(cell_vmem, cell, sem)
    fetch.start()
    low, high = flags[0:1, :], flags[1:2, :]
    kext[...] = jnp.zeros((128, 128), F32)
    for side, msg in enumerate((ylo, yhi)):
        flag = flags[2 + side : 3 + side, :]
        kext[0:4, :] = msg[CX + 8 : CX + 12, 0:128]
        shifted = jnp.transpose(kext[...])[0:TALL, :] - CENTRE
        upper = (lax.broadcasted_iota(jnp.int32, (TALL, 128), 1) >= MEMBERS).astype(jnp.int32)
        for p in (-2, -1):
            i = p + 2 if side == 0 else -1 - p
            halo = msg[CX : CX + 4, lanes(i)], msg[CX + 4 : CX + 8, lanes(i)]
            fill(ext_out, p + 2, msg[0:CX, lanes(i)] * flag, *halo, low * flag, high * flag)
            alpha_out[rows_of(p + 2), :] = jnp.take_along_axis(shifted, upper + 2 * i, axis=1)

        def local(p):
            return p if side == 0 else BLOCKS - 1 - p

        def run(near, far, mine, first, last, step, scale, store, at=0, count=TALL):
            def pick(p, here, there, ours, start):
                return here[rows_of(p + 2, start, count), :] if p in ours else there[rows_of(local(p), start, count), :]

            get = lambda p, shift: pick(p, near, far, mine, shift)
            xi = lambda p: pick(p, ext_out, ext, (-2, -1), at)
            diag = lambda p: pick(p, alpha_out, alpha, (-2, -1), at)
            order = [(p, max(p - 1, -2), p + 1) for p in range(first, last + 1)]
            if side == 1:
                order = [(p, b, a) for p, a, b in order]
            sweep(get, xi, diag, order, COEFFS[step], scale, store, at, count)

        def keep(dst):
            plain = keep_rows(dst, flags)
            return lambda p, new: plain(p + 2, new * flag if p < 0 else new)

        run(ext_out, ext, (-2, -1), -2, 0, 3, COEFFS[4], keep(v3))
        run(v3, u3, (-2, -1, 0), -1, 0, 2, 1.0, keep(v2))
        run(v2, u2, (-2, -1, 0), -1, 1, 1, 1.0, keep(v1))
        run(v1, u1, (-2, -1, 0, 1), 0, 1, 0, 1.0, lambda p, new: into_tiles(tiles, local(p), new), 8, CX)

    fetch.wait()
    for j in range(OBS):
        pbuf[j : j + 1, :] = tiles[pl.ds(cell[j], 1), :]
    both = pbuf[...]
    lane = lax.broadcasted_iota(jnp.int32, (OBS, 128), 1)
    member = lane < MEMBERS
    predicted = jnp.where(odd[...] > 0.5, pltpu.roll(both, 64, 1), both)
    predicted = jnp.where(member, predicted, 0.0)
    mean = jnp.sum(predicted, axis=1, keepdims=True) * (1.0 / MEMBERS)
    spread = jnp.where(member, predicted - mean, jnp.where(lane == MEMBERS, value[...] - mean, 0.0))
    full = lax.dot_general(
        spread * weight[...],
        spread,
        (((0,), (0,)), ((), ())),
        precision=lax.Precision.HIGHEST,
        preferred_element_type=F32,
    )
    lane = lax.broadcasted_iota(jnp.int32, (HALF, 128), 1)
    row = lax.broadcasted_iota(jnp.int32, (HALF, 128), 0)
    first, second = full[0:HALF], full[HALF:MEMBERS]
    packed = jnp.where(lane >= row, first, pltpu.roll(second, 96, 1))
    folded = jnp.where(lane[0:16] < MEMBERS, packed[0:16], pltpu.roll(packed[16:32], 64, 1))
    diagonal = jnp.sum(jnp.where(lane == row + 96, pltpu.roll(second, 64, 1), 0.0), axis=0, keepdims=True)
    last = jnp.where(lane[0:1] < 96, full[MEMBERS : MEMBERS + 1], diagonal)
    stat[0 : STAT - 1, :] = folded
    stat[STAT - 1 : STAT, :] = last


def eliminate(aug):
    size = 8
    row = lax.broadcasted_iota(jnp.int32, (size, 128), 0)
    for start in range(0, MEMBERS, size):
        columns = [jnp.broadcast_to(aug[:, k : k + 1], (MEMBERS, 128)) for k in range(start, start + size)]
        block = [column[start : start + size] for column in columns]
        pivot_rows = aug[start : start + size]
        for i in range(size):
            here = row == i
            inverse = 1.0 / block[i][i : i + 1]

            def clear(a):
                scaled = a[i : i + 1] * inverse
                return jnp.where(here, scaled, a - block[i] * scaled)

            block = block[: i + 1] + [clear(a) for a in block[i + 1 :]]
            pivot_rows = clear(pivot_rows)
        pieces = []
        for at in range(0, MEMBERS, size):
            if at == start:
                pieces.append(pivot_rows)
                continue
            terms = [column[at : at + size] * pivot_rows[i : i + 1] for i, column in enumerate(columns)]
            while len(terms) > 1:
                terms = [a + b for a, b in zip(terms[0::2], terms[1::2])]
            pieces.append(aug[at : at + size] - terms[0])
        aug = jnp.concatenate(pieces, axis=0)
    return aug


def split(a):
    hi = a.astype(jnp.bfloat16)
    return hi, (a - hi.astype(F32)).astype(jnp.bfloat16)


def solve_kernel(parts, tiles, weights_out, prior_hbm, total, sem):
    copy = pltpu.make_async_copy(tiles, prior_hbm, sem)
    copy.start()
    for i in range(STAT):
        row = parts[0, i]
        for d in range(1, parts.shape[0]):
            row = row + parts[d, i]
        total[i : i + 1, :] = row
    folded, last = total[0:16, :], total[16:17, :]
    packed = jnp.concatenate([folded, pltpu.roll(folded, 64, 1)], axis=0)
    tall = jnp.concatenate([packed, jnp.zeros((32, 128), F32), jnp.broadcast_to(last, (64, 128))], axis=0)
    turned = jnp.transpose(tall)
    lane = lax.broadcasted_iota(jnp.int32, (HALF, 128), 1)
    row = lax.broadcasted_iota(jnp.int32, (HALF, 128), 0)
    first = jnp.where(lane >= row, packed, turned[0:HALF])
    corner = jnp.where(lane < row + HALF, pltpu.roll(packed, 32, 1), pltpu.roll(turned[0:HALF], 32, 1))
    corner = jnp.where(lane == row + HALF, pltpu.roll(last, 64, 1), corner)
    second = jnp.where(lane < HALF, turned[HALF:MEMBERS], corner)
    gram = jnp.concatenate([first, second], axis=0)

    shape = (MEMBERS, 128)
    row = lax.broadcasted_iota(jnp.int32, shape, 0)
    lane = lax.broadcasted_iota(jnp.int32, shape, 1)
    eye = row == lane
    low = lane < MEMBERS
    square = jnp.where(lane[0:1] == MEMBERS, last, 0.0) * float(MEMBERS)
    trace = jnp.sum(jnp.where(eye, gram, 0.0), axis=0, keepdims=True)
    misfit = jnp.sum(square + trace, axis=1, keepdims=True)
    inflation = 1.0 + misfit / float(MEMBERS * (MEMBERS - 1))
    shift = (MEMBERS - 1) * inflation
    right = turned[0:MEMBERS] - pltpu.roll(gram, 64, 1)
    aug = eliminate(jnp.where(low, gram + jnp.where(eye, shift, 0.0), right))
    gain = aug - jnp.sum(aug, axis=0, keepdims=True) * (1.0 / MEMBERS)
    weights = jnp.concatenate(
        [jnp.where(low, pltpu.roll(gain, 64, 1), 0.0), jnp.where(low, 0.0, gain)], axis=0
    )

    w_hi, w_lo = split(weights)
    weights_out[0:128, 0:128] = w_hi
    weights_out[0:128, 128:256] = w_lo
    weights_out[128:256, 0:128] = w_hi
    weights_out[128:256, 128:256] = jnp.zeros((128, 128), jnp.bfloat16)
    copy.wait()


def update_kernel(lat, weights, out_hbm, out, sems):
    both = weights[...]
    copies = []
    for t in range(CX // 8):
        at = slice(t * 256, (t + 1) * 256)
        x = lat[at, :]
        product = jnp.dot(jnp.concatenate(split(x), axis=1), both, preferred_element_type=F32)
        out[at, :] = x + (product[:, 0:128] + product[:, 128:256])
        copies.append(pltpu.make_async_copy(out.at[at, :], out_hbm.at[at, :], sems.at[t]))
        copies[-1].start()
    for copy in copies:
        copy.wait()


def ring(axis, step):
    count = lax.axis_size(axis)
    return [(i, (i + step) % count) for i in range(count)]


def arr(*shape):
    return jax.ShapeDtypeStruct(shape, F32)


def buf(*shape):
    return pltpu.VMEM(shape, F32)


def params(mib):
    return pltpu.CompilerParams(vmem_limit_bytes=mib << 20)


def cost(flops, moved):
    return pl.CostEstimate(flops=flops, bytes_accessed=moved, transcendentals=0)


def to_tiles(a):
    return a.reshape(CX // 8, 8, BLOCKS, 128).transpose(0, 2, 1, 3).reshape(CX * BLOCKS, 128)


def from_tiles(a):
    return a.reshape(CX // 8, BLOCKS, 8, 128).transpose(0, 2, 1, 3).reshape(CX, WIDTH)


def per_device(latent, kappa, obs_cell, obs_value, obs_var):
    gx, gy = lax.axis_index("gx"), lax.axis_index("gy")
    last_x, last_y = lax.axis_size("gx") - 1, lax.axis_size("gy") - 1
    inside = jnp.stack([gx > 0, gx < last_x, gy > 0, gy < last_y] * 2).astype(F32)
    flags = jnp.broadcast_to(inside[:, None], (8, 128))
    odd = (obs_cell & 1).astype(F32)
    obs_x, obs_y = obs_cell >> 6, obs_cell & (CY - 1)
    obs_row = (obs_x & 56) * BLOCKS + (obs_y >> 1) * 8 + (obs_x & 7)
    val = jnp.concatenate([obs_value.reshape(2, 128), odd.reshape(2, 128)], axis=0)
    var = obs_var.reshape(2, 128)
    vmem, anywhere = pl.BlockSpec(memory_space=VMEM), pl.BlockSpec(memory_space=pl.ANY)
    hbm = pl.BlockSpec(memory_space=pltpu.MemorySpace.HBM)

    def part(shape, *at):
        return pl.BlockSpec(shape, lambda i: at)

    to_lo, to_hi = pl.pallas_call(
        rows_kernel,
        out_shape=(arr(HALO, WIDTH + 128),) * 2,
        in_specs=[hbm, hbm],
        out_specs=(vmem, vmem),
        scratch_shapes=[buf(16, CY), pltpu.SemaphoreType.DMA((4,))],
        compiler_params=params(4),
        name="rows",
    )(*(pltpu.with_memory_space_constraint(a, pltpu.MemorySpace.HBM) for a in (latent, kappa)))
    xlo = lax.ppermute(to_hi, "gx", ring("gx", 1))
    xhi = lax.ppermute(to_lo, "gx", ring("gx", -1))

    whole = part((HALO, WIDTH + 128), 0, 0)
    to_lo, to_hi = pl.pallas_call(
        cols_kernel,
        grid=(1,),
        out_shape=(arr(CX + 16, EDGE),) * 2,
        in_specs=[part((CX, EDGE), 0, 0), part((CX, EDGE), 0, WIDTH // EDGE - 1), part((CX, CY), 0, 0), whole, whole],
        out_specs=(part((CX + 16, EDGE), 0, 0),) * 2,
        scratch_shapes=[buf(128, 128)],
        compiler_params=params(4),
        name="cols",
    )(latent, latent, kappa, xlo, xhi)
    ylo = lax.ppermute(to_hi, "gy", ring("gy", 1))
    yhi = lax.ppermute(to_lo, "gy", ring("gy", -1))

    field = arr(BLOCKS * TALL + 2 * PAD, 128)
    tiles, *rest = pl.pallas_call(
        inner_kernel,
        out_shape=(arr(CX * BLOCKS, 128),) + (arr(OBS, 128),) * 3 + (field,) * 5,
        in_specs=[vmem] * 7,
        out_specs=(vmem,) * 9,
        scratch_shapes=[buf(128, 128)],
        compiler_params=params(12),
        cost_estimate=cost(20_000_000, 12_000_000),
        name="inner",
    )(flags, latent, kappa, xlo, xhi, val, var)

    tiles, stat = pl.pallas_call(
        rim_kernel,
        out_shape=(arr(CX * BLOCKS, 128), arr(STAT, 128)),
        in_specs=[vmem, anywhere] + [vmem] * 11,
        out_specs=(vmem, vmem),
        scratch_shapes=[pltpu.SMEM((OBS,), jnp.int32), pltpu.SemaphoreType.DMA]
        + [stencil_buf(4)] * 5
        + [buf(128, 128), buf(OBS, 128)],
        input_output_aliases={12: 0},
        compiler_params=params(12),
        name="rim",
    )(flags, obs_row, ylo, yhi, *rest, tiles)

    stat = stat[:, None, :]
    for axis in ("gy", "gx"):
        count = lax.axis_size(axis)
        parts = lax.all_to_all(jnp.broadcast_to(stat[None], (count,) + stat.shape), axis, 0, 0)
        if axis == "gy":
            stat = jnp.sum(parts, axis=0)

    weights, prior = pl.pallas_call(
        solve_kernel,
        out_shape=(jax.ShapeDtypeStruct((256, 256), jnp.bfloat16), arr(CX * BLOCKS, 128)),
        in_specs=[vmem] * 2,
        out_specs=(vmem, anywhere),
        scratch_shapes=[buf(24, 128), pltpu.SemaphoreType.DMA],
        compiler_params=params(12),
        name="solve",
    )(parts, tiles)
    latent_new = pl.pallas_call(
        update_kernel,
        out_shape=arr(CX * BLOCKS, 128),
        in_specs=[vmem] * 2,
        out_specs=anywhere,
        scratch_shapes=[buf(CX * BLOCKS, 128), pltpu.SemaphoreType.DMA((CX // 8,))],
        compiler_params=params(12),
        name="update",
    )(to_tiles(latent), weights)
    return (from_tiles(latent_new), from_tiles(prior))


def solution(mesh):
    placed = (P("gx", "gy"), P("gx", "gy"), P(("gx", "gy")), P(("gx", "gy")), P(("gx", "gy")))
    return jax.shard_map(
        per_device,
        mesh=mesh,
        in_specs=placed,
        out_specs=(P("gx", "gy"), P("gx", "gy")),
        check_vma=False,
    )
```

```python
import jax
import jax.numpy as jnp
import numpy as np
from jax import lax
from jax.experimental import pallas as pl
from jax.experimental.pallas import tpu as pltpu
from jax.sharding import PartitionSpec as P

MEMBERS = 64
SWEEPS = 4
LOWER_EDGE = 0.25
UPPER_EDGE = 12.0
HALO = SWEEPS
CX = 64
CY = 64
OBS = 256
TALL = CX + 16
WIDTH = CY * MEMBERS
BLOCKS = WIDTH // 128
EDGE = HALO * MEMBERS
STAT = 17
HALF = MEMBERS // 2
VMEM = pltpu.MemorySpace.VMEM
SMEM = pltpu.MemorySpace.SMEM
F32 = jnp.float32


def power_coeffs():
    angles = np.pi * (np.arange(64) + 0.5) / 64.0
    centre, half = 0.5 * (UPPER_EDGE + LOWER_EDGE), 0.5 * (UPPER_EDGE - LOWER_EDGE)
    nodes = centre + half * np.cos(angles)
    cheb = [2.0 / 64.0 * np.sum(np.cos(k * angles) / nodes) for k in range(SWEEPS + 1)]
    cheb[0] *= 0.5
    mono = np.polynomial.chebyshev.cheb2poly(cheb)
    return [float(v / half**k) for k, v in enumerate(mono)]


COEFFS = power_coeffs()
CENTRE = 0.5 * (UPPER_EDGE + LOWER_EDGE) - 4.0


PAD = 8


def lanes(c):
    return slice(c * 128, (c + 1) * 128)


def stencil_buf(blocks):
    return pltpu.VMEM((blocks * TALL + 2 * PAD, 128), F32)


def rows_of(c, first=0, count=TALL):
    at = PAD + c * TALL + first
    return slice(at, at + count)


def sweep(get, xi, alpha, order, coeff, scale, store, at=0, count=TALL):
    low_half = lax.broadcasted_iota(jnp.int32, (count, 128), 1) < MEMBERS
    turned = {}

    def turn(c):
        if c not in turned:
            turned[c] = pltpu.roll(get(c, at), 64, 1)
        return turned[c]

    for c, lower, upper in order:
        beside = turn(c) + jnp.where(low_half, turn(lower), turn(upper))
        beside = beside + (get(c, at - 1) + get(c, at + 1))
        applied = alpha(c) * get(c, at) - beside
        if scale != 1.0:
            applied = applied * scale
        store(c, coeff * xi(c) + applied)


def spread_kappa(alpha, shifted, count, start):
    upper = (lax.broadcasted_iota(jnp.int32, (TALL, 128), 1) >= MEMBERS).astype(jnp.int32)
    for c in range(count):
        alpha[rows_of(c), :] = jnp.take_along_axis(shifted, upper + (2 * c + start), axis=1)


def rows_kernel(lat_hbm, kap_hbm, to_lo, to_hi, kap, sems):
    copies = [
        pltpu.make_async_copy(kap_hbm, kap, sems.at[0]),
        pltpu.make_async_copy(lat_hbm.at[0:HALO, :], to_lo.at[:, 0:WIDTH], sems.at[1]),
        pltpu.make_async_copy(lat_hbm.at[CX - HALO : CX, :], to_hi.at[:, 0:WIDTH], sems.at[2]),
    ]
    for copy in copies:
        copy.start()
    copies[0].wait()
    blank = jnp.zeros((HALO, 128 - CY), F32)
    to_lo[:, WIDTH:] = jnp.concatenate([kap[0:HALO, :], blank], axis=1)
    to_hi[:, WIDTH:] = jnp.concatenate([kap[CX - HALO : CX, :], blank], axis=1)
    copies[1].wait()
    copies[2].wait()


def kappa_rows(dst, kap, xlo, xhi):
    dst[...] = jnp.zeros(dst.shape, F32)
    dst[8 : 8 + CX, 0:CY] = kap[...]
    dst[4:8, :] = xlo[:, WIDTH:]
    dst[8 + CX : 12 + CX, :] = xhi[:, WIDTH:]


def cols_kernel(flags, first, last, kap, xhi, xlo, to_odd, to_even, kext):
    kappa_rows(kext, kap, xlo, xhi)
    turned = jnp.transpose(kext[...])
    at = (0, CY - HALO)
    spans = [slice(a * MEMBERS, a * MEMBERS + EDGE) for a in at]
    odd = jnp.broadcast_to(flags[4:5, :], (8, 128)) > 0.5
    wide = jnp.concatenate([odd, odd], axis=1)
    for dst, pick in ((to_odd, lambda low, high, mask: jnp.where(mask, high, low)), (to_even, lambda low, high, mask: jnp.where(mask, low, high))):
        for r in range(0, CX, 8):
            dst[r : r + 8, :] = pick(first[r : r + 8, :], last[r : r + 8, :], wide)
        for r, halo in ((CX, xlo), (CX + 4, xhi)):
            dst[r : r + 4, :] = pick(halo[:, spans[0]], halo[:, spans[1]], wide[0:4])
        dst[CX + 8 : CX + 16, 128:256] = jnp.zeros((8, 128), F32)
        dst[CX + 12 : CX + 16, 0:128] = jnp.zeros((4, 128), F32)
        dst[CX + 8 : CX + 12, 0:128] = pick(turned[0:HALO, :], turned[CY - HALO : CY, :], odd[0:4])


def keep_rows(dst, flags):
    def store(c, new):
        dst[rows_of(c, 0, 8), :] = new[0:8] * flags[0:1, :]
        dst[rows_of(c, 8, CX), :] = new[8 : 8 + CX]
        dst[rows_of(c, 8 + CX, 8), :] = new[8 + CX : TALL] * flags[1:2, :]

    return store


def into_tiles(tiles, c, new):
    for t in range(CX // 8):
        at = (t * BLOCKS + c) * 8
        tiles[at : at + 8, :] = new[8 * t : 8 * t + 8]


def fill(ext, c, body, xlo, xhi, low, high):
    zero4 = jnp.zeros((4, 128), F32)
    ext[rows_of(c, 0, 4), :] = zero4
    ext[rows_of(c, 4, 4), :] = xlo * low
    ext[rows_of(c, 8, CX), :] = body
    ext[rows_of(c, 8 + CX, 4), :] = xhi * high
    ext[rows_of(c, 12 + CX, 4), :] = zero4


def inner_kernel(flags, lat, kap, xhi, xlo, val, var, tiles, value, weight, odd, ext, alpha, u3, u2, u1, kext):
    for c in range(BLOCKS):
        fill(ext, c, lat[:, lanes(c)], xlo[:, lanes(c)], xhi[:, lanes(c)], flags[0:1, :], flags[1:2, :])
    kappa_rows(kext, kap, xlo, xhi)
    spread_kappa(alpha, kext[0:TALL, :] - CENTRE, BLOCKS, 0)

    def run(src, depth, step, scale, store, at=0, count=TALL):
        order = [(c, max(c - 1, 0), min(c + 1, BLOCKS - 1)) for c in range(depth, BLOCKS - depth)]
        get = lambda c, shift: src[rows_of(c, shift, count), :]
        xi = lambda c: ext[rows_of(c, at, count), :]
        diag = lambda c: alpha[rows_of(c, at, count), :]
        sweep(get, xi, diag, order, COEFFS[step], scale, store, at, count)

    run(ext, 0, 3, COEFFS[4], keep_rows(u3, flags))
    run(u3, 1, 2, 1.0, keep_rows(u2, flags))
    run(u2, 1, 1, 1.0, keep_rows(u1, flags))
    run(u1, 2, 0, 1.0, lambda c, new: into_tiles(tiles, c, new), 8, CX)

    def column(row):
        pieces = [jnp.transpose(jnp.broadcast_to(row[i : i + 1, :], (128, 128))) for i in range(OBS // 128)]
        return jnp.concatenate(pieces, axis=0)

    value[...] = column(val[0:2, :])
    odd[...] = column(val[2:4, :])
    weight[...] = 1.0 / column(var[0:2, :])


def rim_kernel(
    flags, cell_vmem, y_odd, y_even, value, weight, odd, ext, alpha, u3, u2, u1, held,
    tiles, stat, cell, sem, ext_out, alpha_out, v3, v2, v1, kext, pbuf,
):
    fetch = pltpu.make_async_copy(cell_vmem, cell, sem)
    fetch.start()
    low, high = flags[0:1, :], flags[1:2, :]
    kext[...] = jnp.zeros((128, 128), F32)
    is_odd = jnp.broadcast_to(flags[4:5, :], (CX + 16, 128)) > 0.5
    is_odd = jnp.concatenate([is_odd, is_odd], axis=1)
    for side in range(2):
        lower, upper = (y_even, y_odd) if side == 0 else (y_odd, y_even)
        msg = jnp.where(is_odd, lower[...], upper[...])
        flag = flags[2 + side : 3 + side, :]
        kext[0:4, :] = msg[CX + 8 : CX + 12, 0:128]
        shifted = jnp.transpose(kext[...])[0:TALL, :] - CENTRE
        upper = (lax.broadcasted_iota(jnp.int32, (TALL, 128), 1) >= MEMBERS).astype(jnp.int32)
        for p in (-2, -1):
            i = p + 2 if side == 0 else -1 - p
            halo = msg[CX : CX + 4, lanes(i)], msg[CX + 4 : CX + 8, lanes(i)]
            fill(ext_out, p + 2, msg[0:CX, lanes(i)] * flag, *halo, low * flag, high * flag)
            alpha_out[rows_of(p + 2), :] = jnp.take_along_axis(shifted, upper + 2 * i, axis=1)

        def local(p):
            return p if side == 0 else BLOCKS - 1 - p

        def run(near, far, mine, first, last, step, scale, store, at=0, count=TALL):
            def pick(p, here, there, ours, start):
                return here[rows_of(p + 2, start, count), :] if p in ours else there[rows_of(local(p), start, count), :]

            get = lambda p, shift: pick(p, near, far, mine, shift)
            xi = lambda p: pick(p, ext_out, ext, (-2, -1), at)
            diag = lambda p: pick(p, alpha_out, alpha, (-2, -1), at)
            order = [(p, max(p - 1, -2), p + 1) for p in range(first, last + 1)]
            if side == 1:
                order = [(p, b, a) for p, a, b in order]
            sweep(get, xi, diag, order, COEFFS[step], scale, store, at, count)

        def keep(dst):
            plain = keep_rows(dst, flags)
            return lambda p, new: plain(p + 2, new * flag if p < 0 else new)

        run(ext_out, ext, (-2, -1), -2, 0, 3, COEFFS[4], keep(v3))
        run(v3, u3, (-2, -1, 0), -1, 0, 2, 1.0, keep(v2))
        run(v2, u2, (-2, -1, 0), -1, 1, 1, 1.0, keep(v1))
        run(v1, u1, (-2, -1, 0, 1), 0, 1, 0, 1.0, lambda p, new: into_tiles(tiles, local(p), new), 8, CX)

    fetch.wait()
    for j in range(OBS):
        pbuf[j : j + 1, :] = tiles[pl.ds(cell[j], 1), :]
    both = pbuf[...]
    lane = lax.broadcasted_iota(jnp.int32, (OBS, 128), 1)
    member = lane < MEMBERS
    predicted = jnp.where(odd[...] > 0.5, pltpu.roll(both, 64, 1), both)
    predicted = jnp.where(member, predicted, 0.0)
    mean = jnp.sum(predicted, axis=1, keepdims=True) * (1.0 / MEMBERS)
    spread = jnp.where(member, predicted - mean, jnp.where(lane == MEMBERS, value[...] - mean, 0.0))
    full = lax.dot_general(
        spread * weight[...],
        spread,
        (((0,), (0,)), ((), ())),
        precision=lax.Precision.HIGHEST,
        preferred_element_type=F32,
    )
    lane = lax.broadcasted_iota(jnp.int32, (HALF, 128), 1)
    row = lax.broadcasted_iota(jnp.int32, (HALF, 128), 0)
    first, second = full[0:HALF], full[HALF:MEMBERS]
    packed = jnp.where(lane >= row, first, pltpu.roll(second, 96, 1))
    folded = jnp.where(lane[0:16] < MEMBERS, packed[0:16], pltpu.roll(packed[16:32], 64, 1))
    diagonal = jnp.sum(jnp.where(lane == row + 96, pltpu.roll(second, 64, 1), 0.0), axis=0, keepdims=True)
    last = jnp.where(lane[0:1] < 96, full[MEMBERS : MEMBERS + 1], diagonal)
    stat[0 : STAT - 1, :] = folded
    stat[STAT - 1 : STAT, :] = last


def eliminate(aug):
    size = 8
    row = lax.broadcasted_iota(jnp.int32, (size, 128), 0)
    for start in range(0, MEMBERS, size):
        columns = [jnp.broadcast_to(aug[:, k : k + 1], (MEMBERS, 128)) for k in range(start, start + size)]
        block = [column[start : start + size] for column in columns]
        pivot_rows = aug[start : start + size]
        for i in range(size):
            here = row == i
            inverse = 1.0 / block[i][i : i + 1]

            def clear(a):
                scaled = a[i : i + 1] * inverse
                return jnp.where(here, scaled, a - block[i] * scaled)

            block = block[: i + 1] + [clear(a) for a in block[i + 1 :]]
            pivot_rows = clear(pivot_rows)
        pieces = []
        for at in range(0, MEMBERS, size):
            if at == start:
                pieces.append(pivot_rows)
                continue
            terms = [column[at : at + size] * pivot_rows[i : i + 1] for i, column in enumerate(columns)]
            while len(terms) > 1:
                terms = [a + b for a, b in zip(terms[0::2], terms[1::2])]
            pieces.append(aug[at : at + size] - terms[0])
        aug = jnp.concatenate(pieces, axis=0)
    return aug


def split(a):
    hi = a.astype(jnp.bfloat16)
    return hi, (a - hi.astype(F32)).astype(jnp.bfloat16)


def solve_kernel(parts, tiles, weights_out, prior_hbm, total, sem):
    copy = pltpu.make_async_copy(tiles, prior_hbm, sem)
    copy.start()
    for i in range(STAT):
        row = parts[0, i]
        for d in range(1, parts.shape[0]):
            row = row + parts[d, i]
        total[i : i + 1, :] = row
    folded, last = total[0:16, :], total[16:17, :]
    packed = jnp.concatenate([folded, pltpu.roll(folded, 64, 1)], axis=0)
    tall = jnp.concatenate([packed, jnp.zeros((32, 128), F32), jnp.broadcast_to(last, (64, 128))], axis=0)
    turned = jnp.transpose(tall)
    lane = lax.broadcasted_iota(jnp.int32, (HALF, 128), 1)
    row = lax.broadcasted_iota(jnp.int32, (HALF, 128), 0)
    first = jnp.where(lane >= row, packed, turned[0:HALF])
    corner = jnp.where(lane < row + HALF, pltpu.roll(packed, 32, 1), pltpu.roll(turned[0:HALF], 32, 1))
    corner = jnp.where(lane == row + HALF, pltpu.roll(last, 64, 1), corner)
    second = jnp.where(lane < HALF, turned[HALF:MEMBERS], corner)
    gram = jnp.concatenate([first, second], axis=0)

    shape = (MEMBERS, 128)
    row = lax.broadcasted_iota(jnp.int32, shape, 0)
    lane = lax.broadcasted_iota(jnp.int32, shape, 1)
    eye = row == lane
    low = lane < MEMBERS
    square = jnp.where(lane[0:1] == MEMBERS, last, 0.0) * float(MEMBERS)
    trace = jnp.sum(jnp.where(eye, gram, 0.0), axis=0, keepdims=True)
    misfit = jnp.sum(square + trace, axis=1, keepdims=True)
    inflation = 1.0 + misfit / float(MEMBERS * (MEMBERS - 1))
    shift = (MEMBERS - 1) * inflation
    right = turned[0:MEMBERS] - pltpu.roll(gram, 64, 1)
    aug = eliminate(jnp.where(low, gram + jnp.where(eye, shift, 0.0), right))
    gain = aug - jnp.sum(aug, axis=0, keepdims=True) * (1.0 / MEMBERS)
    weights = jnp.concatenate(
        [jnp.where(low, pltpu.roll(gain, 64, 1), 0.0), jnp.where(low, 0.0, gain)], axis=0
    )

    w_hi, w_lo = split(weights)
    weights_out[0:128, 0:128] = w_hi
    weights_out[0:128, 128:256] = w_lo
    weights_out[128:256, 0:128] = w_hi
    weights_out[128:256, 128:256] = jnp.zeros((128, 128), jnp.bfloat16)
    copy.wait()


def update_kernel(lat, weights, out_hbm, out, sems):
    both = weights[...]
    copies = []
    for t in range(CX // 8):
        at = slice(t * 256, (t + 1) * 256)
        x = lat[at, :]
        product = jnp.dot(jnp.concatenate(split(x), axis=1), both, preferred_element_type=F32)
        out[at, :] = x + (product[:, 0:128] + product[:, 128:256])
        copies.append(pltpu.make_async_copy(out.at[at, :], out_hbm.at[at, :], sems.at[t]))
        copies[-1].start()
    for copy in copies:
        copy.wait()


def ring(axis, step):
    count = lax.axis_size(axis)
    return [(i, (i + step) % count) for i in range(count)]


def pairs(axis, first):
    count = lax.axis_size(axis)
    ends = [(i % count, (i + 1) % count) for i in range(first, count + first, 2)]
    return sorted(ends + [(b, a) for a, b in ends])


def arr(*shape):
    return jax.ShapeDtypeStruct(shape, F32)


def buf(*shape):
    return pltpu.VMEM(shape, F32)


def params(mib):
    return pltpu.CompilerParams(vmem_limit_bytes=mib << 20)


def cost(flops, moved):
    return pl.CostEstimate(flops=flops, bytes_accessed=moved, transcendentals=0)


def to_tiles(a):
    return a.reshape(CX // 8, 8, BLOCKS, 128).transpose(0, 2, 1, 3).reshape(CX * BLOCKS, 128)


def from_tiles(a):
    return a.reshape(CX // 8, BLOCKS, 8, 128).transpose(0, 2, 1, 3).reshape(CX, WIDTH)


def per_device(latent, kappa, obs_cell, obs_value, obs_var):
    gx, gy = lax.axis_index("gx"), lax.axis_index("gy")
    last_x, last_y = lax.axis_size("gx") - 1, lax.axis_size("gy") - 1
    states = [gx > 0, gx < last_x, gy > 0, gy < last_y, gy % 2 == 1]
    flags = jnp.broadcast_to(jnp.stack(states + states[:3]).astype(F32)[:, None], (8, 128))
    odd = (obs_cell & 1).astype(F32)
    obs_x, obs_y = obs_cell >> 6, obs_cell & (CY - 1)
    obs_row = (obs_x & 56) * BLOCKS + (obs_y >> 1) * 8 + (obs_x & 7)
    val = jnp.concatenate([obs_value.reshape(2, 128), odd.reshape(2, 128)], axis=0)
    var = obs_var.reshape(2, 128)
    vmem, anywhere = pl.BlockSpec(memory_space=VMEM), pl.BlockSpec(memory_space=pl.ANY)
    hbm = pl.BlockSpec(memory_space=pltpu.MemorySpace.HBM)

    def part(shape, *at):
        return pl.BlockSpec(shape, lambda i: at)

    to_lo, to_hi, kappa = pl.pallas_call(
        rows_kernel,
        out_shape=(arr(HALO, WIDTH + 128),) * 2 + (arr(CX, CY),),
        in_specs=[hbm, hbm],
        out_specs=(vmem,) * 3,
        scratch_shapes=[pltpu.SemaphoreType.DMA((3,))],
        compiler_params=params(4),
        name="rows",
    )(*(pltpu.with_memory_space_constraint(a, pltpu.MemorySpace.HBM) for a in (latent, kappa)))
    xhi = lax.ppermute(to_lo, "gx", ring("gx", -1))
    xlo = lax.ppermute(to_hi, "gx", ring("gx", 1))

    whole = part((HALO, WIDTH + 128), 0, 0)
    to_odd, to_even = pl.pallas_call(
        cols_kernel,
        grid=(1,),
        out_shape=(arr(CX + 16, EDGE),) * 2,
        in_specs=[part((8, 128), 0, 0), part((CX, EDGE), 0, 0), part((CX, EDGE), 0, WIDTH // EDGE - 1), part((CX, CY), 0, 0), whole, whole],
        out_specs=(part((CX + 16, EDGE), 0, 0),) * 2,
        scratch_shapes=[buf(128, 128)],
        compiler_params=params(4),
        name="cols",
    )(flags, latent, latent, kappa, xhi, xlo)
    y_odd = lax.ppermute(to_odd, "gy", pairs("gy", 1))
    y_even = lax.ppermute(to_even, "gy", pairs("gy", 0))

    field = arr(BLOCKS * TALL + 2 * PAD, 128)
    tiles, *rest = pl.pallas_call(
        inner_kernel,
        out_shape=(arr(CX * BLOCKS, 128),) + (arr(OBS, 128),) * 3 + (field,) * 5,
        in_specs=[vmem] * 7,
        out_specs=(vmem,) * 9,
        scratch_shapes=[buf(128, 128)],
        compiler_params=params(12),
        cost_estimate=cost(20_000_000, 12_000_000),
        name="inner",
    )(flags, latent, kappa, xhi, xlo, val, var)

    tiles, stat = pl.pallas_call(
        rim_kernel,
        out_shape=(arr(CX * BLOCKS, 128), arr(STAT, 128)),
        in_specs=[vmem, anywhere] + [vmem] * 11,
        out_specs=(vmem, vmem),
        scratch_shapes=[pltpu.SMEM((OBS,), jnp.int32), pltpu.SemaphoreType.DMA]
        + [stencil_buf(4)] * 5
        + [buf(128, 128), buf(OBS, 128)],
        input_output_aliases={12: 0},
        compiler_params=params(12),
        name="rim",
    )(flags, obs_row, y_odd, y_even, *rest, tiles)

    stat = stat[:, None, :]
    stat = stat + lax.ppermute(stat, "gx", pairs("gx", 0))
    width = lax.axis_size("gy")
    parts = lax.all_to_all(jnp.broadcast_to(stat[None], (width,) + stat.shape), "gy", 0, 0)
    stat = jnp.sum(parts, axis=0)
    count = lax.axis_size("gx")
    groups = [list(range(i, count, 2)) for i in range(2)]
    parts = jnp.broadcast_to(stat[None], (count // 2,) + stat.shape)
    parts = lax.all_to_all(parts, "gx", 0, 0, axis_index_groups=groups)

    weights, prior = pl.pallas_call(
        solve_kernel,
        out_shape=(jax.ShapeDtypeStruct((256, 256), jnp.bfloat16), arr(CX * BLOCKS, 128)),
        in_specs=[vmem] * 2,
        out_specs=(vmem, anywhere),
        scratch_shapes=[buf(24, 128), pltpu.SemaphoreType.DMA],
        compiler_params=params(12),
        name="solve",
    )(parts, tiles)
    latent_new = pl.pallas_call(
        update_kernel,
        out_shape=arr(CX * BLOCKS, 128),
        in_specs=[vmem] * 2,
        out_specs=anywhere,
        scratch_shapes=[buf(CX * BLOCKS, 128), pltpu.SemaphoreType.DMA((CX // 8,))],
        compiler_params=params(12),
        name="update",
    )(to_tiles(latent), weights)
    return (from_tiles(latent_new), from_tiles(prior))


def solution(mesh):
    placed = (P("gx", "gy"), P("gx", "gy"), P(("gx", "gy")), P(("gx", "gy")), P(("gx", "gy")))
    return jax.shard_map(
        per_device,
        mesh=mesh,
        in_specs=placed,
        out_specs=(P("gx", "gy"), P("gx", "gy")),
        check_vma=False,
    )
```

```python
import jax
import jax.numpy as jnp
import numpy as np
from jax import lax
from jax.experimental import pallas as pl
from jax.experimental.pallas import tpu as pltpu
from jax.sharding import PartitionSpec as P

MEMBERS = 64
SWEEPS = 4
LOWER_EDGE = 0.25
UPPER_EDGE = 12.0
HALO = SWEEPS
CX = 64
CY = 64
OBS = 256
TALL = CX + 16
WIDTH = CY * MEMBERS
BLOCKS = WIDTH // 128
EDGE = HALO * MEMBERS
STAT = 17
HALF = MEMBERS // 2
VMEM = pltpu.MemorySpace.VMEM
SMEM = pltpu.MemorySpace.SMEM
F32 = jnp.float32


def power_coeffs():
    angles = np.pi * (np.arange(64) + 0.5) / 64.0
    centre, half = 0.5 * (UPPER_EDGE + LOWER_EDGE), 0.5 * (UPPER_EDGE - LOWER_EDGE)
    nodes = centre + half * np.cos(angles)
    cheb = [2.0 / 64.0 * np.sum(np.cos(k * angles) / nodes) for k in range(SWEEPS + 1)]
    cheb[0] *= 0.5
    mono = np.polynomial.chebyshev.cheb2poly(cheb)
    return [float(v / half**k) for k, v in enumerate(mono)]


COEFFS = power_coeffs()
CENTRE = 0.5 * (UPPER_EDGE + LOWER_EDGE) - 4.0


PAD = 8


def lanes(c):
    return slice(c * 128, (c + 1) * 128)


def stencil_buf(blocks):
    return pltpu.VMEM((blocks * TALL + 2 * PAD, 128), F32)


def rows_of(c, first=0, count=TALL):
    at = PAD + c * TALL + first
    return slice(at, at + count)


def sweep(get, xi, alpha, order, coeff, scale, store, at=0, count=TALL):
    low_half = lax.broadcasted_iota(jnp.int32, (count, 128), 1) < MEMBERS
    turned = {}

    def turn(c):
        if c not in turned:
            turned[c] = pltpu.roll(get(c, at), 64, 1)
        return turned[c]

    for c, lower, upper in order:
        beside = turn(c) + jnp.where(low_half, turn(lower), turn(upper))
        beside = beside + (get(c, at - 1) + get(c, at + 1))
        applied = alpha(c) * get(c, at) - beside
        if scale != 1.0:
            applied = applied * scale
        store(c, coeff * xi(c) + applied)


def spread_kappa(alpha, shifted, count, start):
    upper = (lax.broadcasted_iota(jnp.int32, (TALL, 128), 1) >= MEMBERS).astype(jnp.int32)
    for c in range(count):
        alpha[rows_of(c), :] = jnp.take_along_axis(shifted, upper + (2 * c + start), axis=1)


def rows_kernel(lat_hbm, kap_hbm, to_odd, to_even, kap, sems):
    is_odd = lax.rem(lax.axis_index("gx"), 2) == 1
    fetch = pltpu.make_async_copy(kap_hbm, kap, sems.at[0])
    fetch.start()

    def copies(low, high):
        return (
            pltpu.make_async_copy(lat_hbm.at[0:HALO, :], low.at[:, 0:WIDTH], sems.at[1]),
            pltpu.make_async_copy(lat_hbm.at[CX - HALO : CX, :], high.at[:, 0:WIDTH], sems.at[2]),
        )

    @pl.when(is_odd)
    def _():
        for copy in copies(to_even, to_odd):
            copy.start()

    @pl.when(jnp.logical_not(is_odd))
    def _():
        for copy in copies(to_odd, to_even):
            copy.start()

    fetch.wait()
    blank = jnp.zeros((HALO, 128 - CY), F32)
    low = jnp.concatenate([kap[0:HALO, :], blank], axis=1)
    high = jnp.concatenate([kap[CX - HALO : CX, :], blank], axis=1)
    to_odd[:, WIDTH:] = jnp.where(is_odd, high, low)
    to_even[:, WIDTH:] = jnp.where(is_odd, low, high)
    for copy in copies(to_odd, to_even):
        copy.wait()


class Received:
    def __init__(self, flags, x_odd, x_even, below):
        self.is_odd = jnp.broadcast_to(flags[5:6, :], (HALO, 128)) > 0.5
        self.odd_has, self.even_has = (x_even, x_odd) if below else (x_odd, x_even)

    def __getitem__(self, c):
        return jnp.where(self.is_odd, self.odd_has[:, lanes(c)], self.even_has[:, lanes(c)])


def kappa_rows(dst, kap, xlo, xhi):
    dst[...] = jnp.zeros(dst.shape, F32)
    dst[8 : 8 + CX, 0:CY] = kap[...]
    dst[4:8, :] = xlo[BLOCKS]
    dst[8 + CX : 12 + CX, :] = xhi[BLOCKS]


def cols_kernel(flags, first, last, kap, x_odd, x_even, to_odd, to_even, kext):
    xlo, xhi = Received(flags, x_odd, x_even, True), Received(flags, x_odd, x_even, False)
    kappa_rows(kext, kap, xlo, xhi)
    turned = jnp.transpose(kext[...])
    is_odd = jnp.broadcast_to(flags[4:5, :], (8, 128)) > 0.5
    far = BLOCKS - 2
    for dst, swap in ((to_odd, False), (to_even, True)):

        def pick(low, high):
            low, high = (high, low) if swap else (low, high)
            return jnp.where(is_odd[0 : low.shape[0]], high, low)

        for i in range(2):
            for r in range(0, CX, 8):
                dst[r : r + 8, lanes(i)] = pick(first[r : r + 8, lanes(i)], last[r : r + 8, lanes(i)])
            dst[CX : CX + 4, lanes(i)] = pick(xlo[i], xlo[far + i])
            dst[CX + 4 : CX + 8, lanes(i)] = pick(xhi[i], xhi[far + i])
        columns = pick(turned[0:HALO, :], turned[CY - HALO : CY, :])
        for i in range(HALO):
            r = CX if i < 2 else CX + 7
            dst[r : r + 1, lanes(i % 2)] = columns[i : i + 1]


def keep_rows(dst, flags):
    def store(c, new):
        dst[rows_of(c, 0, 8), :] = new[0:8] * flags[0:1, :]
        dst[rows_of(c, 8, CX), :] = new[8 : 8 + CX]
        dst[rows_of(c, 8 + CX, 8), :] = new[8 + CX : TALL] * flags[1:2, :]

    return store


def into_tiles(tiles, c, new):
    for t in range(CX // 8):
        at = (t * BLOCKS + c) * 8
        tiles[at : at + 8, :] = new[8 * t : 8 * t + 8]


def fill(ext, c, body, xlo, xhi, low, high):
    zero4 = jnp.zeros((4, 128), F32)
    ext[rows_of(c, 0, 4), :] = zero4
    ext[rows_of(c, 4, 4), :] = xlo * low
    ext[rows_of(c, 8, CX), :] = body
    ext[rows_of(c, 8 + CX, 4), :] = xhi * high
    ext[rows_of(c, 12 + CX, 4), :] = zero4


def inner_kernel(flags, lat, kap, x_odd, x_even, val, var, tiles, value, weight, odd, ext, alpha, u3, u2, u1, kext):
    xlo, xhi = Received(flags, x_odd, x_even, True), Received(flags, x_odd, x_even, False)
    for c in range(BLOCKS):
        fill(ext, c, lat[:, lanes(c)], xlo[c], xhi[c], flags[0:1, :], flags[1:2, :])
    kappa_rows(kext, kap, xlo, xhi)
    spread_kappa(alpha, kext[0:TALL, :] - CENTRE, BLOCKS, 0)

    def run(src, depth, step, scale, store, at=0, count=TALL):
        order = [(c, max(c - 1, 0), min(c + 1, BLOCKS - 1)) for c in range(depth, BLOCKS - depth)]
        get = lambda c, shift: src[rows_of(c, shift, count), :]
        xi = lambda c: ext[rows_of(c, at, count), :]
        diag = lambda c: alpha[rows_of(c, at, count), :]
        sweep(get, xi, diag, order, COEFFS[step], scale, store, at, count)

    run(ext, 0, 3, COEFFS[4], keep_rows(u3, flags))
    run(u3, 1, 2, 1.0, keep_rows(u2, flags))
    run(u2, 1, 1, 1.0, keep_rows(u1, flags))
    run(u1, 2, 0, 1.0, lambda c, new: into_tiles(tiles, c, new), 8, CX)

    def column(row):
        pieces = [jnp.transpose(jnp.broadcast_to(row[i : i + 1, :], (128, 128))) for i in range(OBS // 128)]
        return jnp.concatenate(pieces, axis=0)

    value[...] = column(val[0:2, :])
    odd[...] = column(val[2:4, :])
    weight[...] = 1.0 / column(var[0:2, :])


def rim_kernel(
    flags, cell_vmem, y_odd, y_even, value, weight, odd, ext, alpha, u3, u2, u1, held,
    tiles, stat, cell, sem, ext_out, alpha_out, v3, v2, v1, kext, pbuf,
):
    fetch = pltpu.make_async_copy(cell_vmem, cell, sem)
    fetch.start()
    low, high = flags[0:1, :], flags[1:2, :]
    kext[...] = jnp.zeros((128, 128), F32)
    is_odd = jnp.broadcast_to(flags[4:5, :], (CX + 8, 128)) > 0.5
    is_odd = jnp.concatenate([is_odd, is_odd], axis=1)
    for side in range(2):
        lower, upper = (y_even, y_odd) if side == 0 else (y_odd, y_even)
        msg = jnp.where(is_odd, lower[...], upper[...])
        flag = flags[2 + side : 3 + side, :]
        for i in range(HALO):
            r = CX if i < 2 else CX + 7
            kext[i : i + 1, :] = msg[r : r + 1, lanes(i % 2)]
        shifted = jnp.transpose(kext[...])[0:TALL, :] - CENTRE
        upper = (lax.broadcasted_iota(jnp.int32, (TALL, 128), 1) >= MEMBERS).astype(jnp.int32)
        for p in (-2, -1):
            i = p + 2 if side == 0 else -1 - p
            halo = msg[CX : CX + 4, lanes(i)], msg[CX + 4 : CX + 8, lanes(i)]
            fill(ext_out, p + 2, msg[0:CX, lanes(i)] * flag, *halo, low * flag, high * flag)
            alpha_out[rows_of(p + 2), :] = jnp.take_along_axis(shifted, upper + 2 * i, axis=1)

        def local(p):
            return p if side == 0 else BLOCKS - 1 - p

        def run(near, far, mine, first, last, step, scale, store, at=0, count=TALL):
            def pick(p, here, there, ours, start):
                return here[rows_of(p + 2, start, count), :] if p in ours else there[rows_of(local(p), start, count), :]

            get = lambda p, shift: pick(p, near, far, mine, shift)
            xi = lambda p: pick(p, ext_out, ext, (-2, -1), at)
            diag = lambda p: pick(p, alpha_out, alpha, (-2, -1), at)
            order = [(p, max(p - 1, -2), p + 1) for p in range(first, last + 1)]
            if side == 1:
                order = [(p, b, a) for p, a, b in order]
            sweep(get, xi, diag, order, COEFFS[step], scale, store, at, count)

        def keep(dst):
            plain = keep_rows(dst, flags)
            return lambda p, new: plain(p + 2, new * flag if p < 0 else new)

        run(ext_out, ext, (-2, -1), -2, 0, 3, COEFFS[4], keep(v3))
        run(v3, u3, (-2, -1, 0), -1, 0, 2, 1.0, keep(v2))
        run(v2, u2, (-2, -1, 0), -1, 1, 1, 1.0, keep(v1))
        run(v1, u1, (-2, -1, 0, 1), 0, 1, 0, 1.0, lambda p, new: into_tiles(tiles, local(p), new), 8, CX)

    fetch.wait()
    for j in range(OBS):
        pbuf[j : j + 1, :] = tiles[pl.ds(cell[j], 1), :]
    both = pbuf[...]
    lane = lax.broadcasted_iota(jnp.int32, (OBS, 128), 1)
    member = lane < MEMBERS
    predicted = jnp.where(odd[...] > 0.5, pltpu.roll(both, 64, 1), both)
    predicted = jnp.where(member, predicted, 0.0)
    mean = jnp.sum(predicted, axis=1, keepdims=True) * (1.0 / MEMBERS)
    spread = jnp.where(member, predicted - mean, jnp.where(lane == MEMBERS, value[...] - mean, 0.0))
    full = lax.dot_general(
        spread * weight[...],
        spread,
        (((0,), (0,)), ((), ())),
        precision=lax.Precision.HIGHEST,
        preferred_element_type=F32,
    )
    lane = lax.broadcasted_iota(jnp.int32, (HALF, 128), 1)
    row = lax.broadcasted_iota(jnp.int32, (HALF, 128), 0)
    first, second = full[0:HALF], full[HALF:MEMBERS]
    packed = jnp.where(lane >= row, first, pltpu.roll(second, 96, 1))
    folded = jnp.where(lane[0:16] < MEMBERS, packed[0:16], pltpu.roll(packed[16:32], 64, 1))
    diagonal = jnp.sum(jnp.where(lane == row + 96, pltpu.roll(second, 64, 1), 0.0), axis=0, keepdims=True)
    last = jnp.where(lane[0:1] < 96, full[MEMBERS : MEMBERS + 1], diagonal)
    stat[0 : STAT - 1, :] = folded
    stat[STAT - 1 : STAT, :] = last


def eliminate(aug):
    size = 8
    row = lax.broadcasted_iota(jnp.int32, (size, 128), 0)
    for start in range(0, MEMBERS, size):
        columns = [jnp.broadcast_to(aug[:, k : k + 1], (MEMBERS, 128)) for k in range(start, start + size)]
        block = [column[start : start + size] for column in columns]
        pivot_rows = aug[start : start + size]
        for i in range(size):
            here = row == i
            inverse = 1.0 / block[i][i : i + 1]

            def clear(a):
                scaled = a[i : i + 1] * inverse
                return jnp.where(here, scaled, a - block[i] * scaled)

            block = block[: i + 1] + [clear(a) for a in block[i + 1 :]]
            pivot_rows = clear(pivot_rows)
        pieces = []
        for at in range(0, MEMBERS, size):
            if at == start:
                pieces.append(pivot_rows)
                continue
            terms = [column[at : at + size] * pivot_rows[i : i + 1] for i, column in enumerate(columns)]
            while len(terms) > 1:
                terms = [a + b for a, b in zip(terms[0::2], terms[1::2])]
            pieces.append(aug[at : at + size] - terms[0])
        aug = jnp.concatenate(pieces, axis=0)
    return aug


def split(a):
    hi = a.astype(jnp.bfloat16)
    return hi, (a - hi.astype(F32)).astype(jnp.bfloat16)


def solve_kernel(parts, tiles, weights_out, prior_hbm, total, sem):
    copy = pltpu.make_async_copy(tiles, prior_hbm, sem)
    copy.start()
    for i in range(STAT):
        row = parts[0, i]
        for d in range(1, parts.shape[0]):
            row = row + parts[d, i]
        total[i : i + 1, :] = row
    folded, last = total[0:16, :], total[16:17, :]
    packed = jnp.concatenate([folded, pltpu.roll(folded, 64, 1)], axis=0)
    tall = jnp.concatenate([packed, jnp.zeros((32, 128), F32), jnp.broadcast_to(last, (64, 128))], axis=0)
    turned = jnp.transpose(tall)
    lane = lax.broadcasted_iota(jnp.int32, (HALF, 128), 1)
    row = lax.broadcasted_iota(jnp.int32, (HALF, 128), 0)
    first = jnp.where(lane >= row, packed, turned[0:HALF])
    corner = jnp.where(lane < row + HALF, pltpu.roll(packed, 32, 1), pltpu.roll(turned[0:HALF], 32, 1))
    corner = jnp.where(lane == row + HALF, pltpu.roll(last, 64, 1), corner)
    second = jnp.where(lane < HALF, turned[HALF:MEMBERS], corner)
    gram = jnp.concatenate([first, second], axis=0)

    shape = (MEMBERS, 128)
    row = lax.broadcasted_iota(jnp.int32, shape, 0)
    lane = lax.broadcasted_iota(jnp.int32, shape, 1)
    eye = row == lane
    low = lane < MEMBERS
    square = jnp.where(lane[0:1] == MEMBERS, last, 0.0) * float(MEMBERS)
    trace = jnp.sum(jnp.where(eye, gram, 0.0), axis=0, keepdims=True)
    misfit = jnp.sum(square + trace, axis=1, keepdims=True)
    inflation = 1.0 + misfit / float(MEMBERS * (MEMBERS - 1))
    shift = (MEMBERS - 1) * inflation
    right = turned[0:MEMBERS] - pltpu.roll(gram, 64, 1)
    aug = eliminate(jnp.where(low, gram + jnp.where(eye, shift, 0.0), right))
    gain = aug - jnp.sum(aug, axis=0, keepdims=True) * (1.0 / MEMBERS)
    weights = jnp.concatenate(
        [jnp.where(low, pltpu.roll(gain, 64, 1), 0.0), jnp.where(low, 0.0, gain)], axis=0
    )

    w_hi, w_lo = split(weights)
    weights_out[0:128, 0:128] = w_hi
    weights_out[0:128, 128:256] = w_lo
    weights_out[128:256, 0:128] = w_hi
    weights_out[128:256, 128:256] = jnp.zeros((128, 128), jnp.bfloat16)
    copy.wait()


def update_kernel(lat, weights, out_hbm, out, sems):
    both = weights[...]
    copies = []
    for t in range(CX // 8):
        at = slice(t * 256, (t + 1) * 256)
        x = lat[at, :]
        product = jnp.dot(jnp.concatenate(split(x), axis=1), both, preferred_element_type=F32)
        out[at, :] = x + (product[:, 0:128] + product[:, 128:256])
        copies.append(pltpu.make_async_copy(out.at[at, :], out_hbm.at[at, :], sems.at[t]))
        copies[-1].start()
    for copy in copies:
        copy.wait()


def pairs(axis, first):
    count = lax.axis_size(axis)
    ends = [(i % count, (i + 1) % count) for i in range(first, count + first, 2)]
    return sorted(ends + [(b, a) for a, b in ends])


def arr(*shape):
    return jax.ShapeDtypeStruct(shape, F32)


def buf(*shape):
    return pltpu.VMEM(shape, F32)


def params(mib):
    return pltpu.CompilerParams(vmem_limit_bytes=mib << 20)


def cost(flops, moved):
    return pl.CostEstimate(flops=flops, bytes_accessed=moved, transcendentals=0)


def to_tiles(a):
    return a.reshape(CX // 8, 8, BLOCKS, 128).transpose(0, 2, 1, 3).reshape(CX * BLOCKS, 128)


def from_tiles(a):
    return a.reshape(CX // 8, BLOCKS, 8, 128).transpose(0, 2, 1, 3).reshape(CX, WIDTH)


def per_device(latent, kappa, obs_cell, obs_value, obs_var):
    gx, gy = lax.axis_index("gx"), lax.axis_index("gy")
    last_x, last_y = lax.axis_size("gx") - 1, lax.axis_size("gy") - 1
    states = [gx > 0, gx < last_x, gy > 0, gy < last_y, gy % 2 == 1, gx % 2 == 1]
    flags = jnp.broadcast_to(jnp.stack(states + states[:2]).astype(F32)[:, None], (8, 128))
    odd = (obs_cell & 1).astype(F32)
    obs_x, obs_y = obs_cell >> 6, obs_cell & (CY - 1)
    obs_row = (obs_x & 56) * BLOCKS + (obs_y >> 1) * 8 + (obs_x & 7)
    val = jnp.concatenate([obs_value.reshape(2, 128), odd.reshape(2, 128)], axis=0)
    var = obs_var.reshape(2, 128)
    vmem, anywhere = pl.BlockSpec(memory_space=VMEM), pl.BlockSpec(memory_space=pl.ANY)
    hbm = pl.BlockSpec(memory_space=pltpu.MemorySpace.HBM)

    def part(shape, *at):
        return pl.BlockSpec(shape, lambda i: at)

    to_odd, to_even, kappa = pl.pallas_call(
        rows_kernel,
        out_shape=(arr(HALO, WIDTH + 128),) * 2 + (arr(CX, CY),),
        in_specs=[hbm, hbm],
        out_specs=(vmem,) * 3,
        scratch_shapes=[pltpu.SemaphoreType.DMA((3,))],
        compiler_params=params(4),
        name="rows",
    )(*(pltpu.with_memory_space_constraint(a, pltpu.MemorySpace.HBM) for a in (latent, kappa)))
    x_odd = lax.ppermute(to_odd, "gx", pairs("gx", 1))
    x_even = lax.ppermute(to_even, "gx", pairs("gx", 0))

    whole = part((HALO, WIDTH + 128), 0, 0)
    to_odd, to_even = pl.pallas_call(
        cols_kernel,
        grid=(1,),
        out_shape=(arr(CX + 8, EDGE),) * 2,
        in_specs=[part((8, 128), 0, 0), part((CX, EDGE), 0, 0), part((CX, EDGE), 0, WIDTH // EDGE - 1), part((CX, CY), 0, 0), whole, whole],
        out_specs=(part((CX + 8, EDGE), 0, 0),) * 2,
        scratch_shapes=[buf(128, 128)],
        compiler_params=params(4),
        name="cols",
    )(flags, latent, latent, kappa, x_odd, x_even)
    y_odd = lax.ppermute(to_odd, "gy", pairs("gy", 1))
    y_even = lax.ppermute(to_even, "gy", pairs("gy", 0))

    field = arr(BLOCKS * TALL + 2 * PAD, 128)
    tiles, *rest = pl.pallas_call(
        inner_kernel,
        out_shape=(arr(CX * BLOCKS, 128),) + (arr(OBS, 128),) * 3 + (field,) * 5,
        in_specs=[vmem] * 7,
        out_specs=(vmem,) * 9,
        scratch_shapes=[buf(128, 128)],
        compiler_params=params(12),
        cost_estimate=cost(20_000_000, 12_000_000),
        name="inner",
    )(flags, latent, kappa, x_odd, x_even, val, var)

    tiles, stat = pl.pallas_call(
        rim_kernel,
        out_shape=(arr(CX * BLOCKS, 128), arr(STAT, 128)),
        in_specs=[vmem, anywhere] + [vmem] * 11,
        out_specs=(vmem, vmem),
        scratch_shapes=[pltpu.SMEM((OBS,), jnp.int32), pltpu.SemaphoreType.DMA]
        + [stencil_buf(4)] * 5
        + [buf(128, 128), buf(OBS, 128)],
        input_output_aliases={12: 0},
        compiler_params=params(12),
        name="rim",
    )(flags, obs_row, y_odd, y_even, *rest, tiles)

    stat = stat[:, None, :]
    stat = stat + lax.ppermute(stat, "gx", pairs("gx", 0))
    width = lax.axis_size("gy")
    parts = lax.all_to_all(jnp.broadcast_to(stat[None], (width,) + stat.shape), "gy", 0, 0)
    stat = jnp.sum(parts, axis=0)
    count = lax.axis_size("gx")
    groups = [list(range(i, count, 2)) for i in range(2)]
    parts = jnp.broadcast_to(stat[None], (count // 2,) + stat.shape)
    parts = lax.all_to_all(parts, "gx", 0, 0, axis_index_groups=groups)

    weights, prior = pl.pallas_call(
        solve_kernel,
        out_shape=(jax.ShapeDtypeStruct((256, 256), jnp.bfloat16), arr(CX * BLOCKS, 128)),
        in_specs=[vmem] * 2,
        out_specs=(vmem, anywhere),
        scratch_shapes=[buf(24, 128), pltpu.SemaphoreType.DMA],
        compiler_params=params(12),
        name="solve",
    )(parts, tiles)
    latent_new = pl.pallas_call(
        update_kernel,
        out_shape=arr(CX * BLOCKS, 128),
        in_specs=[vmem] * 2,
        out_specs=anywhere,
        scratch_shapes=[buf(CX * BLOCKS, 128), pltpu.SemaphoreType.DMA((CX // 8,))],
        compiler_params=params(12),
        name="update",
    )(to_tiles(latent), weights)
    return (from_tiles(latent_new), from_tiles(prior))


def solution(mesh):
    placed = (P("gx", "gy"), P("gx", "gy"), P(("gx", "gy")), P(("gx", "gy")), P(("gx", "gy")))
    return jax.shard_map(
        per_device,
        mesh=mesh,
        in_specs=placed,
        out_specs=(P("gx", "gy"), P("gx", "gy")),
        check_vma=False,
    )
```

```python
import jax
import jax.numpy as jnp
import numpy as np
from jax import lax
from jax.experimental import pallas as pl
from jax.experimental.pallas import tpu as pltpu
from jax.sharding import PartitionSpec as P

MEMBERS = 64
SWEEPS = 4
LOWER_EDGE = 0.25
UPPER_EDGE = 12.0
HALO = SWEEPS
CX = 64
CY = 64
OBS = 256
TALL = CX + 16
WIDTH = CY * MEMBERS
BLOCKS = WIDTH // 128
EDGE = HALO * MEMBERS
STAT = 17
HALF = MEMBERS // 2
VMEM = pltpu.MemorySpace.VMEM
SMEM = pltpu.MemorySpace.SMEM
F32 = jnp.float32


def power_coeffs():
    angles = np.pi * (np.arange(64) + 0.5) / 64.0
    centre, half = 0.5 * (UPPER_EDGE + LOWER_EDGE), 0.5 * (UPPER_EDGE - LOWER_EDGE)
    nodes = centre + half * np.cos(angles)
    cheb = [2.0 / 64.0 * np.sum(np.cos(k * angles) / nodes) for k in range(SWEEPS + 1)]
    cheb[0] *= 0.5
    mono = np.polynomial.chebyshev.cheb2poly(cheb)
    return [float(v / half**k) for k, v in enumerate(mono)]


COEFFS = power_coeffs()
CENTRE = 0.5 * (UPPER_EDGE + LOWER_EDGE) - 4.0


PAD = 8


def lanes(c):
    return slice(c * 128, (c + 1) * 128)


def stencil_buf(blocks):
    return pltpu.VMEM((blocks * TALL + 2 * PAD, 128), F32)


def rows_of(c, first=0, count=TALL):
    at = PAD + c * TALL + first
    return slice(at, at + count)


def sweep(get, xi, alpha, order, coeff, scale, store, at=0, count=TALL):
    low_half = lax.broadcasted_iota(jnp.int32, (count, 128), 1) < MEMBERS
    turned = {}

    def turn(c):
        if c not in turned:
            turned[c] = pltpu.roll(get(c, at), 64, 1)
        return turned[c]

    for c, lower, upper in order:
        beside = turn(c) + jnp.where(low_half, turn(lower), turn(upper))
        beside = beside + (get(c, at - 1) + get(c, at + 1))
        applied = alpha(c) * get(c, at) - beside
        if scale != 1.0:
            applied = applied * scale
        store(c, coeff * xi(c) + applied)


def spread_kappa(alpha, shifted, count, start):
    upper = (lax.broadcasted_iota(jnp.int32, (TALL, 128), 1) >= MEMBERS).astype(jnp.int32)
    for c in range(count):
        alpha[rows_of(c), :] = jnp.take_along_axis(shifted, upper + (2 * c + start), axis=1)


def rows_kernel(lat_hbm, kap_hbm, to_odd, to_even, kap, sems):
    is_odd = lax.rem(lax.axis_index("gx"), 2) == 1
    fetch = pltpu.make_async_copy(kap_hbm, kap, sems.at[0])
    fetch.start()

    def copies(low, high):
        return (
            pltpu.make_async_copy(lat_hbm.at[0:HALO, :], low.at[:, 0:WIDTH], sems.at[1]),
            pltpu.make_async_copy(lat_hbm.at[CX - HALO : CX, :], high.at[:, 0:WIDTH], sems.at[2]),
        )

    @pl.when(is_odd)
    def _():
        for copy in copies(to_even, to_odd):
            copy.start()

    @pl.when(jnp.logical_not(is_odd))
    def _():
        for copy in copies(to_odd, to_even):
            copy.start()

    fetch.wait()
    blank = jnp.zeros((HALO, 128 - CY), F32)
    low = jnp.concatenate([kap[0:HALO, :], blank], axis=1)
    high = jnp.concatenate([kap[CX - HALO : CX, :], blank], axis=1)
    to_odd[:, WIDTH:] = jnp.where(is_odd, high, low)
    to_even[:, WIDTH:] = jnp.where(is_odd, low, high)
    for copy in copies(to_odd, to_even):
        copy.wait()


class Received:
    def __init__(self, flags, x_odd, x_even, below):
        self.is_odd = jnp.broadcast_to(flags[5:6, :], (HALO, 128)) > 0.5
        self.odd_has, self.even_has = (x_even, x_odd) if below else (x_odd, x_even)

    def __getitem__(self, c):
        return jnp.where(self.is_odd, self.odd_has[:, lanes(c)], self.even_has[:, lanes(c)])


def kappa_rows(dst, kap, xlo, xhi):
    dst[...] = jnp.zeros(dst.shape, F32)
    dst[8 : 8 + CX, 0:CY] = kap[...]
    dst[4:8, :] = xlo[BLOCKS]
    dst[8 + CX : 12 + CX, :] = xhi[BLOCKS]


def cols_kernel(flags, first, last, kap, x_odd, x_even, to_odd, to_even, kext):
    xlo, xhi = Received(flags, x_odd, x_even, True), Received(flags, x_odd, x_even, False)
    kappa_rows(kext, kap, xlo, xhi)
    turned = jnp.transpose(kext[...])
    is_odd = jnp.broadcast_to(flags[4:5, :], (8, 128)) > 0.5
    far = BLOCKS - 2
    for dst, swap in ((to_odd, False), (to_even, True)):

        def pick(low, high):
            low, high = (high, low) if swap else (low, high)
            return jnp.where(is_odd[0 : low.shape[0]], high, low)

        for i in range(2):
            for r in range(0, CX, 8):
                dst[r : r + 8, lanes(i)] = pick(first[r : r + 8, lanes(i)], last[r : r + 8, lanes(i)])
            dst[CX : CX + 4, lanes(i)] = pick(xlo[i], xlo[far + i])
            dst[CX + 4 : CX + 8, lanes(i)] = pick(xhi[i], xhi[far + i])
        columns = pick(turned[0:HALO, :], turned[CY - HALO : CY, :])
        for i in range(HALO):
            r = CX if i < 2 else CX + 7
            dst[r : r + 1, lanes(i % 2)] = columns[i : i + 1]


def keep_rows(dst, flags):
    def store(c, new):
        dst[rows_of(c, 0, 8), :] = new[0:8] * flags[0:1, :]
        dst[rows_of(c, 8, CX), :] = new[8 : 8 + CX]
        dst[rows_of(c, 8 + CX, 8), :] = new[8 + CX : TALL] * flags[1:2, :]

    return store


def into_tiles(tiles, c, new):
    for t in range(CX // 8):
        at = (t * BLOCKS + c) * 8
        tiles[at : at + 8, :] = new[8 * t : 8 * t + 8]


def fill(ext, c, body, xlo, xhi, low, high):
    zero4 = jnp.zeros((4, 128), F32)
    ext[rows_of(c, 0, 4), :] = zero4
    ext[rows_of(c, 4, 4), :] = xlo * low
    ext[rows_of(c, 8, CX), :] = body
    ext[rows_of(c, 8 + CX, 4), :] = xhi * high
    ext[rows_of(c, 12 + CX, 4), :] = zero4


def inner_kernel(flags, lat, kap, x_odd, x_even, val, var, tiles, value, weight, odd, ext, alpha, u3, u2, u1, kext):
    xlo, xhi = Received(flags, x_odd, x_even, True), Received(flags, x_odd, x_even, False)
    for c in range(BLOCKS):
        fill(ext, c, lat[:, lanes(c)], xlo[c], xhi[c], flags[0:1, :], flags[1:2, :])
    kappa_rows(kext, kap, xlo, xhi)
    spread_kappa(alpha, kext[0:TALL, :] - CENTRE, BLOCKS, 0)

    def run(src, depth, step, scale, store, at=0, count=TALL):
        order = [(c, max(c - 1, 0), min(c + 1, BLOCKS - 1)) for c in range(depth, BLOCKS - depth)]
        get = lambda c, shift: src[rows_of(c, shift, count), :]
        xi = lambda c: ext[rows_of(c, at, count), :]
        diag = lambda c: alpha[rows_of(c, at, count), :]
        sweep(get, xi, diag, order, COEFFS[step], scale, store, at, count)

    run(ext, 0, 3, COEFFS[4], keep_rows(u3, flags))
    run(u3, 1, 2, 1.0, keep_rows(u2, flags))
    run(u2, 1, 1, 1.0, keep_rows(u1, flags))
    run(u1, 2, 0, 1.0, lambda c, new: into_tiles(tiles, c, new), 8, CX)

    def column(row):
        pieces = [jnp.transpose(jnp.broadcast_to(row[i : i + 1, :], (128, 128))) for i in range(OBS // 128)]
        return jnp.concatenate(pieces, axis=0)

    value[...] = column(val[0:2, :])
    odd[...] = column(val[2:4, :])
    weight[...] = 1.0 / column(var[0:2, :])


def rim_kernel(
    flags, cell_vmem, y_odd, y_even, value, weight, odd, ext, alpha, u3, u2, u1, held,
    tiles, stat, cell, sem, ext_out, alpha_out, v3, v2, v1, kext, pbuf,
):
    fetch = pltpu.make_async_copy(cell_vmem, cell, sem)
    fetch.start()
    low, high = flags[0:1, :], flags[1:2, :]
    kext[...] = jnp.zeros((128, 128), F32)
    is_odd = jnp.broadcast_to(flags[4:5, :], (CX + 8, 128)) > 0.5
    is_odd = jnp.concatenate([is_odd, is_odd], axis=1)
    for side in range(2):
        lower, upper = (y_even, y_odd) if side == 0 else (y_odd, y_even)
        msg = jnp.where(is_odd, lower[...], upper[...])
        flag = flags[2 + side : 3 + side, :]
        for i in range(HALO):
            r = CX if i < 2 else CX + 7
            kext[i : i + 1, :] = msg[r : r + 1, lanes(i % 2)]
        shifted = jnp.transpose(kext[...])[0:TALL, :] - CENTRE
        upper = (lax.broadcasted_iota(jnp.int32, (TALL, 128), 1) >= MEMBERS).astype(jnp.int32)
        for p in (-2, -1):
            i = p + 2 if side == 0 else -1 - p
            halo = msg[CX : CX + 4, lanes(i)], msg[CX + 4 : CX + 8, lanes(i)]
            fill(ext_out, p + 2, msg[0:CX, lanes(i)] * flag, *halo, low * flag, high * flag)
            alpha_out[rows_of(p + 2), :] = jnp.take_along_axis(shifted, upper + 2 * i, axis=1)

        def local(p):
            return p if side == 0 else BLOCKS - 1 - p

        def run(near, far, mine, first, last, step, scale, store, at=0, count=TALL):
            def pick(p, here, there, ours, start):
                return here[rows_of(p + 2, start, count), :] if p in ours else there[rows_of(local(p), start, count), :]

            get = lambda p, shift: pick(p, near, far, mine, shift)
            xi = lambda p: pick(p, ext_out, ext, (-2, -1), at)
            diag = lambda p: pick(p, alpha_out, alpha, (-2, -1), at)
            order = [(p, max(p - 1, -2), p + 1) for p in range(first, last + 1)]
            if side == 1:
                order = [(p, b, a) for p, a, b in order]
            sweep(get, xi, diag, order, COEFFS[step], scale, store, at, count)

        def keep(dst):
            plain = keep_rows(dst, flags)
            return lambda p, new: plain(p + 2, new * flag if p < 0 else new)

        run(ext_out, ext, (-2, -1), -2, 0, 3, COEFFS[4], keep(v3))
        run(v3, u3, (-2, -1, 0), -1, 0, 2, 1.0, keep(v2))
        run(v2, u2, (-2, -1, 0), -1, 1, 1, 1.0, keep(v1))
        run(v1, u1, (-2, -1, 0, 1), 0, 1, 0, 1.0, lambda p, new: into_tiles(tiles, local(p), new), 8, CX)

    fetch.wait()
    for j in range(OBS):
        pbuf[j : j + 1, :] = tiles[pl.ds(cell[j], 1), :]
    both = pbuf[...]
    lane = lax.broadcasted_iota(jnp.int32, (OBS, 128), 1)
    member = lane < MEMBERS
    predicted = jnp.where(odd[...] > 0.5, pltpu.roll(both, 64, 1), both)
    predicted = jnp.where(member, predicted, 0.0)
    mean = jnp.sum(predicted, axis=1, keepdims=True) * (1.0 / MEMBERS)
    spread = jnp.where(member, predicted - mean, jnp.where(lane == MEMBERS, value[...] - mean, 0.0))
    full = lax.dot_general(
        spread * weight[...],
        spread,
        (((0,), (0,)), ((), ())),
        precision=lax.Precision.HIGHEST,
        preferred_element_type=F32,
    )
    lane = lax.broadcasted_iota(jnp.int32, (HALF, 128), 1)
    row = lax.broadcasted_iota(jnp.int32, (HALF, 128), 0)
    first, second = full[0:HALF], full[HALF:MEMBERS]
    packed = jnp.where(lane >= row, first, pltpu.roll(second, 96, 1))
    folded = jnp.where(lane[0:16] < MEMBERS, packed[0:16], pltpu.roll(packed[16:32], 64, 1))
    diagonal = jnp.sum(jnp.where(lane == row + 96, pltpu.roll(second, 64, 1), 0.0), axis=0, keepdims=True)
    last = jnp.where(lane[0:1] < 96, full[MEMBERS : MEMBERS + 1], diagonal)
    stat[0 : STAT - 1, :] = folded
    stat[STAT - 1 : STAT, :] = last


def eliminate(aug):
    size = 8
    row = lax.broadcasted_iota(jnp.int32, (size, 128), 0)
    for start in range(0, MEMBERS, size):
        columns = [jnp.broadcast_to(aug[:, k : k + 1], (MEMBERS, 128)) for k in range(start, start + size)]
        block = [column[start : start + size] for column in columns]
        pivot_rows = aug[start : start + size]
        for i in range(size):
            here = row == i
            inverse = 1.0 / block[i][i : i + 1]

            def clear(a):
                scaled = a[i : i + 1] * inverse
                return jnp.where(here, scaled, a - block[i] * scaled)

            block = block[: i + 1] + [clear(a) for a in block[i + 1 :]]
            pivot_rows = clear(pivot_rows)
        pieces = []
        for at in range(0, MEMBERS, size):
            if at == start:
                pieces.append(pivot_rows)
                continue
            terms = [column[at : at + size] * pivot_rows[i : i + 1] for i, column in enumerate(columns)]
            while len(terms) > 1:
                terms = [a + b for a, b in zip(terms[0::2], terms[1::2])]
            pieces.append(aug[at : at + size] - terms[0])
        aug = jnp.concatenate(pieces, axis=0)
    return aug


def split(a):
    hi = a.astype(jnp.bfloat16)
    return hi, (a - hi.astype(F32)).astype(jnp.bfloat16)


def solve_kernel(parts, tiles, weights_out, prior_hbm, total, sem):
    copy = pltpu.make_async_copy(tiles, prior_hbm, sem)
    copy.start()
    for i in range(STAT):
        row = parts[0, i]
        for d in range(1, parts.shape[0]):
            row = row + parts[d, i]
        total[i : i + 1, :] = row
    folded, last = total[0:16, :], total[16:17, :]
    packed = jnp.concatenate([folded, pltpu.roll(folded, 64, 1)], axis=0)
    tall = jnp.concatenate([packed, jnp.zeros((32, 128), F32), jnp.broadcast_to(last, (64, 128))], axis=0)
    turned = jnp.transpose(tall)
    lane = lax.broadcasted_iota(jnp.int32, (HALF, 128), 1)
    row = lax.broadcasted_iota(jnp.int32, (HALF, 128), 0)
    first = jnp.where(lane >= row, packed, turned[0:HALF])
    corner = jnp.where(lane < row + HALF, pltpu.roll(packed, 32, 1), pltpu.roll(turned[0:HALF], 32, 1))
    corner = jnp.where(lane == row + HALF, pltpu.roll(last, 64, 1), corner)
    second = jnp.where(lane < HALF, turned[HALF:MEMBERS], corner)
    gram = jnp.concatenate([first, second], axis=0)

    shape = (MEMBERS, 128)
    row = lax.broadcasted_iota(jnp.int32, shape, 0)
    lane = lax.broadcasted_iota(jnp.int32, shape, 1)
    eye = row == lane
    low = lane < MEMBERS
    square = jnp.where(lane[0:1] == MEMBERS, last, 0.0) * float(MEMBERS)
    trace = jnp.sum(jnp.where(eye, gram, 0.0), axis=0, keepdims=True)
    misfit = jnp.sum(square + trace, axis=1, keepdims=True)
    inflation = 1.0 + misfit / float(MEMBERS * (MEMBERS - 1))
    shift = (MEMBERS - 1) * inflation
    right = turned[0:MEMBERS] - pltpu.roll(gram, 64, 1)
    aug = eliminate(jnp.where(low, gram + jnp.where(eye, shift, 0.0), right))
    gain = aug - jnp.sum(aug, axis=0, keepdims=True) * (1.0 / MEMBERS)
    weights = jnp.concatenate(
        [jnp.where(low, pltpu.roll(gain, 64, 1), 0.0), jnp.where(low, 0.0, gain)], axis=0
    )

    w_hi, w_lo = split(weights)
    weights_out[0:128, 0:128] = w_hi
    weights_out[0:128, 128:256] = w_lo
    weights_out[128:256, 0:128] = w_hi
    weights_out[128:256, 128:256] = jnp.zeros((128, 128), jnp.bfloat16)
    copy.wait()


def update_kernel(lat, weights, out_hbm, out, sems):
    both = weights[...]
    copies = []
    for t in range(CX // 8):
        at = slice(t * 256, (t + 1) * 256)
        x = lat[at, :]
        product = jnp.dot(jnp.concatenate(split(x), axis=1), both, preferred_element_type=F32)
        out[at, :] = x + (product[:, 0:128] + product[:, 128:256])
        copies.append(pltpu.make_async_copy(out.at[at, :], out_hbm.at[at, :], sems.at[t]))
        copies[-1].start()
    for copy in copies:
        copy.wait()


def pairs(axis, first):
    count_x, count_y = lax.axis_size("gx"), lax.axis_size("gy")
    count = count_x if axis == "gx" else count_y
    moves = []
    for x in range(count_x):
        for y in range(count_y):
            at = x if axis == "gx" else y
            to = at + 1 if (at - first) % 2 == 0 else at - 1
            if not 0 <= to < count:
                target = (x, y ^ 1) if axis == "gx" else (x ^ 1, y)
            else:
                target = (to, y) if axis == "gx" else (x, to)
            moves.append((x * count_y + y, target[0] * count_y + target[1]))
    return moves


def exchange(block, axis, first):
    return lax.ppermute(block, ("gx", "gy"), pairs(axis, first))


def arr(*shape):
    return jax.ShapeDtypeStruct(shape, F32)


def buf(*shape):
    return pltpu.VMEM(shape, F32)


def params(mib):
    return pltpu.CompilerParams(vmem_limit_bytes=mib << 20)


def cost(flops, moved):
    return pl.CostEstimate(flops=flops, bytes_accessed=moved, transcendentals=0)


def to_tiles(a):
    return a.reshape(CX // 8, 8, BLOCKS, 128).transpose(0, 2, 1, 3).reshape(CX * BLOCKS, 128)


def from_tiles(a):
    return a.reshape(CX // 8, BLOCKS, 8, 128).transpose(0, 2, 1, 3).reshape(CX, WIDTH)


def per_device(latent, kappa, obs_cell, obs_value, obs_var):
    gx, gy = lax.axis_index("gx"), lax.axis_index("gy")
    last_x, last_y = lax.axis_size("gx") - 1, lax.axis_size("gy") - 1
    states = [gx > 0, gx < last_x, gy > 0, gy < last_y, gy % 2 == 1, gx % 2 == 1]
    flags = jnp.broadcast_to(jnp.stack(states + states[:2]).astype(F32)[:, None], (8, 128))
    odd = (obs_cell & 1).astype(F32)
    obs_x, obs_y = obs_cell >> 6, obs_cell & (CY - 1)
    obs_row = (obs_x & 56) * BLOCKS + (obs_y >> 1) * 8 + (obs_x & 7)
    val = jnp.concatenate([obs_value.reshape(2, 128), odd.reshape(2, 128)], axis=0)
    var = obs_var.reshape(2, 128)
    vmem, anywhere = pl.BlockSpec(memory_space=VMEM), pl.BlockSpec(memory_space=pl.ANY)
    hbm = pl.BlockSpec(memory_space=pltpu.MemorySpace.HBM)

    def part(shape, *at):
        return pl.BlockSpec(shape, lambda i: at)

    to_odd, to_even, kappa = pl.pallas_call(
        rows_kernel,
        out_shape=(arr(HALO, WIDTH + 128),) * 2 + (arr(CX, CY),),
        in_specs=[hbm, hbm],
        out_specs=(vmem,) * 3,
        scratch_shapes=[pltpu.SemaphoreType.DMA((3,))],
        compiler_params=params(4),
        name="rows",
    )(*(pltpu.with_memory_space_constraint(a, pltpu.MemorySpace.HBM) for a in (latent, kappa)))
    x_odd = exchange(to_odd, "gx", 1)
    x_even = exchange(to_even, "gx", 0)

    whole = part((HALO, WIDTH + 128), 0, 0)
    to_odd, to_even = pl.pallas_call(
        cols_kernel,
        grid=(1,),
        out_shape=(arr(CX + 8, EDGE),) * 2,
        in_specs=[part((8, 128), 0, 0), part((CX, EDGE), 0, 0), part((CX, EDGE), 0, WIDTH // EDGE - 1), part((CX, CY), 0, 0), whole, whole],
        out_specs=(part((CX + 8, EDGE), 0, 0),) * 2,
        scratch_shapes=[buf(128, 128)],
        compiler_params=params(4),
        name="cols",
    )(flags, latent, latent, kappa, x_odd, x_even)
    y_odd = exchange(to_odd, "gy", 1)
    y_even = exchange(to_even, "gy", 0)

    field = arr(BLOCKS * TALL + 2 * PAD, 128)
    tiles, *rest = pl.pallas_call(
        inner_kernel,
        out_shape=(arr(CX * BLOCKS, 128),) + (arr(OBS, 128),) * 3 + (field,) * 5,
        in_specs=[vmem] * 7,
        out_specs=(vmem,) * 9,
        scratch_shapes=[buf(128, 128)],
        compiler_params=params(12),
        cost_estimate=cost(20_000_000, 12_000_000),
        name="inner",
    )(flags, latent, kappa, x_odd, x_even, val, var)

    tiles, stat = pl.pallas_call(
        rim_kernel,
        out_shape=(arr(CX * BLOCKS, 128), arr(STAT, 128)),
        in_specs=[vmem, anywhere] + [vmem] * 11,
        out_specs=(vmem, vmem),
        scratch_shapes=[pltpu.SMEM((OBS,), jnp.int32), pltpu.SemaphoreType.DMA]
        + [stencil_buf(4)] * 5
        + [buf(128, 128), buf(OBS, 128)],
        input_output_aliases={12: 0},
        compiler_params=params(12),
        name="rim",
    )(flags, obs_row, y_odd, y_even, *rest, tiles)

    stat = stat[:, None, :]
    stat = stat + exchange(stat, "gx", 0)
    width = lax.axis_size("gy")
    parts = lax.all_to_all(jnp.broadcast_to(stat[None], (width,) + stat.shape), "gy", 0, 0)
    stat = jnp.sum(parts, axis=0)
    count = lax.axis_size("gx")
    groups = [list(range(i, count, 2)) for i in range(2)]
    parts = jnp.broadcast_to(stat[None], (count // 2,) + stat.shape)
    parts = lax.all_to_all(parts, "gx", 0, 0, axis_index_groups=groups)

    weights, prior = pl.pallas_call(
        solve_kernel,
        out_shape=(jax.ShapeDtypeStruct((256, 256), jnp.bfloat16), arr(CX * BLOCKS, 128)),
        in_specs=[vmem] * 2,
        out_specs=(vmem, anywhere),
        scratch_shapes=[buf(24, 128), pltpu.SemaphoreType.DMA],
        compiler_params=params(12),
        name="solve",
    )(parts, tiles)
    latent_new = pl.pallas_call(
        update_kernel,
        out_shape=arr(CX * BLOCKS, 128),
        in_specs=[vmem] * 2,
        out_specs=anywhere,
        scratch_shapes=[buf(CX * BLOCKS, 128), pltpu.SemaphoreType.DMA((CX // 8,))],
        compiler_params=params(12),
        name="update",
    )(to_tiles(latent), weights)
    return (from_tiles(latent_new), from_tiles(prior))


def solution(mesh):
    placed = (P("gx", "gy"), P("gx", "gy"), P(("gx", "gy")), P(("gx", "gy")), P(("gx", "gy")))
    return jax.shard_map(
        per_device,
        mesh=mesh,
        in_specs=placed,
        out_specs=(P("gx", "gy"), P("gx", "gy")),
        check_vma=False,
    )
```

```python
import jax
import jax.numpy as jnp
import numpy as np
from jax import lax
from jax.experimental import pallas as pl
from jax.experimental.pallas import tpu as pltpu
from jax.sharding import PartitionSpec as P

MEMBERS = 64
SWEEPS = 4
LOWER_EDGE = 0.25
UPPER_EDGE = 12.0
HALO = SWEEPS
CX = 64
CY = 64
OBS = 256
TALL = CX + 16
WIDTH = CY * MEMBERS
BLOCKS = WIDTH // 128
EDGE = HALO * MEMBERS
STAT = 17
HALF = MEMBERS // 2
VMEM = pltpu.MemorySpace.VMEM
SMEM = pltpu.MemorySpace.SMEM
F32 = jnp.float32


def power_coeffs():
    angles = np.pi * (np.arange(64) + 0.5) / 64.0
    centre, half = 0.5 * (UPPER_EDGE + LOWER_EDGE), 0.5 * (UPPER_EDGE - LOWER_EDGE)
    nodes = centre + half * np.cos(angles)
    cheb = [2.0 / 64.0 * np.sum(np.cos(k * angles) / nodes) for k in range(SWEEPS + 1)]
    cheb[0] *= 0.5
    mono = np.polynomial.chebyshev.cheb2poly(cheb)
    return [float(v / half**k) for k, v in enumerate(mono)]


COEFFS = power_coeffs()
CENTRE = 0.5 * (UPPER_EDGE + LOWER_EDGE) - 4.0


PAD = 8


def lanes(c):
    return slice(c * 128, (c + 1) * 128)


def stencil_buf(blocks):
    return pltpu.VMEM((blocks * TALL + 2 * PAD, 128), F32)


def rows_of(c, first=0, count=TALL):
    at = PAD + c * TALL + first
    return slice(at, at + count)


def sweep(get, xi, alpha, order, coeff, scale, store, at=0, count=TALL):
    low_half = lax.broadcasted_iota(jnp.int32, (count, 128), 1) < MEMBERS
    turned = {}

    def turn(c):
        if c not in turned:
            turned[c] = pltpu.roll(get(c, at), 64, 1)
        return turned[c]

    for c, lower, upper in order:
        beside = turn(c) + jnp.where(low_half, turn(lower), turn(upper))
        beside = beside + (get(c, at - 1) + get(c, at + 1))
        applied = alpha(c) * get(c, at) - beside
        if scale != 1.0:
            applied = applied * scale
        store(c, coeff * xi(c) + applied)


def spread_kappa(alpha, shifted, count, start):
    upper = (lax.broadcasted_iota(jnp.int32, (TALL, 128), 1) >= MEMBERS).astype(jnp.int32)
    for c in range(count):
        alpha[rows_of(c), :] = jnp.take_along_axis(shifted, upper + (2 * c + start), axis=1)


def rows_kernel(lat_hbm, kap_hbm, to_odd, to_even, kap, sems):
    is_odd = lax.rem(lax.axis_index("gx"), 2) == 1
    fetch = pltpu.make_async_copy(kap_hbm, kap, sems.at[0])
    fetch.start()

    def copies(low, high):
        return (
            pltpu.make_async_copy(lat_hbm.at[0:HALO, :], low.at[:, 0:WIDTH], sems.at[1]),
            pltpu.make_async_copy(lat_hbm.at[CX - HALO : CX, :], high.at[:, 0:WIDTH], sems.at[2]),
        )

    @pl.when(is_odd)
    def _():
        for copy in copies(to_even, to_odd):
            copy.start()

    @pl.when(jnp.logical_not(is_odd))
    def _():
        for copy in copies(to_odd, to_even):
            copy.start()

    fetch.wait()
    blank = jnp.zeros((HALO, 128 - CY), F32)
    low = jnp.concatenate([kap[0:HALO, :], blank], axis=1)
    high = jnp.concatenate([kap[CX - HALO : CX, :], blank], axis=1)
    to_odd[:, WIDTH:] = jnp.where(is_odd, high, low)
    to_even[:, WIDTH:] = jnp.where(is_odd, low, high)
    for copy in copies(to_odd, to_even):
        copy.wait()


class Received:
    def __init__(self, flags, x_odd, x_even, below):
        self.is_odd = jnp.broadcast_to(flags[5:6, :], (HALO, 128)) > 0.5
        self.odd_has, self.even_has = (x_even, x_odd) if below else (x_odd, x_even)

    def __getitem__(self, c):
        return jnp.where(self.is_odd, self.odd_has[:, lanes(c)], self.even_has[:, lanes(c)])


def kappa_rows(dst, kap, xlo, xhi):
    dst[...] = jnp.zeros(dst.shape, F32)
    dst[8 : 8 + CX, 0:CY] = kap[...]
    dst[4:8, :] = xlo[BLOCKS]
    dst[8 + CX : 12 + CX, :] = xhi[BLOCKS]


def cols_kernel(flags, first, last, kap, x_odd, x_even, to_odd, to_even, kext):
    xlo, xhi = Received(flags, x_odd, x_even, True), Received(flags, x_odd, x_even, False)
    kappa_rows(kext, kap, xlo, xhi)
    turned = jnp.transpose(kext[...])
    is_odd = jnp.broadcast_to(flags[4:5, :], (8, 128)) > 0.5
    far = BLOCKS - 2
    for dst, swap in ((to_odd, False), (to_even, True)):

        def pick(low, high):
            low, high = (high, low) if swap else (low, high)
            return jnp.where(is_odd[0 : low.shape[0]], high, low)

        for i in range(2):
            for r in range(0, CX, 8):
                dst[r : r + 8, lanes(i)] = pick(first[r : r + 8, lanes(i)], last[r : r + 8, lanes(i)])
            dst[CX : CX + 4, lanes(i)] = pick(xlo[i], xlo[far + i])
            dst[CX + 4 : CX + 8, lanes(i)] = pick(xhi[i], xhi[far + i])
        columns = pick(turned[0:HALO, :], turned[CY - HALO : CY, :])
        for i in range(HALO):
            r = CX if i < 2 else CX + 7
            dst[r : r + 1, lanes(i % 2)] = columns[i : i + 1]


def keep_rows(dst, flags):
    def store(c, new):
        dst[rows_of(c, 0, 8), :] = new[0:8] * flags[0:1, :]
        dst[rows_of(c, 8, CX), :] = new[8 : 8 + CX]
        dst[rows_of(c, 8 + CX, 8), :] = new[8 + CX : TALL] * flags[1:2, :]

    return store


def into_tiles(tiles, c, new):
    for t in range(CX // 8):
        at = (t * BLOCKS + c) * 8
        tiles[at : at + 8, :] = new[8 * t : 8 * t + 8]


def fill(ext, c, body, xlo, xhi, low, high):
    zero4 = jnp.zeros((4, 128), F32)
    ext[rows_of(c, 0, 4), :] = zero4
    ext[rows_of(c, 4, 4), :] = xlo * low
    ext[rows_of(c, 8, CX), :] = body
    ext[rows_of(c, 8 + CX, 4), :] = xhi * high
    ext[rows_of(c, 12 + CX, 4), :] = zero4


def inner_kernel(flags, lat, kap, x_odd, x_even, val, var, tiles, value, weight, odd, ext, alpha, u3, u2, u1, kext):
    xlo, xhi = Received(flags, x_odd, x_even, True), Received(flags, x_odd, x_even, False)
    for c in range(BLOCKS):
        fill(ext, c, lat[:, lanes(c)], xlo[c], xhi[c], flags[0:1, :], flags[1:2, :])
    kappa_rows(kext, kap, xlo, xhi)
    spread_kappa(alpha, kext[0:TALL, :] - CENTRE, BLOCKS, 0)

    def run(src, depth, step, scale, store, at=0, count=TALL):
        order = [(c, max(c - 1, 0), min(c + 1, BLOCKS - 1)) for c in range(depth, BLOCKS - depth)]
        get = lambda c, shift: src[rows_of(c, shift, count), :]
        xi = lambda c: ext[rows_of(c, at, count), :]
        diag = lambda c: alpha[rows_of(c, at, count), :]
        sweep(get, xi, diag, order, COEFFS[step], scale, store, at, count)

    run(ext, 0, 3, COEFFS[4], keep_rows(u3, flags))
    run(u3, 1, 2, 1.0, keep_rows(u2, flags))
    run(u2, 1, 1, 1.0, keep_rows(u1, flags))
    run(u1, 2, 0, 1.0, lambda c, new: into_tiles(tiles, c, new), 8, CX)

    def column(row):
        pieces = [jnp.transpose(jnp.broadcast_to(row[i : i + 1, :], (128, 128))) for i in range(OBS // 128)]
        return jnp.concatenate(pieces, axis=0)

    value[...] = column(val[0:2, :])
    odd[...] = column(val[2:4, :])
    weight[...] = 1.0 / column(var[0:2, :])


def rim_kernel(
    flags, cell_vmem, y_odd, y_even, value, weight, odd, ext, alpha, u3, u2, u1, held,
    tiles, stat, cell, sem, kext, pbuf, *own,
):
    fetch = pltpu.make_async_copy(cell_vmem, cell, sem)
    fetch.start()
    low, high = flags[0:1, :], flags[1:2, :]
    is_odd = jnp.broadcast_to(flags[4:5, :], (CX + 8, 128)) > 0.5
    is_odd = jnp.concatenate([is_odd, is_odd], axis=1)
    odd_has, even_has = y_odd[...], y_even[...]
    messages = (jnp.where(is_odd, even_has, odd_has), jnp.where(is_odd, odd_has, even_has))
    kext[...] = jnp.zeros((128, 128), F32)
    for side, msg in enumerate(messages):
        for i in range(HALO):
            r = CX if i < 2 else CX + 7
            kext[side * HALO + i : side * HALO + i + 1, :] = msg[r : r + 1, lanes(i % 2)]
    shifted = jnp.transpose(kext[...])[0:TALL, :] - CENTRE
    upper = (lax.broadcasted_iota(jnp.int32, (TALL, 128), 1) >= MEMBERS).astype(jnp.int32)
    bufs = (own[0:5], own[5:10])

    def local(side, p):
        return p if side == 0 else BLOCKS - 1 - p

    for side, msg in enumerate(messages):
        flag = flags[2 + side : 3 + side, :]
        ext_out, alpha_out = bufs[side][0:2]
        for p in (-2, -1):
            i = p + 2 if side == 0 else -1 - p
            halo = msg[CX : CX + 4, lanes(i)], msg[CX + 4 : CX + 8, lanes(i)]
            fill(ext_out, p + 2, msg[0:CX, lanes(i)] * flag, *halo, low * flag, high * flag)
            alpha_out[rows_of(p + 2), :] = jnp.take_along_axis(shifted, upper + (side * HALO + 2 * i), axis=1)

    def run(side, near, far, mine, first, last, step, scale, store, at=0, count=TALL):
        def pick(p, here, there, ours, start):
            return here[rows_of(p + 2, start, count), :] if p in ours else there[rows_of(local(side, p), start, count), :]

        ext_out, alpha_out = bufs[side][0:2]
        get = lambda p, shift: pick(p, near, far, mine, shift)
        xi = lambda p: pick(p, ext_out, ext, (-2, -1), at)
        diag = lambda p: pick(p, alpha_out, alpha, (-2, -1), at)
        order = [(p, max(p - 1, -2), p + 1) for p in range(first, last + 1)]
        if side == 1:
            order = [(p, b, a) for p, a, b in order]
        sweep(get, xi, diag, order, COEFFS[step], scale, store, at, count)

    def keep(side, dst):
        plain = keep_rows(dst, flags)
        flag = flags[2 + side : 3 + side, :]
        return lambda p, new: plain(p + 2, new * flag if p < 0 else new)

    for side in range(2):
        ext_out, _, v3, _, _ = bufs[side]
        run(side, ext_out, ext, (-2, -1), -2, 0, 3, COEFFS[4], keep(side, v3))
    for side in range(2):
        _, _, v3, v2, _ = bufs[side]
        run(side, v3, u3, (-2, -1, 0), -1, 0, 2, 1.0, keep(side, v2))
    for side in range(2):
        _, _, _, v2, v1 = bufs[side]
        run(side, v2, u2, (-2, -1, 0), -1, 1, 1, 1.0, keep(side, v1))
    for side in range(2):
        finish = lambda p, new, side=side: into_tiles(tiles, local(side, p), new)
        run(side, bufs[side][4], u1, (-2, -1, 0, 1), 0, 1, 0, 1.0, finish, 8, CX)

    fetch.wait()
    for j in range(OBS):
        pbuf[j : j + 1, :] = tiles[pl.ds(cell[j], 1), :]
    both = pbuf[...]
    lane = lax.broadcasted_iota(jnp.int32, (OBS, 128), 1)
    member = lane < MEMBERS
    predicted = jnp.where(odd[...] > 0.5, pltpu.roll(both, 64, 1), both)
    predicted = jnp.where(member, predicted, 0.0)
    mean = jnp.sum(predicted, axis=1, keepdims=True) * (1.0 / MEMBERS)
    spread = jnp.where(member, predicted - mean, jnp.where(lane == MEMBERS, value[...] - mean, 0.0))
    full = lax.dot_general(
        spread * weight[...],
        spread,
        (((0,), (0,)), ((), ())),
        precision=lax.Precision.HIGHEST,
        preferred_element_type=F32,
    )
    lane = lax.broadcasted_iota(jnp.int32, (HALF, 128), 1)
    row = lax.broadcasted_iota(jnp.int32, (HALF, 128), 0)
    first, second = full[0:HALF], full[HALF:MEMBERS]
    packed = jnp.where(lane >= row, first, pltpu.roll(second, 96, 1))
    folded = jnp.where(lane[0:16] < MEMBERS, packed[0:16], pltpu.roll(packed[16:32], 64, 1))
    diagonal = jnp.sum(jnp.where(lane == row + 96, pltpu.roll(second, 64, 1), 0.0), axis=0, keepdims=True)
    last = jnp.where(lane[0:1] < 96, full[MEMBERS : MEMBERS + 1], diagonal)
    stat[0 : STAT - 1, :] = folded
    stat[STAT - 1 : STAT, :] = last


def eliminate(aug):
    size = 8
    row = lax.broadcasted_iota(jnp.int32, (size, 128), 0)
    for start in range(0, MEMBERS, size):
        columns = [jnp.broadcast_to(aug[:, k : k + 1], (MEMBERS, 128)) for k in range(start, start + size)]
        block = [column[start : start + size] for column in columns]
        pivot_rows = aug[start : start + size]
        for i in range(size):
            here = row == i
            inverse = 1.0 / block[i][i : i + 1]

            def clear(a):
                scaled = a[i : i + 1] * inverse
                return jnp.where(here, scaled, a - block[i] * scaled)

            block = block[: i + 1] + [clear(a) for a in block[i + 1 :]]
            pivot_rows = clear(pivot_rows)
        pieces = []
        for at in range(0, MEMBERS, size):
            if at == start:
                pieces.append(pivot_rows)
                continue
            terms = [column[at : at + size] * pivot_rows[i : i + 1] for i, column in enumerate(columns)]
            while len(terms) > 1:
                terms = [a + b for a, b in zip(terms[0::2], terms[1::2])]
            pieces.append(aug[at : at + size] - terms[0])
        aug = jnp.concatenate(pieces, axis=0)
    return aug


def split(a):
    hi = a.astype(jnp.bfloat16)
    return hi, (a - hi.astype(F32)).astype(jnp.bfloat16)


def solve_kernel(parts, tiles, weights_out, prior_hbm, total, sem):
    copy = pltpu.make_async_copy(tiles, prior_hbm, sem)
    copy.start()
    for i in range(STAT):
        row = parts[0, i]
        for d in range(1, parts.shape[0]):
            row = row + parts[d, i]
        total[i : i + 1, :] = row
    folded, last = total[0:16, :], total[16:17, :]
    packed = jnp.concatenate([folded, pltpu.roll(folded, 64, 1)], axis=0)
    tall = jnp.concatenate([packed, jnp.zeros((32, 128), F32), jnp.broadcast_to(last, (64, 128))], axis=0)
    turned = jnp.transpose(tall)
    lane = lax.broadcasted_iota(jnp.int32, (HALF, 128), 1)
    row = lax.broadcasted_iota(jnp.int32, (HALF, 128), 0)
    first = jnp.where(lane >= row, packed, turned[0:HALF])
    corner = jnp.where(lane < row + HALF, pltpu.roll(packed, 32, 1), pltpu.roll(turned[0:HALF], 32, 1))
    corner = jnp.where(lane == row + HALF, pltpu.roll(last, 64, 1), corner)
    second = jnp.where(lane < HALF, turned[HALF:MEMBERS], corner)
    gram = jnp.concatenate([first, second], axis=0)

    shape = (MEMBERS, 128)
    row = lax.broadcasted_iota(jnp.int32, shape, 0)
    lane = lax.broadcasted_iota(jnp.int32, shape, 1)
    eye = row == lane
    low = lane < MEMBERS
    square = jnp.where(lane[0:1] == MEMBERS, last, 0.0) * float(MEMBERS)
    trace = jnp.sum(jnp.where(eye, gram, 0.0), axis=0, keepdims=True)
    misfit = jnp.sum(square + trace, axis=1, keepdims=True)
    inflation = 1.0 + misfit / float(MEMBERS * (MEMBERS - 1))
    shift = (MEMBERS - 1) * inflation
    right = turned[0:MEMBERS] - pltpu.roll(gram, 64, 1)
    aug = eliminate(jnp.where(low, gram + jnp.where(eye, shift, 0.0), right))
    gain = aug - jnp.sum(aug, axis=0, keepdims=True) * (1.0 / MEMBERS)
    weights = jnp.concatenate(
        [jnp.where(low, pltpu.roll(gain, 64, 1), 0.0), jnp.where(low, 0.0, gain)], axis=0
    )

    w_hi, w_lo = split(weights)
    weights_out[0:128, 0:128] = w_hi
    weights_out[0:128, 128:256] = w_lo
    weights_out[128:256, 0:128] = w_hi
    weights_out[128:256, 128:256] = jnp.zeros((128, 128), jnp.bfloat16)
    copy.wait()


def update_kernel(lat, weights, out_hbm, out, sems):
    both = weights[...]
    copies = []
    for t in range(CX // 8):
        at = slice(t * 256, (t + 1) * 256)
        x = lat[at, :]
        product = jnp.dot(jnp.concatenate(split(x), axis=1), both, preferred_element_type=F32)
        out[at, :] = x + (product[:, 0:128] + product[:, 128:256])
        copies.append(pltpu.make_async_copy(out.at[at, :], out_hbm.at[at, :], sems.at[t]))
        copies[-1].start()
    for copy in copies:
        copy.wait()


def pairs(axis, first):
    count_x, count_y = lax.axis_size("gx"), lax.axis_size("gy")
    count = count_x if axis == "gx" else count_y
    moves = []
    for x in range(count_x):
        for y in range(count_y):
            at = x if axis == "gx" else y
            to = at + 1 if (at - first) % 2 == 0 else at - 1
            if not 0 <= to < count:
                target = (x, y ^ 1) if axis == "gx" else (x ^ 1, y)
            else:
                target = (to, y) if axis == "gx" else (x, to)
            moves.append((x * count_y + y, target[0] * count_y + target[1]))
    return moves


def exchange(block, axis, first):
    return lax.ppermute(block, ("gx", "gy"), pairs(axis, first))


def arr(*shape):
    return jax.ShapeDtypeStruct(shape, F32)


def buf(*shape):
    return pltpu.VMEM(shape, F32)


def params(mib):
    return pltpu.CompilerParams(vmem_limit_bytes=mib << 20)


def cost(flops, moved):
    return pl.CostEstimate(flops=flops, bytes_accessed=moved, transcendentals=0)


def to_tiles(a):
    return a.reshape(CX // 8, 8, BLOCKS, 128).transpose(0, 2, 1, 3).reshape(CX * BLOCKS, 128)


def from_tiles(a):
    return a.reshape(CX // 8, BLOCKS, 8, 128).transpose(0, 2, 1, 3).reshape(CX, WIDTH)


def per_device(latent, kappa, obs_cell, obs_value, obs_var):
    gx, gy = lax.axis_index("gx"), lax.axis_index("gy")
    last_x, last_y = lax.axis_size("gx") - 1, lax.axis_size("gy") - 1
    states = [gx > 0, gx < last_x, gy > 0, gy < last_y, gy % 2 == 1, gx % 2 == 1]
    flags = jnp.broadcast_to(jnp.stack(states + states[:2]).astype(F32)[:, None], (8, 128))
    odd = (obs_cell & 1).astype(F32)
    obs_x, obs_y = obs_cell >> 6, obs_cell & (CY - 1)
    obs_row = (obs_x & 56) * BLOCKS + (obs_y >> 1) * 8 + (obs_x & 7)
    val = jnp.concatenate([obs_value.reshape(2, 128), odd.reshape(2, 128)], axis=0)
    var = obs_var.reshape(2, 128)
    vmem, anywhere = pl.BlockSpec(memory_space=VMEM), pl.BlockSpec(memory_space=pl.ANY)
    hbm = pl.BlockSpec(memory_space=pltpu.MemorySpace.HBM)

    def part(shape, *at):
        return pl.BlockSpec(shape, lambda i: at)

    to_odd, to_even, kappa = pl.pallas_call(
        rows_kernel,
        out_shape=(arr(HALO, WIDTH + 128),) * 2 + (arr(CX, CY),),
        in_specs=[hbm, hbm],
        out_specs=(vmem,) * 3,
        scratch_shapes=[pltpu.SemaphoreType.DMA((3,))],
        compiler_params=params(4),
        name="rows",
    )(*(pltpu.with_memory_space_constraint(a, pltpu.MemorySpace.HBM) for a in (latent, kappa)))
    x_odd = exchange(to_odd, "gx", 1)
    x_even = exchange(to_even, "gx", 0)

    whole = part((HALO, WIDTH + 128), 0, 0)
    to_odd, to_even = pl.pallas_call(
        cols_kernel,
        grid=(1,),
        out_shape=(arr(CX + 8, EDGE),) * 2,
        in_specs=[part((8, 128), 0, 0), part((CX, EDGE), 0, 0), part((CX, EDGE), 0, WIDTH // EDGE - 1), part((CX, CY), 0, 0), whole, whole],
        out_specs=(part((CX + 8, EDGE), 0, 0),) * 2,
        scratch_shapes=[buf(128, 128)],
        compiler_params=params(4),
        name="cols",
    )(flags, latent, latent, kappa, x_odd, x_even)
    y_odd = exchange(to_odd, "gy", 1)
    y_even = exchange(to_even, "gy", 0)

    field = arr(BLOCKS * TALL + 2 * PAD, 128)
    tiles, *rest = pl.pallas_call(
        inner_kernel,
        out_shape=(arr(CX * BLOCKS, 128),) + (arr(OBS, 128),) * 3 + (field,) * 5,
        in_specs=[vmem] * 7,
        out_specs=(vmem,) * 9,
        scratch_shapes=[buf(128, 128)],
        compiler_params=params(12),
        cost_estimate=cost(20_000_000, 12_000_000),
        name="inner",
    )(flags, latent, kappa, x_odd, x_even, val, var)

    tiles, stat = pl.pallas_call(
        rim_kernel,
        out_shape=(arr(CX * BLOCKS, 128), arr(STAT, 128)),
        in_specs=[vmem, anywhere] + [vmem] * 11,
        out_specs=(vmem, vmem),
        scratch_shapes=[pltpu.SMEM((OBS,), jnp.int32), pltpu.SemaphoreType.DMA]
        + [buf(128, 128), buf(OBS, 128)]
        + [stencil_buf(4)] * 10,
        input_output_aliases={12: 0},
        compiler_params=params(12),
        name="rim",
    )(flags, obs_row, y_odd, y_even, *rest, tiles)

    stat = stat[:, None, :]
    stat = stat + exchange(stat, "gx", 0)
    width = lax.axis_size("gy")
    parts = lax.all_to_all(jnp.broadcast_to(stat[None], (width,) + stat.shape), "gy", 0, 0)
    stat = jnp.sum(parts, axis=0)
    count = lax.axis_size("gx")
    groups = [list(range(i, count, 2)) for i in range(2)]
    parts = jnp.broadcast_to(stat[None], (count // 2,) + stat.shape)
    parts = lax.all_to_all(parts, "gx", 0, 0, axis_index_groups=groups)

    weights, prior = pl.pallas_call(
        solve_kernel,
        out_shape=(jax.ShapeDtypeStruct((256, 256), jnp.bfloat16), arr(CX * BLOCKS, 128)),
        in_specs=[vmem] * 2,
        out_specs=(vmem, anywhere),
        scratch_shapes=[buf(24, 128), pltpu.SemaphoreType.DMA],
        compiler_params=params(12),
        name="solve",
    )(parts, tiles)
    latent_new = pl.pallas_call(
        update_kernel,
        out_shape=arr(CX * BLOCKS, 128),
        in_specs=[vmem] * 2,
        out_specs=anywhere,
        scratch_shapes=[buf(CX * BLOCKS, 128), pltpu.SemaphoreType.DMA((CX // 8,))],
        compiler_params=params(12),
        name="update",
    )(to_tiles(latent), weights)
    return (from_tiles(latent_new), from_tiles(prior))


def solution(mesh):
    placed = (P("gx", "gy"), P("gx", "gy"), P(("gx", "gy")), P(("gx", "gy")), P(("gx", "gy")))
    return jax.shard_map(
        per_device,
        mesh=mesh,
        in_specs=placed,
        out_specs=(P("gx", "gy"), P("gx", "gy")),
        check_vma=False,
    )
```

```python
import jax
import jax.numpy as jnp
import numpy as np
from jax import lax
from jax.experimental import pallas as pl
from jax.experimental.pallas import tpu as pltpu
from jax.sharding import PartitionSpec as P

MEMBERS = 64
SWEEPS = 4
LOWER_EDGE = 0.25
UPPER_EDGE = 12.0
HALO = SWEEPS
CX = 64
CY = 64
OBS = 256
TALL = CX + 16
WIDTH = CY * MEMBERS
BLOCKS = WIDTH // 128
EDGE = HALO * MEMBERS
STAT = 17
HALF = MEMBERS // 2
VMEM = pltpu.MemorySpace.VMEM
SMEM = pltpu.MemorySpace.SMEM
F32 = jnp.float32


def power_coeffs():
    angles = np.pi * (np.arange(64) + 0.5) / 64.0
    centre, half = 0.5 * (UPPER_EDGE + LOWER_EDGE), 0.5 * (UPPER_EDGE - LOWER_EDGE)
    nodes = centre + half * np.cos(angles)
    cheb = [2.0 / 64.0 * np.sum(np.cos(k * angles) / nodes) for k in range(SWEEPS + 1)]
    cheb[0] *= 0.5
    mono = np.polynomial.chebyshev.cheb2poly(cheb)
    return [float(v / half**k) for k, v in enumerate(mono)]


COEFFS = power_coeffs()
CENTRE = 0.5 * (UPPER_EDGE + LOWER_EDGE) - 4.0


PAD = 8


def lanes(c):
    return slice(c * 128, (c + 1) * 128)


def stencil_buf(blocks):
    return pltpu.VMEM((blocks * TALL + 2 * PAD, 128), F32)


def rows_of(c, first=0, count=TALL):
    at = PAD + c * TALL + first
    return slice(at, at + count)


def sweep(get, xi, alpha, order, coeff, scale, store, at=0, count=TALL):
    low_half = lax.broadcasted_iota(jnp.int32, (count, 128), 1) < MEMBERS
    turned = {}

    def turn(c):
        if c not in turned:
            turned[c] = pltpu.roll(get(c, at), 64, 1)
        return turned[c]

    for c, lower, upper in order:
        beside = turn(c) + jnp.where(low_half, turn(lower), turn(upper))
        beside = beside + (get(c, at - 1) + get(c, at + 1))
        applied = alpha(c) * get(c, at) - beside
        if scale != 1.0:
            applied = applied * scale
        store(c, coeff * xi(c) + applied)


def spread_kappa(alpha, shifted, count, start):
    upper = (lax.broadcasted_iota(jnp.int32, (TALL, 128), 1) >= MEMBERS).astype(jnp.int32)
    for c in range(count):
        alpha[rows_of(c), :] = jnp.take_along_axis(shifted, upper + (2 * c + start), axis=1)


def rows_kernel(lat_hbm, kap_hbm, to_odd, to_even, kap, sems):
    is_odd = lax.rem(lax.axis_index("gx"), 2) == 1
    fetch = pltpu.make_async_copy(kap_hbm, kap, sems.at[0])
    fetch.start()

    def copies(low, high):
        return (
            pltpu.make_async_copy(lat_hbm.at[0:HALO, :], low.at[:, 0:WIDTH], sems.at[1]),
            pltpu.make_async_copy(lat_hbm.at[CX - HALO : CX, :], high.at[:, 0:WIDTH], sems.at[2]),
        )

    @pl.when(is_odd)
    def _():
        for copy in copies(to_even, to_odd):
            copy.start()

    @pl.when(jnp.logical_not(is_odd))
    def _():
        for copy in copies(to_odd, to_even):
            copy.start()

    fetch.wait()
    blank = jnp.zeros((HALO, 128 - CY), F32)
    low = jnp.concatenate([kap[0:HALO, :], blank], axis=1)
    high = jnp.concatenate([kap[CX - HALO : CX, :], blank], axis=1)
    to_odd[:, WIDTH:] = jnp.where(is_odd, high, low)
    to_even[:, WIDTH:] = jnp.where(is_odd, low, high)
    for copy in copies(to_odd, to_even):
        copy.wait()


class Received:
    def __init__(self, flags, x_odd, x_even, below):
        self.is_odd = jnp.broadcast_to(flags[5:6, :], (HALO, 128)) > 0.5
        self.odd_has, self.even_has = (x_even, x_odd) if below else (x_odd, x_even)

    def __getitem__(self, c):
        return jnp.where(self.is_odd, self.odd_has[:, lanes(c)], self.even_has[:, lanes(c)])


def kappa_rows(dst, kap, xlo, xhi):
    dst[...] = jnp.zeros(dst.shape, F32)
    dst[8 : 8 + CX, 0:CY] = kap[...]
    dst[4:8, :] = xlo[BLOCKS]
    dst[8 + CX : 12 + CX, :] = xhi[BLOCKS]


def cols_kernel(flags, first, last, kap, x_odd, x_even, to_odd, to_even, kext):
    xlo, xhi = Received(flags, x_odd, x_even, True), Received(flags, x_odd, x_even, False)
    kappa_rows(kext, kap, xlo, xhi)
    turned = jnp.transpose(kext[...])
    is_odd = jnp.broadcast_to(flags[4:5, :], (8, 128)) > 0.5
    far = BLOCKS - 2
    for dst, swap in ((to_odd, False), (to_even, True)):

        def pick(low, high):
            low, high = (high, low) if swap else (low, high)
            return jnp.where(is_odd[0 : low.shape[0]], high, low)

        for i in range(2):
            for r in range(0, CX, 8):
                dst[r : r + 8, lanes(i)] = pick(first[r : r + 8, lanes(i)], last[r : r + 8, lanes(i)])
            dst[CX : CX + 4, lanes(i)] = pick(xlo[i], xlo[far + i])
            dst[CX + 4 : CX + 8, lanes(i)] = pick(xhi[i], xhi[far + i])
        columns = pick(turned[0:HALO, :], turned[CY - HALO : CY, :])
        for i in range(HALO):
            r = CX if i < 2 else CX + 7
            dst[r : r + 1, lanes(i % 2)] = columns[i : i + 1]


def keep_rows(dst, flags):
    def store(c, new):
        dst[rows_of(c, 0, 8), :] = new[0:8] * flags[0:1, :]
        dst[rows_of(c, 8, CX), :] = new[8 : 8 + CX]
        dst[rows_of(c, 8 + CX, 8), :] = new[8 + CX : TALL] * flags[1:2, :]

    return store


def into_tiles(tiles, c, new):
    for t in range(CX // 8):
        at = (t * BLOCKS + c) * 8
        tiles[at : at + 8, :] = new[8 * t : 8 * t + 8]


def fill(ext, c, body, xlo, xhi, low, high):
    zero4 = jnp.zeros((4, 128), F32)
    ext[rows_of(c, 0, 4), :] = zero4
    ext[rows_of(c, 4, 4), :] = xlo * low
    ext[rows_of(c, 8, CX), :] = body
    ext[rows_of(c, 8 + CX, 4), :] = xhi * high
    ext[rows_of(c, 12 + CX, 4), :] = zero4


def inner_kernel(flags, lat, kap, x_odd, x_even, val, var, tiles, value, weight, odd, parts, ext, alpha, u3, u2, u1, kext):
    xlo, xhi = Received(flags, x_odd, x_even, True), Received(flags, x_odd, x_even, False)
    for c in range(BLOCKS):
        fill(ext, c, lat[:, lanes(c)], xlo[c], xhi[c], flags[0:1, :], flags[1:2, :])
    kappa_rows(kext, kap, xlo, xhi)
    spread_kappa(alpha, kext[0:TALL, :] - CENTRE, BLOCKS, 0)

    def run(src, depth, step, scale, store, at=0, count=TALL):
        order = [(c, max(c - 1, 0), min(c + 1, BLOCKS - 1)) for c in range(depth, BLOCKS - depth)]
        get = lambda c, shift: src[rows_of(c, shift, count), :]
        xi = lambda c: ext[rows_of(c, at, count), :]
        diag = lambda c: alpha[rows_of(c, at, count), :]
        sweep(get, xi, diag, order, COEFFS[step], scale, store, at, count)

    run(ext, 0, 3, COEFFS[4], keep_rows(u3, flags))
    run(u3, 1, 2, 1.0, keep_rows(u2, flags))
    run(u2, 1, 1, 1.0, keep_rows(u1, flags))
    run(u1, 2, 0, 1.0, lambda c, new: into_tiles(tiles, c, new), 8, CX)

    def column(row):
        pieces = [jnp.transpose(jnp.broadcast_to(row[i : i + 1, :], (128, 128))) for i in range(OBS // 128)]
        return jnp.concatenate(pieces, axis=0)

    for t in range(CX // 8):
        for c in range(0, BLOCKS, 2):
            rows = slice(8 * t, 8 * t + 8)
            pair = jnp.concatenate([lat[rows, lanes(c)], lat[rows, lanes(c + 1)]], axis=0)
            at = (t * BLOCKS + c) * 8
            parts[at : at + 16, 0:128], parts[at : at + 16, 128:256] = split(pair)
    value[...] = column(val[0:2, :])
    odd[...] = column(val[2:4, :])
    weight[...] = 1.0 / column(var[0:2, :])


def rim_kernel(
    flags, cell_vmem, y_odd, y_even, value, weight, odd, ext, alpha, u3, u2, u1, held,
    tiles, stat, cell, sem, ext_out, alpha_out, v3, v2, v1, kext, pbuf,
):
    fetch = pltpu.make_async_copy(cell_vmem, cell, sem)
    fetch.start()
    low, high = flags[0:1, :], flags[1:2, :]
    kext[...] = jnp.zeros((128, 128), F32)
    is_odd = jnp.broadcast_to(flags[4:5, :], (CX + 8, 128)) > 0.5
    is_odd = jnp.concatenate([is_odd, is_odd], axis=1)
    for side in range(2):
        lower, upper = (y_even, y_odd) if side == 0 else (y_odd, y_even)
        msg = jnp.where(is_odd, lower[...], upper[...])
        flag = flags[2 + side : 3 + side, :]
        for i in range(HALO):
            r = CX if i < 2 else CX + 7
            kext[i : i + 1, :] = msg[r : r + 1, lanes(i % 2)]
        shifted = jnp.transpose(kext[...])[0:TALL, :] - CENTRE
        upper = (lax.broadcasted_iota(jnp.int32, (TALL, 128), 1) >= MEMBERS).astype(jnp.int32)
        for p in (-2, -1):
            i = p + 2 if side == 0 else -1 - p
            halo = msg[CX : CX + 4, lanes(i)], msg[CX + 4 : CX + 8, lanes(i)]
            fill(ext_out, p + 2, msg[0:CX, lanes(i)] * flag, *halo, low * flag, high * flag)
            alpha_out[rows_of(p + 2), :] = jnp.take_along_axis(shifted, upper + 2 * i, axis=1)

        def local(p):
            return p if side == 0 else BLOCKS - 1 - p

        def run(near, far, mine, first, last, step, scale, store, at=0, count=TALL):
            def pick(p, here, there, ours, start):
                return here[rows_of(p + 2, start, count), :] if p in ours else there[rows_of(local(p), start, count), :]

            get = lambda p, shift: pick(p, near, far, mine, shift)
            xi = lambda p: pick(p, ext_out, ext, (-2, -1), at)
            diag = lambda p: pick(p, alpha_out, alpha, (-2, -1), at)
            order = [(p, max(p - 1, -2), p + 1) for p in range(first, last + 1)]
            if side == 1:
                order = [(p, b, a) for p, a, b in order]
            sweep(get, xi, diag, order, COEFFS[step], scale, store, at, count)

        def keep(dst):
            plain = keep_rows(dst, flags)
            return lambda p, new: plain(p + 2, new * flag if p < 0 else new)

        run(ext_out, ext, (-2, -1), -2, 0, 3, COEFFS[4], keep(v3))
        run(v3, u3, (-2, -1, 0), -1, 0, 2, 1.0, keep(v2))
        run(v2, u2, (-2, -1, 0), -1, 1, 1, 1.0, keep(v1))
        run(v1, u1, (-2, -1, 0, 1), 0, 1, 0, 1.0, lambda p, new: into_tiles(tiles, local(p), new), 8, CX)

    fetch.wait()
    for j in range(OBS):
        pbuf[j : j + 1, :] = tiles[pl.ds(cell[j], 1), :]
    both = pbuf[...]
    lane = lax.broadcasted_iota(jnp.int32, (OBS, 128), 1)
    member = lane < MEMBERS
    predicted = jnp.where(odd[...] > 0.5, pltpu.roll(both, 64, 1), both)
    predicted = jnp.where(member, predicted, 0.0)
    mean = jnp.sum(predicted, axis=1, keepdims=True) * (1.0 / MEMBERS)
    spread = jnp.where(member, predicted - mean, jnp.where(lane == MEMBERS, value[...] - mean, 0.0))
    full = lax.dot_general(
        spread * weight[...],
        spread,
        (((0,), (0,)), ((), ())),
        precision=lax.Precision.HIGHEST,
        preferred_element_type=F32,
    )
    lane = lax.broadcasted_iota(jnp.int32, (HALF, 128), 1)
    row = lax.broadcasted_iota(jnp.int32, (HALF, 128), 0)
    first, second = full[0:HALF], full[HALF:MEMBERS]
    packed = jnp.where(lane >= row, first, pltpu.roll(second, 96, 1))
    folded = jnp.where(lane[0:16] < MEMBERS, packed[0:16], pltpu.roll(packed[16:32], 64, 1))
    diagonal = jnp.sum(jnp.where(lane == row + 96, pltpu.roll(second, 64, 1), 0.0), axis=0, keepdims=True)
    last = jnp.where(lane[0:1] < 96, full[MEMBERS : MEMBERS + 1], diagonal)
    stat[0 : STAT - 1, :] = folded
    stat[STAT - 1 : STAT, :] = last


def eliminate(aug):
    size = 8
    row = lax.broadcasted_iota(jnp.int32, (size, 128), 0)
    for start in range(0, MEMBERS, size):
        columns = [jnp.broadcast_to(aug[:, k : k + 1], (MEMBERS, 128)) for k in range(start, start + size)]
        block = [column[start : start + size] for column in columns]
        pivot_rows = aug[start : start + size]
        for i in range(size):
            here = row == i
            inverse = 1.0 / block[i][i : i + 1]

            def clear(a):
                scaled = a[i : i + 1] * inverse
                return jnp.where(here, scaled, a - block[i] * scaled)

            block = block[: i + 1] + [clear(a) for a in block[i + 1 :]]
            pivot_rows = clear(pivot_rows)
        pieces = []
        for at in range(0, MEMBERS, size):
            if at == start:
                pieces.append(pivot_rows)
                continue
            terms = [column[at : at + size] * pivot_rows[i : i + 1] for i, column in enumerate(columns)]
            while len(terms) > 1:
                terms = [a + b for a, b in zip(terms[0::2], terms[1::2])]
            pieces.append(aug[at : at + size] - terms[0])
        aug = jnp.concatenate(pieces, axis=0)
    return aug


def split(a):
    hi = a.astype(jnp.bfloat16)
    return hi, (a - hi.astype(F32)).astype(jnp.bfloat16)


def solve_kernel(parts, tiles, weights_out, prior_hbm, total, sem):
    copy = pltpu.make_async_copy(tiles, prior_hbm, sem)
    copy.start()
    for i in range(STAT):
        row = parts[0, i]
        for d in range(1, parts.shape[0]):
            row = row + parts[d, i]
        total[i : i + 1, :] = row
    folded, last = total[0:16, :], total[16:17, :]
    packed = jnp.concatenate([folded, pltpu.roll(folded, 64, 1)], axis=0)
    tall = jnp.concatenate([packed, jnp.zeros((32, 128), F32), jnp.broadcast_to(last, (64, 128))], axis=0)
    turned = jnp.transpose(tall)
    lane = lax.broadcasted_iota(jnp.int32, (HALF, 128), 1)
    row = lax.broadcasted_iota(jnp.int32, (HALF, 128), 0)
    first = jnp.where(lane >= row, packed, turned[0:HALF])
    corner = jnp.where(lane < row + HALF, pltpu.roll(packed, 32, 1), pltpu.roll(turned[0:HALF], 32, 1))
    corner = jnp.where(lane == row + HALF, pltpu.roll(last, 64, 1), corner)
    second = jnp.where(lane < HALF, turned[HALF:MEMBERS], corner)
    gram = jnp.concatenate([first, second], axis=0)

    shape = (MEMBERS, 128)
    row = lax.broadcasted_iota(jnp.int32, shape, 0)
    lane = lax.broadcasted_iota(jnp.int32, shape, 1)
    eye = row == lane
    low = lane < MEMBERS
    square = jnp.where(lane[0:1] == MEMBERS, last, 0.0) * float(MEMBERS)
    trace = jnp.sum(jnp.where(eye, gram, 0.0), axis=0, keepdims=True)
    misfit = jnp.sum(square + trace, axis=1, keepdims=True)
    inflation = 1.0 + misfit / float(MEMBERS * (MEMBERS - 1))
    shift = (MEMBERS - 1) * inflation
    right = turned[0:MEMBERS] - pltpu.roll(gram, 64, 1)
    aug = eliminate(jnp.where(low, gram + jnp.where(eye, shift, 0.0), right))
    gain = aug - jnp.sum(aug, axis=0, keepdims=True) * (1.0 / MEMBERS)
    weights = jnp.concatenate(
        [jnp.where(low, pltpu.roll(gain, 64, 1), 0.0), jnp.where(low, 0.0, gain)], axis=0
    )

    w_hi, w_lo = split(weights)
    weights_out[0:128, 0:128] = w_hi
    weights_out[0:128, 128:256] = w_lo
    weights_out[128:256, 0:128] = w_hi
    weights_out[128:256, 128:256] = jnp.zeros((128, 128), jnp.bfloat16)
    copy.wait()


def update_kernel(lat, parts, weights, out_hbm, out, sems):
    both = weights[...]
    copies = []
    for t in range(CX // 8):
        at = slice(t * 256, (t + 1) * 256)
        product = jnp.dot(parts[at, :], both, preferred_element_type=F32)
        out[at, :] = lat[at, :] + (product[:, 0:128] + product[:, 128:256])
        copies.append(pltpu.make_async_copy(out.at[at, :], out_hbm.at[at, :], sems.at[t]))
        copies[-1].start()
    for copy in copies:
        copy.wait()


def pairs(axis, first):
    count_x, count_y = lax.axis_size("gx"), lax.axis_size("gy")
    count = count_x if axis == "gx" else count_y
    moves = []
    for x in range(count_x):
        for y in range(count_y):
            at = x if axis == "gx" else y
            to = at + 1 if (at - first) % 2 == 0 else at - 1
            if not 0 <= to < count:
                target = (x, y ^ 1) if axis == "gx" else (x ^ 1, y)
            else:
                target = (to, y) if axis == "gx" else (x, to)
            moves.append((x * count_y + y, target[0] * count_y + target[1]))
    return moves


def exchange(block, axis, first):
    return lax.ppermute(block, ("gx", "gy"), pairs(axis, first))


def arr(*shape):
    return jax.ShapeDtypeStruct(shape, F32)


def buf(*shape):
    return pltpu.VMEM(shape, F32)


def params(mib):
    return pltpu.CompilerParams(vmem_limit_bytes=mib << 20)


def cost(flops, moved):
    return pl.CostEstimate(flops=flops, bytes_accessed=moved, transcendentals=0)


def to_tiles(a):
    return a.reshape(CX // 8, 8, BLOCKS, 128).transpose(0, 2, 1, 3).reshape(CX * BLOCKS, 128)


def from_tiles(a):
    return a.reshape(CX // 8, BLOCKS, 8, 128).transpose(0, 2, 1, 3).reshape(CX, WIDTH)


def per_device(latent, kappa, obs_cell, obs_value, obs_var):
    gx, gy = lax.axis_index("gx"), lax.axis_index("gy")
    last_x, last_y = lax.axis_size("gx") - 1, lax.axis_size("gy") - 1
    states = [gx > 0, gx < last_x, gy > 0, gy < last_y, gy % 2 == 1, gx % 2 == 1]
    flags = jnp.broadcast_to(jnp.stack(states + states[:2]).astype(F32)[:, None], (8, 128))
    odd = (obs_cell & 1).astype(F32)
    obs_x, obs_y = obs_cell >> 6, obs_cell & (CY - 1)
    obs_row = (obs_x & 56) * BLOCKS + (obs_y >> 1) * 8 + (obs_x & 7)
    val = jnp.concatenate([obs_value.reshape(2, 128), odd.reshape(2, 128)], axis=0)
    var = obs_var.reshape(2, 128)
    vmem, anywhere = pl.BlockSpec(memory_space=VMEM), pl.BlockSpec(memory_space=pl.ANY)
    hbm = pl.BlockSpec(memory_space=pltpu.MemorySpace.HBM)

    def part(shape, *at):
        return pl.BlockSpec(shape, lambda i: at)

    to_odd, to_even, kappa = pl.pallas_call(
        rows_kernel,
        out_shape=(arr(HALO, WIDTH + 128),) * 2 + (arr(CX, CY),),
        in_specs=[hbm, hbm],
        out_specs=(vmem,) * 3,
        scratch_shapes=[pltpu.SemaphoreType.DMA((3,))],
        compiler_params=params(4),
        name="rows",
    )(*(pltpu.with_memory_space_constraint(a, pltpu.MemorySpace.HBM) for a in (latent, kappa)))
    x_odd = exchange(to_odd, "gx", 1)
    x_even = exchange(to_even, "gx", 0)

    whole = part((HALO, WIDTH + 128), 0, 0)
    to_odd, to_even = pl.pallas_call(
        cols_kernel,
        grid=(1,),
        out_shape=(arr(CX + 8, EDGE),) * 2,
        in_specs=[part((8, 128), 0, 0), part((CX, EDGE), 0, 0), part((CX, EDGE), 0, WIDTH // EDGE - 1), part((CX, CY), 0, 0), whole, whole],
        out_specs=(part((CX + 8, EDGE), 0, 0),) * 2,
        scratch_shapes=[buf(128, 128)],
        compiler_params=params(4),
        name="cols",
    )(flags, latent, latent, kappa, x_odd, x_even)
    y_odd = exchange(to_odd, "gy", 1)
    y_even = exchange(to_even, "gy", 0)

    field = arr(BLOCKS * TALL + 2 * PAD, 128)
    tiles, value, weight, odd, split_latent, *rest = pl.pallas_call(
        inner_kernel,
        out_shape=(arr(CX * BLOCKS, 128),) + (arr(OBS, 128),) * 3
        + (jax.ShapeDtypeStruct((CX * BLOCKS, 256), jnp.bfloat16),)
        + (field,) * 5,
        in_specs=[vmem] * 7,
        out_specs=(vmem,) * 10,
        scratch_shapes=[buf(128, 128)],
        compiler_params=params(12),
        cost_estimate=cost(20_000_000, 12_000_000),
        name="inner",
    )(flags, latent, kappa, x_odd, x_even, val, var)

    tiles, stat = pl.pallas_call(
        rim_kernel,
        out_shape=(arr(CX * BLOCKS, 128), arr(STAT, 128)),
        in_specs=[vmem, anywhere] + [vmem] * 11,
        out_specs=(vmem, vmem),
        scratch_shapes=[pltpu.SMEM((OBS,), jnp.int32), pltpu.SemaphoreType.DMA]
        + [stencil_buf(4)] * 5
        + [buf(128, 128), buf(OBS, 128)],
        input_output_aliases={12: 0},
        compiler_params=params(12),
        name="rim",
    )(flags, obs_row, y_odd, y_even, value, weight, odd, *rest, tiles)

    stat = stat[:, None, :]
    stat = stat + exchange(stat, "gx", 0)
    width = lax.axis_size("gy")
    parts = lax.all_to_all(jnp.broadcast_to(stat[None], (width,) + stat.shape), "gy", 0, 0)
    stat = jnp.sum(parts, axis=0)
    count = lax.axis_size("gx")
    groups = [list(range(i, count, 2)) for i in range(2)]
    parts = jnp.broadcast_to(stat[None], (count // 2,) + stat.shape)
    parts = lax.all_to_all(parts, "gx", 0, 0, axis_index_groups=groups)

    weights, prior = pl.pallas_call(
        solve_kernel,
        out_shape=(jax.ShapeDtypeStruct((256, 256), jnp.bfloat16), arr(CX * BLOCKS, 128)),
        in_specs=[vmem] * 2,
        out_specs=(vmem, anywhere),
        scratch_shapes=[buf(24, 128), pltpu.SemaphoreType.DMA],
        compiler_params=params(12),
        name="solve",
    )(parts, tiles)
    latent_new = pl.pallas_call(
        update_kernel,
        out_shape=arr(CX * BLOCKS, 128),
        in_specs=[vmem] * 3,
        out_specs=anywhere,
        scratch_shapes=[buf(CX * BLOCKS, 128), pltpu.SemaphoreType.DMA((CX // 8,))],
        compiler_params=params(12),
        name="update",
    )(to_tiles(latent), split_latent, weights)
    return (from_tiles(latent_new), from_tiles(prior))


def solution(mesh):
    placed = (P("gx", "gy"), P("gx", "gy"), P(("gx", "gy")), P(("gx", "gy")), P(("gx", "gy")))
    return jax.shard_map(
        per_device,
        mesh=mesh,
        in_specs=placed,
        out_specs=(P("gx", "gy"), P("gx", "gy")),
        check_vma=False,
    )
```

```python
import jax
import jax.numpy as jnp
import numpy as np
from jax import lax
from jax.experimental import pallas as pl
from jax.experimental.pallas import tpu as pltpu
from jax.sharding import PartitionSpec as P

MEMBERS = 64
SWEEPS = 4
LOWER_EDGE = 0.25
UPPER_EDGE = 12.0
HALO = SWEEPS
CX = 64
CY = 64
OBS = 256
TALL = CX + 16
WIDTH = CY * MEMBERS
BLOCKS = WIDTH // 128
EDGE = HALO * MEMBERS
STAT = 17
HALF = MEMBERS // 2
VMEM = pltpu.MemorySpace.VMEM
SMEM = pltpu.MemorySpace.SMEM
F32 = jnp.float32


def power_coeffs():
    angles = np.pi * (np.arange(64) + 0.5) / 64.0
    centre, half = 0.5 * (UPPER_EDGE + LOWER_EDGE), 0.5 * (UPPER_EDGE - LOWER_EDGE)
    nodes = centre + half * np.cos(angles)
    cheb = [2.0 / 64.0 * np.sum(np.cos(k * angles) / nodes) for k in range(SWEEPS + 1)]
    cheb[0] *= 0.5
    mono = np.polynomial.chebyshev.cheb2poly(cheb)
    return [float(v / half**k) for k, v in enumerate(mono)]


COEFFS = power_coeffs()
CENTRE = 0.5 * (UPPER_EDGE + LOWER_EDGE) - 4.0


PAD = 8


def lanes(c):
    return slice(c * 128, (c + 1) * 128)


def stencil_buf(blocks):
    return pltpu.VMEM((blocks * TALL + 2 * PAD, 128), F32)


def rows_of(c, first=0, count=TALL):
    at = PAD + c * TALL + first
    return slice(at, at + count)


def sweep(get, xi, alpha, order, coeff, scale, store, at=0, count=TALL):
    low_half = lax.broadcasted_iota(jnp.int32, (count, 128), 1) < MEMBERS
    turned = {}

    def turn(c):
        if c not in turned:
            turned[c] = pltpu.roll(get(c, at), 64, 1)
        return turned[c]

    for c, lower, upper in order:
        beside = turn(c) + jnp.where(low_half, turn(lower), turn(upper))
        beside = beside + (get(c, at - 1) + get(c, at + 1))
        applied = alpha(c) * get(c, at) - beside
        if scale != 1.0:
            applied = applied * scale
        store(c, coeff * xi(c) + applied)


def spread_kappa(alpha, shifted, count, start):
    upper = (lax.broadcasted_iota(jnp.int32, (TALL, 128), 1) >= MEMBERS).astype(jnp.int32)
    for c in range(count):
        alpha[rows_of(c), :] = jnp.take_along_axis(shifted, upper + (2 * c + start), axis=1)


def edges_kernel(lat_hbm, kap_hbm, to_odd, to_even, y_to_odd, y_to_even, kap, sems):
    odds = [lax.rem(lax.axis_index(axis), 2) == 1 for axis in ("gx", "gy")]
    is_odd = odds[0]
    fetch = pltpu.make_async_copy(kap_hbm, kap, sems.at[0])
    fetch.start()

    def copies(low, high):
        return (
            pltpu.make_async_copy(lat_hbm.at[0:HALO, :], low.at[:, 0:WIDTH], sems.at[1]),
            pltpu.make_async_copy(lat_hbm.at[CX - HALO : CX, :], high.at[:, 0:WIDTH], sems.at[2]),
        )

    def columns(low, high):
        return (
            pltpu.make_async_copy(lat_hbm.at[:, 0:EDGE], low, sems.at[3]),
            pltpu.make_async_copy(lat_hbm.at[:, WIDTH - EDGE : WIDTH], high, sems.at[4]),
        )

    ways = ((odds[0], copies, to_odd, to_even), (odds[1], columns, y_to_odd, y_to_even))
    for odd, make, first, second in ways:

        @pl.when(odd)
        def _(make=make, first=first, second=second):
            for copy in make(second, first):
                copy.start()

        @pl.when(jnp.logical_not(odd))
        def _(make=make, first=first, second=second):
            for copy in make(first, second):
                copy.start()

    fetch.wait()
    blank = jnp.zeros((HALO, 128 - CY), F32)
    low = jnp.concatenate([kap[0:HALO, :], blank], axis=1)
    high = jnp.concatenate([kap[CX - HALO : CX, :], blank], axis=1)
    to_odd[:, WIDTH:] = jnp.where(is_odd, high, low)
    to_even[:, WIDTH:] = jnp.where(is_odd, low, high)
    for copy in copies(to_odd, to_even) + columns(y_to_odd, y_to_even):
        copy.wait()


class Received:
    def __init__(self, flags, x_odd, x_even, below):
        self.is_odd = jnp.broadcast_to(flags[5:6, :], (HALO, 128)) > 0.5
        self.odd_has, self.even_has = (x_even, x_odd) if below else (x_odd, x_even)

    def __getitem__(self, c):
        return jnp.where(self.is_odd, self.odd_has[:, lanes(c)], self.even_has[:, lanes(c)])


def kappa_rows(dst, kap, xlo, xhi):
    dst[...] = jnp.zeros(dst.shape, F32)
    dst[8 : 8 + CX, 0:CY] = kap[...]
    dst[4:8, :] = xlo[BLOCKS]
    dst[8 + CX : 12 + CX, :] = xhi[BLOCKS]


def corners_kernel(flags, kap, x_odd, x_even, to_odd, to_even, kext):
    xlo, xhi = Received(flags, x_odd, x_even, True), Received(flags, x_odd, x_even, False)
    kappa_rows(kext, kap, xlo, xhi)
    turned = jnp.transpose(kext[...])
    is_odd = jnp.broadcast_to(flags[4:5, :], (HALO, 128)) > 0.5
    far = BLOCKS - 2
    for dst, swap in ((to_odd, False), (to_even, True)):

        def pick(low, high):
            low, high = (high, low) if swap else (low, high)
            return jnp.where(is_odd, high, low)

        for i in range(2):
            dst[0:4, lanes(i)] = pick(xlo[i], xlo[far + i])
            dst[4:8, lanes(i)] = pick(xhi[i], xhi[far + i])
        columns = pick(turned[0:HALO, :], turned[CY - HALO : CY, :])
        for i in range(HALO):
            r = 0 if i < 2 else 7
            dst[r : r + 1, lanes(i % 2)] = columns[i : i + 1]


def keep_rows(dst, flags):
    def store(c, new):
        dst[rows_of(c, 0, 8), :] = new[0:8] * flags[0:1, :]
        dst[rows_of(c, 8, CX), :] = new[8 : 8 + CX]
        dst[rows_of(c, 8 + CX, 8), :] = new[8 + CX : TALL] * flags[1:2, :]

    return store


def into_tiles(tiles, c, new):
    for t in range(CX // 8):
        at = (t * BLOCKS + c) * 8
        tiles[at : at + 8, :] = new[8 * t : 8 * t + 8]


def fill(ext, c, body, xlo, xhi, low, high):
    zero4 = jnp.zeros((4, 128), F32)
    ext[rows_of(c, 0, 4), :] = zero4
    ext[rows_of(c, 4, 4), :] = xlo * low
    ext[rows_of(c, 8, CX), :] = body
    ext[rows_of(c, 8 + CX, 4), :] = xhi * high
    ext[rows_of(c, 12 + CX, 4), :] = zero4


def inner_kernel(flags, lat, kap, x_odd, x_even, val, var, tiles, value, weight, odd, ext, alpha, u3, u2, u1, kext):
    xlo, xhi = Received(flags, x_odd, x_even, True), Received(flags, x_odd, x_even, False)
    for c in range(BLOCKS):
        fill(ext, c, lat[:, lanes(c)], xlo[c], xhi[c], flags[0:1, :], flags[1:2, :])
    kappa_rows(kext, kap, xlo, xhi)
    spread_kappa(alpha, kext[0:TALL, :] - CENTRE, BLOCKS, 0)

    def run(src, depth, step, scale, store, at=0, count=TALL):
        order = [(c, max(c - 1, 0), min(c + 1, BLOCKS - 1)) for c in range(depth, BLOCKS - depth)]
        get = lambda c, shift: src[rows_of(c, shift, count), :]
        xi = lambda c: ext[rows_of(c, at, count), :]
        diag = lambda c: alpha[rows_of(c, at, count), :]
        sweep(get, xi, diag, order, COEFFS[step], scale, store, at, count)

    run(ext, 0, 3, COEFFS[4], keep_rows(u3, flags))
    run(u3, 1, 2, 1.0, keep_rows(u2, flags))
    run(u2, 1, 1, 1.0, keep_rows(u1, flags))
    run(u1, 2, 0, 1.0, lambda c, new: into_tiles(tiles, c, new), 8, CX)

    def column(row):
        pieces = [jnp.transpose(jnp.broadcast_to(row[i : i + 1, :], (128, 128))) for i in range(OBS // 128)]
        return jnp.concatenate(pieces, axis=0)

    value[...] = column(val[0:2, :])
    odd[...] = column(val[2:4, :])
    weight[...] = 1.0 / column(var[0:2, :])


def rim_kernel(
    flags, cell_vmem, y_odd, y_even, corner_odd, corner_even, value, weight, odd, ext, alpha, u3, u2, u1, held,
    tiles, stat, cell, sem, ext_out, alpha_out, v3, v2, v1, kext, pbuf,
):
    fetch = pltpu.make_async_copy(cell_vmem, cell, sem)
    fetch.start()
    low, high = flags[0:1, :], flags[1:2, :]
    kext[...] = jnp.zeros((128, 128), F32)
    is_odd = jnp.broadcast_to(flags[4:5, :], (CX, 128)) > 0.5
    is_odd = jnp.concatenate([is_odd, is_odd], axis=1)
    for side in range(2):
        lower, upper = (y_even, y_odd) if side == 0 else (y_odd, y_even)
        msg = jnp.where(is_odd, lower[...], upper[...])
        lower, upper = (corner_even, corner_odd) if side == 0 else (corner_odd, corner_even)
        corner = jnp.where(is_odd[0:8], lower[...], upper[...])
        flag = flags[2 + side : 3 + side, :]
        for i in range(HALO):
            r = 0 if i < 2 else 7
            kext[i : i + 1, :] = corner[r : r + 1, lanes(i % 2)]
        shifted = jnp.transpose(kext[...])[0:TALL, :] - CENTRE
        upper = (lax.broadcasted_iota(jnp.int32, (TALL, 128), 1) >= MEMBERS).astype(jnp.int32)
        for p in (-2, -1):
            i = p + 2 if side == 0 else -1 - p
            halo = corner[0:4, lanes(i)], corner[4:8, lanes(i)]
            fill(ext_out, p + 2, msg[:, lanes(i)] * flag, *halo, low * flag, high * flag)
            alpha_out[rows_of(p + 2), :] = jnp.take_along_axis(shifted, upper + 2 * i, axis=1)

        def local(p):
            return p if side == 0 else BLOCKS - 1 - p

        def run(near, far, mine, first, last, step, scale, store, at=0, count=TALL):
            def pick(p, here, there, ours, start):
                return here[rows_of(p + 2, start, count), :] if p in ours else there[rows_of(local(p), start, count), :]

            get = lambda p, shift: pick(p, near, far, mine, shift)
            xi = lambda p: pick(p, ext_out, ext, (-2, -1), at)
            diag = lambda p: pick(p, alpha_out, alpha, (-2, -1), at)
            order = [(p, max(p - 1, -2), p + 1) for p in range(first, last + 1)]
            if side == 1:
                order = [(p, b, a) for p, a, b in order]
            sweep(get, xi, diag, order, COEFFS[step], scale, store, at, count)

        def keep(dst):
            plain = keep_rows(dst, flags)
            return lambda p, new: plain(p + 2, new * flag if p < 0 else new)

        run(ext_out, ext, (-2, -1), -2, 0, 3, COEFFS[4], keep(v3))
        run(v3, u3, (-2, -1, 0), -1, 0, 2, 1.0, keep(v2))
        run(v2, u2, (-2, -1, 0), -1, 1, 1, 1.0, keep(v1))
        run(v1, u1, (-2, -1, 0, 1), 0, 1, 0, 1.0, lambda p, new: into_tiles(tiles, local(p), new), 8, CX)

    fetch.wait()
    for j in range(OBS):
        pbuf[j : j + 1, :] = tiles[pl.ds(cell[j], 1), :]
    both = pbuf[...]
    lane = lax.broadcasted_iota(jnp.int32, (OBS, 128), 1)
    member = lane < MEMBERS
    predicted = jnp.where(odd[...] > 0.5, pltpu.roll(both, 64, 1), both)
    predicted = jnp.where(member, predicted, 0.0)
    mean = jnp.sum(predicted, axis=1, keepdims=True) * (1.0 / MEMBERS)
    spread = jnp.where(member, predicted - mean, jnp.where(lane == MEMBERS, value[...] - mean, 0.0))
    full = lax.dot_general(
        spread * weight[...],
        spread,
        (((0,), (0,)), ((), ())),
        precision=lax.Precision.HIGHEST,
        preferred_element_type=F32,
    )
    lane = lax.broadcasted_iota(jnp.int32, (HALF, 128), 1)
    row = lax.broadcasted_iota(jnp.int32, (HALF, 128), 0)
    first, second = full[0:HALF], full[HALF:MEMBERS]
    packed = jnp.where(lane >= row, first, pltpu.roll(second, 96, 1))
    folded = jnp.where(lane[0:16] < MEMBERS, packed[0:16], pltpu.roll(packed[16:32], 64, 1))
    diagonal = jnp.sum(jnp.where(lane == row + 96, pltpu.roll(second, 64, 1), 0.0), axis=0, keepdims=True)
    last = jnp.where(lane[0:1] < 96, full[MEMBERS : MEMBERS + 1], diagonal)
    stat[0 : STAT - 1, :] = folded
    stat[STAT - 1 : STAT, :] = last


def eliminate(aug):
    size = 8
    row = lax.broadcasted_iota(jnp.int32, (size, 128), 0)
    for start in range(0, MEMBERS, size):
        columns = [jnp.broadcast_to(aug[:, k : k + 1], (MEMBERS, 128)) for k in range(start, start + size)]
        block = [column[start : start + size] for column in columns]
        pivot_rows = aug[start : start + size]
        for i in range(size):
            here = row == i
            inverse = 1.0 / block[i][i : i + 1]

            def clear(a):
                scaled = a[i : i + 1] * inverse
                return jnp.where(here, scaled, a - block[i] * scaled)

            block = block[: i + 1] + [clear(a) for a in block[i + 1 :]]
            pivot_rows = clear(pivot_rows)
        pieces = []
        for at in range(0, MEMBERS, size):
            if at == start:
                pieces.append(pivot_rows)
                continue
            terms = [column[at : at + size] * pivot_rows[i : i + 1] for i, column in enumerate(columns)]
            while len(terms) > 1:
                terms = [a + b for a, b in zip(terms[0::2], terms[1::2])]
            pieces.append(aug[at : at + size] - terms[0])
        aug = jnp.concatenate(pieces, axis=0)
    return aug


def split(a):
    hi = a.astype(jnp.bfloat16)
    return hi, (a - hi.astype(F32)).astype(jnp.bfloat16)


def solve_kernel(parts, tiles, weights_out, prior_hbm, total, sem):
    copy = pltpu.make_async_copy(tiles, prior_hbm, sem)
    copy.start()
    for i in range(STAT):
        row = parts[0, i]
        for d in range(1, parts.shape[0]):
            row = row + parts[d, i]
        total[i : i + 1, :] = row
    folded, last = total[0:16, :], total[16:17, :]
    packed = jnp.concatenate([folded, pltpu.roll(folded, 64, 1)], axis=0)
    tall = jnp.concatenate([packed, jnp.zeros((32, 128), F32), jnp.broadcast_to(last, (64, 128))], axis=0)
    turned = jnp.transpose(tall)
    lane = lax.broadcasted_iota(jnp.int32, (HALF, 128), 1)
    row = lax.broadcasted_iota(jnp.int32, (HALF, 128), 0)
    first = jnp.where(lane >= row, packed, turned[0:HALF])
    corner = jnp.where(lane < row + HALF, pltpu.roll(packed, 32, 1), pltpu.roll(turned[0:HALF], 32, 1))
    corner = jnp.where(lane == row + HALF, pltpu.roll(last, 64, 1), corner)
    second = jnp.where(lane < HALF, turned[HALF:MEMBERS], corner)
    gram = jnp.concatenate([first, second], axis=0)

    shape = (MEMBERS, 128)
    row = lax.broadcasted_iota(jnp.int32, shape, 0)
    lane = lax.broadcasted_iota(jnp.int32, shape, 1)
    eye = row == lane
    low = lane < MEMBERS
    square = jnp.where(lane[0:1] == MEMBERS, last, 0.0) * float(MEMBERS)
    trace = jnp.sum(jnp.where(eye, gram, 0.0), axis=0, keepdims=True)
    misfit = jnp.sum(square + trace, axis=1, keepdims=True)
    inflation = 1.0 + misfit / float(MEMBERS * (MEMBERS - 1))
    shift = (MEMBERS - 1) * inflation
    right = turned[0:MEMBERS] - pltpu.roll(gram, 64, 1)
    aug = eliminate(jnp.where(low, gram + jnp.where(eye, shift, 0.0), right))
    gain = aug - jnp.sum(aug, axis=0, keepdims=True) * (1.0 / MEMBERS)
    weights = jnp.concatenate(
        [jnp.where(low, pltpu.roll(gain, 64, 1), 0.0), jnp.where(low, 0.0, gain)], axis=0
    )

    w_hi, w_lo = split(weights)
    weights_out[0:128, 0:128] = w_hi
    weights_out[0:128, 128:256] = w_lo
    weights_out[128:256, 0:128] = w_hi
    weights_out[128:256, 128:256] = jnp.zeros((128, 128), jnp.bfloat16)
    copy.wait()


def update_kernel(lat, weights, out_hbm, out, sems):
    both = weights[...]
    copies = []
    for t in range(CX // 8):
        at = slice(t * 256, (t + 1) * 256)
        x = lat[at, :]
        product = jnp.dot(jnp.concatenate(split(x), axis=1), both, preferred_element_type=F32)
        out[at, :] = x + (product[:, 0:128] + product[:, 128:256])
        copies.append(pltpu.make_async_copy(out.at[at, :], out_hbm.at[at, :], sems.at[t]))
        copies[-1].start()
    for copy in copies:
        copy.wait()


def pairs(axis, first):
    count_x, count_y = lax.axis_size("gx"), lax.axis_size("gy")
    count = count_x if axis == "gx" else count_y
    moves = []
    for x in range(count_x):
        for y in range(count_y):
            at = x if axis == "gx" else y
            to = at + 1 if (at - first) % 2 == 0 else at - 1
            if not 0 <= to < count:
                target = (x, y ^ 1) if axis == "gx" else (x ^ 1, y)
            else:
                target = (to, y) if axis == "gx" else (x, to)
            moves.append((x * count_y + y, target[0] * count_y + target[1]))
    return moves


def exchange(block, axis, first):
    return lax.ppermute(block, ("gx", "gy"), pairs(axis, first))


def arr(*shape):
    return jax.ShapeDtypeStruct(shape, F32)


def buf(*shape):
    return pltpu.VMEM(shape, F32)


def params(mib):
    return pltpu.CompilerParams(vmem_limit_bytes=mib << 20)


def cost(flops, moved):
    return pl.CostEstimate(flops=flops, bytes_accessed=moved, transcendentals=0)


def to_tiles(a):
    return a.reshape(CX // 8, 8, BLOCKS, 128).transpose(0, 2, 1, 3).reshape(CX * BLOCKS, 128)


def from_tiles(a):
    return a.reshape(CX // 8, BLOCKS, 8, 128).transpose(0, 2, 1, 3).reshape(CX, WIDTH)


def per_device(latent, kappa, obs_cell, obs_value, obs_var):
    gx, gy = lax.axis_index("gx"), lax.axis_index("gy")
    last_x, last_y = lax.axis_size("gx") - 1, lax.axis_size("gy") - 1
    states = [gx > 0, gx < last_x, gy > 0, gy < last_y, gy % 2 == 1, gx % 2 == 1]
    flags = jnp.broadcast_to(jnp.stack(states + states[:2]).astype(F32)[:, None], (8, 128))
    odd = (obs_cell & 1).astype(F32)
    obs_x, obs_y = obs_cell >> 6, obs_cell & (CY - 1)
    obs_row = (obs_x & 56) * BLOCKS + (obs_y >> 1) * 8 + (obs_x & 7)
    val = jnp.concatenate([obs_value.reshape(2, 128), odd.reshape(2, 128)], axis=0)
    var = obs_var.reshape(2, 128)
    vmem, anywhere = pl.BlockSpec(memory_space=VMEM), pl.BlockSpec(memory_space=pl.ANY)
    hbm = pl.BlockSpec(memory_space=pltpu.MemorySpace.HBM)

    to_odd, to_even, y_to_odd, y_to_even, kappa = pl.pallas_call(
        edges_kernel,
        out_shape=(arr(HALO, WIDTH + 128),) * 2 + (arr(CX, EDGE),) * 2 + (arr(CX, CY),),
        in_specs=[hbm, hbm],
        out_specs=(vmem,) * 5,
        scratch_shapes=[pltpu.SemaphoreType.DMA((5,))],
        compiler_params=params(4),
        name="edges",
    )(*(pltpu.with_memory_space_constraint(a, pltpu.MemorySpace.HBM) for a in (latent, kappa)))
    x_odd = exchange(to_odd, "gx", 1)
    x_even = exchange(to_even, "gx", 0)
    y_odd = exchange(y_to_odd, "gy", 1)
    y_even = exchange(y_to_even, "gy", 0)

    to_odd, to_even = pl.pallas_call(
        corners_kernel,
        out_shape=(arr(8, EDGE),) * 2,
        in_specs=[vmem] * 4,
        out_specs=(vmem,) * 2,
        scratch_shapes=[buf(128, 128)],
        compiler_params=params(4),
        name="corners",
    )(flags, kappa, x_odd, x_even)
    corner_odd = exchange(to_odd, "gy", 1)
    corner_even = exchange(to_even, "gy", 0)

    field = arr(BLOCKS * TALL + 2 * PAD, 128)
    tiles, *rest = pl.pallas_call(
        inner_kernel,
        out_shape=(arr(CX * BLOCKS, 128),) + (arr(OBS, 128),) * 3 + (field,) * 5,
        in_specs=[vmem] * 7,
        out_specs=(vmem,) * 9,
        scratch_shapes=[buf(128, 128)],
        compiler_params=params(12),
        cost_estimate=cost(20_000_000, 12_000_000),
        name="inner",
    )(flags, latent, kappa, x_odd, x_even, val, var)

    tiles, stat = pl.pallas_call(
        rim_kernel,
        out_shape=(arr(CX * BLOCKS, 128), arr(STAT, 128)),
        in_specs=[vmem, anywhere] + [vmem] * 13,
        out_specs=(vmem, vmem),
        scratch_shapes=[pltpu.SMEM((OBS,), jnp.int32), pltpu.SemaphoreType.DMA]
        + [stencil_buf(4)] * 5
        + [buf(128, 128), buf(OBS, 128)],
        input_output_aliases={14: 0},
        compiler_params=params(12),
        name="rim",
    )(flags, obs_row, y_odd, y_even, corner_odd, corner_even, *rest, tiles)

    stat = stat[:, None, :]
    stat = stat + exchange(stat, "gx", 0)
    width = lax.axis_size("gy")
    parts = lax.all_to_all(jnp.broadcast_to(stat[None], (width,) + stat.shape), "gy", 0, 0)
    stat = jnp.sum(parts, axis=0)
    count = lax.axis_size("gx")
    groups = [list(range(i, count, 2)) for i in range(2)]
    parts = jnp.broadcast_to(stat[None], (count // 2,) + stat.shape)
    parts = lax.all_to_all(parts, "gx", 0, 0, axis_index_groups=groups)

    weights, prior = pl.pallas_call(
        solve_kernel,
        out_shape=(jax.ShapeDtypeStruct((256, 256), jnp.bfloat16), arr(CX * BLOCKS, 128)),
        in_specs=[vmem] * 2,
        out_specs=(vmem, anywhere),
        scratch_shapes=[buf(24, 128), pltpu.SemaphoreType.DMA],
        compiler_params=params(12),
        name="solve",
    )(parts, tiles)
    latent_new = pl.pallas_call(
        update_kernel,
        out_shape=arr(CX * BLOCKS, 128),
        in_specs=[vmem] * 2,
        out_specs=anywhere,
        scratch_shapes=[buf(CX * BLOCKS, 128), pltpu.SemaphoreType.DMA((CX // 8,))],
        compiler_params=params(12),
        name="update",
    )(to_tiles(latent), weights)
    return (from_tiles(latent_new), from_tiles(prior))


def solution(mesh):
    placed = (P("gx", "gy"), P("gx", "gy"), P(("gx", "gy")), P(("gx", "gy")), P(("gx", "gy")))
    return jax.shard_map(
        per_device,
        mesh=mesh,
        in_specs=placed,
        out_specs=(P("gx", "gy"), P("gx", "gy")),
        check_vma=False,
    )
```

```python
import jax
import jax.numpy as jnp
import numpy as np
from jax import lax
from jax.experimental import pallas as pl
from jax.experimental.pallas import tpu as pltpu
from jax.sharding import PartitionSpec as P

MEMBERS = 64
SWEEPS = 4
LOWER_EDGE = 0.25
UPPER_EDGE = 12.0
HALO = SWEEPS
CX = 64
CY = 64
OBS = 256
TALL = CX + 16
WIDTH = CY * MEMBERS
BLOCKS = WIDTH // 128
EDGE = HALO * MEMBERS
STAT = 17
HALF = MEMBERS // 2
VMEM = pltpu.MemorySpace.VMEM
SMEM = pltpu.MemorySpace.SMEM
F32 = jnp.float32


def power_coeffs():
    angles = np.pi * (np.arange(64) + 0.5) / 64.0
    centre, half = 0.5 * (UPPER_EDGE + LOWER_EDGE), 0.5 * (UPPER_EDGE - LOWER_EDGE)
    nodes = centre + half * np.cos(angles)
    cheb = [2.0 / 64.0 * np.sum(np.cos(k * angles) / nodes) for k in range(SWEEPS + 1)]
    cheb[0] *= 0.5
    mono = np.polynomial.chebyshev.cheb2poly(cheb)
    return [float(v / half**k) for k, v in enumerate(mono)]


COEFFS = power_coeffs()
CENTRE = 0.5 * (UPPER_EDGE + LOWER_EDGE) - 4.0


PAD = 8


def lanes(c):
    return slice(c * 128, (c + 1) * 128)


def stencil_buf(blocks):
    return pltpu.VMEM((blocks * TALL + 2 * PAD, 128), F32)


def rows_of(c, first=0, count=TALL):
    at = PAD + c * TALL + first
    return slice(at, at + count)


def sweep(get, xi, alpha, order, coeff, scale, store, at=0, count=TALL):
    low_half = lax.broadcasted_iota(jnp.int32, (count, 128), 1) < MEMBERS
    turned = {}

    def turn(c):
        if c not in turned:
            turned[c] = pltpu.roll(get(c, at), 64, 1)
        return turned[c]

    for c, lower, upper in order:
        beside = turn(c) + jnp.where(low_half, turn(lower), turn(upper))
        beside = beside + (get(c, at - 1) + get(c, at + 1))
        applied = alpha(c) * get(c, at) - beside
        if scale != 1.0:
            applied = applied * scale
        store(c, coeff * xi(c) + applied)


def spread_kappa(alpha, shifted, count, start):
    upper = (lax.broadcasted_iota(jnp.int32, (TALL, 128), 1) >= MEMBERS).astype(jnp.int32)
    for c in range(count):
        alpha[rows_of(c), :] = jnp.take_along_axis(shifted, upper + (2 * c + start), axis=1)


def rows_kernel(lat_hbm, kap_hbm, to_odd, to_even, kap, sems):
    is_odd = lax.rem(lax.axis_index("gx"), 2) == 1
    fetch = pltpu.make_async_copy(kap_hbm, kap, sems.at[0])
    fetch.start()

    def copies(low, high):
        return (
            pltpu.make_async_copy(lat_hbm.at[0:HALO, :], low.at[:, 0:WIDTH], sems.at[1]),
            pltpu.make_async_copy(lat_hbm.at[CX - HALO : CX, :], high.at[:, 0:WIDTH], sems.at[2]),
        )

    @pl.when(is_odd)
    def _():
        for copy in copies(to_even, to_odd):
            copy.start()

    @pl.when(jnp.logical_not(is_odd))
    def _():
        for copy in copies(to_odd, to_even):
            copy.start()

    fetch.wait()
    blank = jnp.zeros((HALO, 128 - CY), F32)
    low = jnp.concatenate([kap[0:HALO, :], blank], axis=1)
    high = jnp.concatenate([kap[CX - HALO : CX, :], blank], axis=1)
    to_odd[:, WIDTH:] = jnp.where(is_odd, high, low)
    to_even[:, WIDTH:] = jnp.where(is_odd, low, high)
    for copy in copies(to_odd, to_even):
        copy.wait()


class Received:
    def __init__(self, flags, x_odd, x_even, below):
        self.is_odd = jnp.broadcast_to(flags[5:6, :], (HALO, 128)) > 0.5
        self.odd_has, self.even_has = (x_even, x_odd) if below else (x_odd, x_even)

    def __getitem__(self, c):
        return jnp.where(self.is_odd, self.odd_has[:, lanes(c)], self.even_has[:, lanes(c)])


def kappa_rows(dst, kap, xlo, xhi):
    dst[...] = jnp.zeros(dst.shape, F32)
    dst[8 : 8 + CX, 0:CY] = kap[...]
    dst[4:8, :] = xlo[BLOCKS]
    dst[8 + CX : 12 + CX, :] = xhi[BLOCKS]


def cols_kernel(flags, first, last, kap, x_odd, x_even, to_odd, to_even, kext):
    xlo, xhi = Received(flags, x_odd, x_even, True), Received(flags, x_odd, x_even, False)
    kappa_rows(kext, kap, xlo, xhi)
    turned = jnp.transpose(kext[...])
    is_odd = jnp.broadcast_to(flags[4:5, :], (8, 128)) > 0.5
    far = BLOCKS - 2
    for dst, swap in ((to_odd, False), (to_even, True)):

        def pick(low, high):
            low, high = (high, low) if swap else (low, high)
            return jnp.where(is_odd[0 : low.shape[0]], high, low)

        for i in range(2):
            for r in range(0, CX, 8):
                dst[r : r + 8, lanes(i)] = pick(first[r : r + 8, lanes(i)], last[r : r + 8, lanes(i)])
            dst[CX : CX + 4, lanes(i)] = pick(xlo[i], xlo[far + i])
            dst[CX + 4 : CX + 8, lanes(i)] = pick(xhi[i], xhi[far + i])
        columns = pick(turned[0:HALO, :], turned[CY - HALO : CY, :])
        for i in range(HALO):
            r = CX if i < 2 else CX + 7
            dst[r : r + 1, lanes(i % 2)] = columns[i : i + 1]


def keep_rows(dst, flags):
    def store(c, new):
        dst[rows_of(c, 0, 8), :] = new[0:8] * flags[0:1, :]
        dst[rows_of(c, 8, CX), :] = new[8 : 8 + CX]
        dst[rows_of(c, 8 + CX, 8), :] = new[8 + CX : TALL] * flags[1:2, :]

    return store


def into_tiles(tiles, c, new):
    for t in range(CX // 8):
        at = (t * BLOCKS + c) * 8
        tiles[at : at + 8, :] = new[8 * t : 8 * t + 8]


def fill(ext, c, body, xlo, xhi, low, high):
    zero4 = jnp.zeros((4, 128), F32)
    ext[rows_of(c, 0, 4), :] = zero4
    ext[rows_of(c, 4, 4), :] = xlo * low
    ext[rows_of(c, 8, CX), :] = body
    ext[rows_of(c, 8 + CX, 4), :] = xhi * high
    ext[rows_of(c, 12 + CX, 4), :] = zero4


def inner_kernel(flags, lat, kap, x_odd, x_even, val, var, tiles, value, weight, odd, ext, alpha, u3, u2, u1, kext):
    xlo, xhi = Received(flags, x_odd, x_even, True), Received(flags, x_odd, x_even, False)
    for c in range(BLOCKS):
        fill(ext, c, lat[:, lanes(c)], xlo[c], xhi[c], flags[0:1, :], flags[1:2, :])
    kappa_rows(kext, kap, xlo, xhi)
    spread_kappa(alpha, kext[0:TALL, :] - CENTRE, BLOCKS, 0)

    def run(src, depth, step, scale, store, at=0, count=TALL):
        order = [(c, max(c - 1, 0), min(c + 1, BLOCKS - 1)) for c in range(depth, BLOCKS - depth)]
        get = lambda c, shift: src[rows_of(c, shift, count), :]
        xi = lambda c: ext[rows_of(c, at, count), :]
        diag = lambda c: alpha[rows_of(c, at, count), :]
        sweep(get, xi, diag, order, COEFFS[step], scale, store, at, count)

    run(ext, 0, 3, COEFFS[4], keep_rows(u3, flags))
    run(u3, 1, 2, 1.0, keep_rows(u2, flags))
    run(u2, 1, 1, 1.0, keep_rows(u1, flags))
    run(u1, 2, 0, 1.0, lambda c, new: into_tiles(tiles, c, new), 8, CX)

    def column(row):
        pieces = [jnp.transpose(jnp.broadcast_to(row[i : i + 1, :], (128, 128))) for i in range(OBS // 128)]
        return jnp.concatenate(pieces, axis=0)

    value[...] = column(val[0:2, :])
    odd[...] = column(val[2:4, :])
    weight[...] = 1.0 / column(var[0:2, :])


def rim_kernel(
    flags, cell_vmem, y_odd, y_even, value, weight, odd, ext, alpha, u3, u2, u1, held,
    tiles, stat, cell, sem, ext_out, alpha_out, v3, v2, v1, kext, pbuf,
):
    fetch = pltpu.make_async_copy(cell_vmem, cell, sem)
    fetch.start()
    low, high = flags[0:1, :], flags[1:2, :]
    kext[...] = jnp.zeros((128, 128), F32)
    is_odd = jnp.broadcast_to(flags[4:5, :], (CX + 8, 128)) > 0.5
    is_odd = jnp.concatenate([is_odd, is_odd], axis=1)
    for side in range(2):
        lower, upper = (y_even, y_odd) if side == 0 else (y_odd, y_even)
        msg = jnp.where(is_odd, lower[...], upper[...])
        flag = flags[2 + side : 3 + side, :]
        for i in range(HALO):
            r = CX if i < 2 else CX + 7
            kext[i : i + 1, :] = msg[r : r + 1, lanes(i % 2)]
        shifted = jnp.transpose(kext[...])[0:TALL, :] - CENTRE
        upper = (lax.broadcasted_iota(jnp.int32, (TALL, 128), 1) >= MEMBERS).astype(jnp.int32)
        for p in (-2, -1):
            i = p + 2 if side == 0 else -1 - p
            halo = msg[CX : CX + 4, lanes(i)], msg[CX + 4 : CX + 8, lanes(i)]
            fill(ext_out, p + 2, msg[0:CX, lanes(i)] * flag, *halo, low * flag, high * flag)
            alpha_out[rows_of(p + 2), :] = jnp.take_along_axis(shifted, upper + 2 * i, axis=1)

        def local(p):
            return p if side == 0 else BLOCKS - 1 - p

        def run(near, far, mine, first, last, step, scale, store, at=0, count=TALL):
            def pick(p, here, there, ours, start):
                return here[rows_of(p + 2, start, count), :] if p in ours else there[rows_of(local(p), start, count), :]

            get = lambda p, shift: pick(p, near, far, mine, shift)
            xi = lambda p: pick(p, ext_out, ext, (-2, -1), at)
            diag = lambda p: pick(p, alpha_out, alpha, (-2, -1), at)
            order = [(p, max(p - 1, -2), p + 1) for p in range(first, last + 1)]
            if side == 1:
                order = [(p, b, a) for p, a, b in order]
            sweep(get, xi, diag, order, COEFFS[step], scale, store, at, count)

        def keep(dst):
            plain = keep_rows(dst, flags)
            return lambda p, new: plain(p + 2, new * flag if p < 0 else new)

        run(ext_out, ext, (-2, -1), -2, 0, 3, COEFFS[4], keep(v3))
        run(v3, u3, (-2, -1, 0), -1, 0, 2, 1.0, keep(v2))
        run(v2, u2, (-2, -1, 0), -1, 1, 1, 1.0, keep(v1))
        run(v1, u1, (-2, -1, 0, 1), 0, 1, 0, 1.0, lambda p, new: into_tiles(tiles, local(p), new), 8, CX)

    fetch.wait()
    for j in range(OBS):
        pbuf[j : j + 1, :] = tiles[pl.ds(cell[j], 1), :]
    both = pbuf[...]
    lane = lax.broadcasted_iota(jnp.int32, (OBS, 128), 1)
    member = lane < MEMBERS
    predicted = jnp.where(odd[...] > 0.5, pltpu.roll(both, 64, 1), both)
    predicted = jnp.where(member, predicted, 0.0)
    mean = jnp.sum(predicted, axis=1, keepdims=True) * (1.0 / MEMBERS)
    spread = jnp.where(member, predicted - mean, jnp.where(lane == MEMBERS, value[...] - mean, 0.0))
    full = lax.dot_general(
        spread * weight[...],
        spread,
        (((0,), (0,)), ((), ())),
        precision=lax.Precision.HIGHEST,
        preferred_element_type=F32,
    )
    lane = lax.broadcasted_iota(jnp.int32, (HALF, 128), 1)
    row = lax.broadcasted_iota(jnp.int32, (HALF, 128), 0)
    first, second = full[0:HALF], full[HALF:MEMBERS]
    packed = jnp.where(lane >= row, first, pltpu.roll(second, 96, 1))
    folded = jnp.where(lane[0:16] < MEMBERS, packed[0:16], pltpu.roll(packed[16:32], 64, 1))
    diagonal = jnp.sum(jnp.where(lane == row + 96, pltpu.roll(second, 64, 1), 0.0), axis=0, keepdims=True)
    last = jnp.where(lane[0:1] < 96, full[MEMBERS : MEMBERS + 1], diagonal)
    stat[0 : STAT - 1, :] = folded
    stat[STAT - 1 : STAT, :] = last


def eliminate(aug):
    size = 8
    row = lax.broadcasted_iota(jnp.int32, (size, 128), 0)
    for start in range(0, MEMBERS, size):
        columns = [jnp.broadcast_to(aug[:, k : k + 1], (MEMBERS, 128)) for k in range(start, start + size)]
        block = [column[start : start + size] for column in columns]
        pivot_rows = aug[start : start + size]
        for i in range(size):
            here = row == i
            inverse = 1.0 / block[i][i : i + 1]

            def clear(a):
                scaled = a[i : i + 1] * inverse
                return jnp.where(here, scaled, a - block[i] * scaled)

            block = block[: i + 1] + [clear(a) for a in block[i + 1 :]]
            pivot_rows = clear(pivot_rows)
        pieces = []
        for at in range(0, MEMBERS, size):
            if at == start:
                pieces.append(pivot_rows)
                continue
            terms = [column[at : at + size] * pivot_rows[i : i + 1] for i, column in enumerate(columns)]
            while len(terms) > 1:
                terms = [a + b for a, b in zip(terms[0::2], terms[1::2])]
            pieces.append(aug[at : at + size] - terms[0])
        aug = jnp.concatenate(pieces, axis=0)
    return aug


def split(a):
    hi = a.astype(jnp.bfloat16)
    return hi, (a - hi.astype(F32)).astype(jnp.bfloat16)


def solve_kernel(parts, tiles, weights_out, prior_hbm, total, sem):
    copy = pltpu.make_async_copy(tiles, prior_hbm, sem)
    copy.start()
    for i in range(STAT):
        row = parts[0, i]
        for d in range(1, parts.shape[0]):
            row = row + parts[d, i]
        total[i : i + 1, :] = row
    folded, last = total[0:16, :], total[16:17, :]
    packed = jnp.concatenate([folded, pltpu.roll(folded, 64, 1)], axis=0)
    tall = jnp.concatenate([packed, jnp.zeros((32, 128), F32), jnp.broadcast_to(last, (64, 128))], axis=0)
    turned = jnp.transpose(tall)
    lane = lax.broadcasted_iota(jnp.int32, (HALF, 128), 1)
    row = lax.broadcasted_iota(jnp.int32, (HALF, 128), 0)
    first = jnp.where(lane >= row, packed, turned[0:HALF])
    corner = jnp.where(lane < row + HALF, pltpu.roll(packed, 32, 1), pltpu.roll(turned[0:HALF], 32, 1))
    corner = jnp.where(lane == row + HALF, pltpu.roll(last, 64, 1), corner)
    second = jnp.where(lane < HALF, turned[HALF:MEMBERS], corner)
    gram = jnp.concatenate([first, second], axis=0)

    shape = (MEMBERS, 128)
    row = lax.broadcasted_iota(jnp.int32, shape, 0)
    lane = lax.broadcasted_iota(jnp.int32, shape, 1)
    eye = row == lane
    low = lane < MEMBERS
    square = jnp.where(lane[0:1] == MEMBERS, last, 0.0) * float(MEMBERS)
    trace = jnp.sum(jnp.where(eye, gram, 0.0), axis=0, keepdims=True)
    misfit = jnp.sum(square + trace, axis=1, keepdims=True)
    inflation = 1.0 + misfit / float(MEMBERS * (MEMBERS - 1))
    shift = (MEMBERS - 1) * inflation
    right = turned[0:MEMBERS] - pltpu.roll(gram, 64, 1)
    aug = eliminate(jnp.where(low, gram + jnp.where(eye, shift, 0.0), right))
    gain = aug - jnp.sum(aug, axis=0, keepdims=True) * (1.0 / MEMBERS)
    weights = jnp.concatenate(
        [jnp.where(low, pltpu.roll(gain, 64, 1), 0.0), jnp.where(low, 0.0, gain)], axis=0
    )

    w_hi, w_lo = split(weights)
    weights_out[0:128, 0:128] = w_hi
    weights_out[0:128, 128:256] = w_lo
    weights_out[128:256, 0:128] = w_hi
    weights_out[128:256, 128:256] = jnp.zeros((128, 128), jnp.bfloat16)
    copy.wait()


def update_kernel(lat, weights, out_hbm, out, sems):
    both = weights[...]
    copies = []
    for t in range(CX // 8):
        at = slice(t * 256, (t + 1) * 256)
        x = lat[at, :]
        product = jnp.dot(jnp.concatenate(split(x), axis=1), both, preferred_element_type=F32)
        out[at, :] = x + (product[:, 0:128] + product[:, 128:256])
        copies.append(pltpu.make_async_copy(out.at[at, :], out_hbm.at[at, :], sems.at[t]))
        copies[-1].start()
    for copy in copies:
        copy.wait()


def pairs(axis, first):
    count_x, count_y = lax.axis_size("gx"), lax.axis_size("gy")
    count = count_x if axis == "gx" else count_y
    moves = []
    for x in range(count_x):
        for y in range(count_y):
            at = x if axis == "gx" else y
            to = at + 1 if (at - first) % 2 == 0 else at - 1
            if not 0 <= to < count:
                target = (x, y ^ 1) if axis == "gx" else (x ^ 1, y)
            else:
                target = (to, y) if axis == "gx" else (x, to)
            moves.append((x * count_y + y, target[0] * count_y + target[1]))
    return moves


def exchange(block, axis, first):
    return lax.ppermute(block, ("gx", "gy"), pairs(axis, first))


def arr(*shape):
    return jax.ShapeDtypeStruct(shape, F32)


def buf(*shape):
    return pltpu.VMEM(shape, F32)


def params(mib):
    return pltpu.CompilerParams(vmem_limit_bytes=mib << 20)


def cost(flops, moved):
    return pl.CostEstimate(flops=flops, bytes_accessed=moved, transcendentals=0)


def to_tiles(a):
    return a.reshape(CX // 8, 8, BLOCKS, 128).transpose(0, 2, 1, 3).reshape(CX * BLOCKS, 128)


def from_tiles(a):
    return a.reshape(CX // 8, BLOCKS, 8, 128).transpose(0, 2, 1, 3).reshape(CX, WIDTH)


def per_device(latent, kappa, obs_cell, obs_value, obs_var):
    gx, gy = lax.axis_index("gx"), lax.axis_index("gy")
    last_x, last_y = lax.axis_size("gx") - 1, lax.axis_size("gy") - 1
    states = [gx > 0, gx < last_x, gy > 0, gy < last_y, gy % 2 == 1, gx % 2 == 1]
    flags = jnp.broadcast_to(jnp.stack(states + states[:2]).astype(F32)[:, None], (8, 128))
    odd = (obs_cell & 1).astype(F32)
    obs_x, obs_y = obs_cell >> 6, obs_cell & (CY - 1)
    obs_row = (obs_x & 56) * BLOCKS + (obs_y >> 1) * 8 + (obs_x & 7)
    val = jnp.concatenate([obs_value.reshape(2, 128), odd.reshape(2, 128)], axis=0)
    var = obs_var.reshape(2, 128)
    vmem, anywhere = pl.BlockSpec(memory_space=VMEM), pl.BlockSpec(memory_space=pl.ANY)
    hbm = pl.BlockSpec(memory_space=pltpu.MemorySpace.HBM)

    def part(shape, *at):
        return pl.BlockSpec(shape, lambda i: at)

    to_odd, to_even, kappa = pl.pallas_call(
        rows_kernel,
        out_shape=(arr(HALO, WIDTH + 128),) * 2 + (arr(CX, CY),),
        in_specs=[hbm, hbm],
        out_specs=(vmem,) * 3,
        scratch_shapes=[pltpu.SemaphoreType.DMA((3,))],
        compiler_params=params(4),
        name="rows",
    )(*(pltpu.with_memory_space_constraint(a, pltpu.MemorySpace.HBM) for a in (latent, kappa)))
    x_odd = exchange(to_odd, "gx", 1)
    x_even = exchange(to_even, "gx", 0)

    whole = part((HALO, WIDTH + 128), 0, 0)
    to_odd, to_even = pl.pallas_call(
        cols_kernel,
        grid=(1,),
        out_shape=(arr(CX + 8, EDGE),) * 2,
        in_specs=[part((8, 128), 0, 0), part((CX, EDGE), 0, 0), part((CX, EDGE), 0, WIDTH // EDGE - 1), part((CX, CY), 0, 0), whole, whole],
        out_specs=(part((CX + 8, EDGE), 0, 0),) * 2,
        scratch_shapes=[buf(128, 128)],
        compiler_params=params(4),
        name="cols",
    )(flags, latent, latent, kappa, x_odd, x_even)
    y_odd = exchange(to_odd, "gy", 1)
    y_even = exchange(to_even, "gy", 0)

    field = arr(BLOCKS * TALL + 2 * PAD, 128)
    tiles, *rest = pl.pallas_call(
        inner_kernel,
        out_shape=(arr(CX * BLOCKS, 128),) + (arr(OBS, 128),) * 3 + (field,) * 5,
        in_specs=[vmem] * 7,
        out_specs=(vmem,) * 9,
        scratch_shapes=[buf(128, 128)],
        compiler_params=params(12),
        cost_estimate=cost(20_000_000, 12_000_000),
        name="inner",
    )(flags, latent, kappa, x_odd, x_even, val, var)

    tiles, stat = pl.pallas_call(
        rim_kernel,
        out_shape=(arr(CX * BLOCKS, 128), arr(STAT, 128)),
        in_specs=[vmem, anywhere] + [vmem] * 11,
        out_specs=(vmem, vmem),
        scratch_shapes=[pltpu.SMEM((OBS,), jnp.int32), pltpu.SemaphoreType.DMA]
        + [stencil_buf(4)] * 5
        + [buf(128, 128), buf(OBS, 128)],
        input_output_aliases={12: 0},
        compiler_params=params(12),
        name="rim",
    )(flags, obs_row, y_odd, y_even, *rest, tiles)

    stat = stat[:, None, :]
    stat = stat + exchange(stat, "gx", 0)
    count = lax.axis_size("gx")
    groups = [list(range(i, count, 2)) for i in range(2)]
    parts = jnp.broadcast_to(stat[None], (count // 2,) + stat.shape)
    parts = lax.all_to_all(parts, "gx", 0, 0, axis_index_groups=groups)
    stat = jnp.sum(parts, axis=0)
    width = lax.axis_size("gy")
    parts = lax.all_to_all(jnp.broadcast_to(stat[None], (width,) + stat.shape), "gy", 0, 0)

    weights, prior = pl.pallas_call(
        solve_kernel,
        out_shape=(jax.ShapeDtypeStruct((256, 256), jnp.bfloat16), arr(CX * BLOCKS, 128)),
        in_specs=[vmem] * 2,
        out_specs=(vmem, anywhere),
        scratch_shapes=[buf(24, 128), pltpu.SemaphoreType.DMA],
        compiler_params=params(12),
        name="solve",
    )(parts, tiles)
    latent_new = pl.pallas_call(
        update_kernel,
        out_shape=arr(CX * BLOCKS, 128),
        in_specs=[vmem] * 2,
        out_specs=anywhere,
        scratch_shapes=[buf(CX * BLOCKS, 128), pltpu.SemaphoreType.DMA((CX // 8,))],
        compiler_params=params(12),
        name="update",
    )(to_tiles(latent), weights)
    return (from_tiles(latent_new), from_tiles(prior))


def solution(mesh):
    placed = (P("gx", "gy"), P("gx", "gy"), P(("gx", "gy")), P(("gx", "gy")), P(("gx", "gy")))
    return jax.shard_map(
        per_device,
        mesh=mesh,
        in_specs=placed,
        out_specs=(P("gx", "gy"), P("gx", "gy")),
        check_vma=False,
    )
```

```python
import jax
import jax.numpy as jnp
import numpy as np
from jax import lax
from jax.experimental import pallas as pl
from jax.experimental.pallas import tpu as pltpu
from jax.sharding import PartitionSpec as P

MEMBERS = 64
SWEEPS = 4
LOWER_EDGE = 0.25
UPPER_EDGE = 12.0
HALO = SWEEPS
CX = 64
CY = 64
OBS = 256
TALL = CX + 16
WIDTH = CY * MEMBERS
BLOCKS = WIDTH // 128
EDGE = HALO * MEMBERS
STAT = 17
HALF = MEMBERS // 2
VMEM = pltpu.MemorySpace.VMEM
SMEM = pltpu.MemorySpace.SMEM
F32 = jnp.float32


def power_coeffs():
    angles = np.pi * (np.arange(64) + 0.5) / 64.0
    centre, half = 0.5 * (UPPER_EDGE + LOWER_EDGE), 0.5 * (UPPER_EDGE - LOWER_EDGE)
    nodes = centre + half * np.cos(angles)
    cheb = [2.0 / 64.0 * np.sum(np.cos(k * angles) / nodes) for k in range(SWEEPS + 1)]
    cheb[0] *= 0.5
    mono = np.polynomial.chebyshev.cheb2poly(cheb)
    return [float(v / half**k) for k, v in enumerate(mono)]


COEFFS = power_coeffs()
CENTRE = 0.5 * (UPPER_EDGE + LOWER_EDGE) - 4.0


PAD = 8


def lanes(c):
    return slice(c * 128, (c + 1) * 128)


def stencil_buf(blocks):
    return pltpu.VMEM((blocks * TALL + 2 * PAD, 128), F32)


def rows_of(c, first=0, count=TALL):
    at = PAD + c * TALL + first
    return slice(at, at + count)


def sweep(get, xi, alpha, order, coeff, scale, store, at=0, count=TALL):
    low_half = lax.broadcasted_iota(jnp.int32, (count, 128), 1) < MEMBERS
    turned = {}

    def turn(c):
        if c not in turned:
            turned[c] = pltpu.roll(get(c, at), 64, 1)
        return turned[c]

    for c, lower, upper in order:
        beside = turn(c) + jnp.where(low_half, turn(lower), turn(upper))
        beside = beside + (get(c, at - 1) + get(c, at + 1))
        applied = alpha(c) * get(c, at) - beside
        if scale != 1.0:
            applied = applied * scale
        store(c, coeff * xi(c) + applied)


def spread_kappa(alpha, shifted, count, start):
    upper = (lax.broadcasted_iota(jnp.int32, (TALL, 128), 1) >= MEMBERS).astype(jnp.int32)
    for c in range(count):
        alpha[rows_of(c), :] = jnp.take_along_axis(shifted, upper + (2 * c + start), axis=1)


def rows_kernel(lat_hbm, kap_hbm, to_odd, to_even, kap, sems):
    is_odd = lax.rem(lax.axis_index("gx"), 2) == 1
    fetch = pltpu.make_async_copy(kap_hbm, kap, sems.at[0])
    fetch.start()

    def copies(low, high):
        return (
            pltpu.make_async_copy(lat_hbm.at[0:HALO, :], low.at[:, 0:WIDTH], sems.at[1]),
            pltpu.make_async_copy(lat_hbm.at[CX - HALO : CX, :], high.at[:, 0:WIDTH], sems.at[2]),
        )

    @pl.when(is_odd)
    def _():
        for copy in copies(to_even, to_odd):
            copy.start()

    @pl.when(jnp.logical_not(is_odd))
    def _():
        for copy in copies(to_odd, to_even):
            copy.start()

    fetch.wait()
    blank = jnp.zeros((HALO, 128 - CY), F32)
    low = jnp.concatenate([kap[0:HALO, :], blank], axis=1)
    high = jnp.concatenate([kap[CX - HALO : CX, :], blank], axis=1)
    to_odd[:, WIDTH:] = jnp.where(is_odd, high, low)
    to_even[:, WIDTH:] = jnp.where(is_odd, low, high)
    for copy in copies(to_odd, to_even):
        copy.wait()


class Received:
    def __init__(self, flags, x_odd, x_even, below):
        self.is_odd = jnp.broadcast_to(flags[5:6, :], (HALO, 128)) > 0.5
        self.odd_has, self.even_has = (x_even, x_odd) if below else (x_odd, x_even)

    def __getitem__(self, c):
        return jnp.where(self.is_odd, self.odd_has[:, lanes(c)], self.even_has[:, lanes(c)])


def kappa_rows(dst, kap, xlo, xhi):
    dst[...] = jnp.zeros(dst.shape, F32)
    dst[8 : 8 + CX, 0:CY] = kap[...]
    dst[4:8, :] = xlo[BLOCKS]
    dst[8 + CX : 12 + CX, :] = xhi[BLOCKS]


def cols_kernel(flags, first, last, kap, x_odd, x_even, to_odd, to_even, kext):
    xlo, xhi = Received(flags, x_odd, x_even, True), Received(flags, x_odd, x_even, False)
    kappa_rows(kext, kap, xlo, xhi)
    turned = jnp.transpose(kext[...])
    is_odd = jnp.broadcast_to(flags[4:5, :], (8, 128)) > 0.5
    far = BLOCKS - 2
    for dst, swap in ((to_odd, False), (to_even, True)):

        def pick(low, high):
            low, high = (high, low) if swap else (low, high)
            return jnp.where(is_odd[0 : low.shape[0]], high, low)

        for i in range(2):
            for r in range(0, CX, 8):
                dst[r : r + 8, lanes(i)] = pick(first[r : r + 8, lanes(i)], last[r : r + 8, lanes(i)])
            dst[CX : CX + 4, lanes(i)] = pick(xlo[i], xlo[far + i])
            dst[CX + 4 : CX + 8, lanes(i)] = pick(xhi[i], xhi[far + i])
        columns = pick(turned[0:HALO, :], turned[CY - HALO : CY, :])
        for i in range(HALO):
            r = CX if i < 2 else CX + 7
            dst[r : r + 1, lanes(i % 2)] = columns[i : i + 1]


def keep_rows(dst, flags):
    def store(c, new):
        dst[rows_of(c, 0, 8), :] = new[0:8] * flags[0:1, :]
        dst[rows_of(c, 8, CX), :] = new[8 : 8 + CX]
        dst[rows_of(c, 8 + CX, 8), :] = new[8 + CX : TALL] * flags[1:2, :]

    return store


def into_tiles(tiles, c, new):
    for t in range(CX // 8):
        at = (t * BLOCKS + c) * 8
        tiles[at : at + 8, :] = new[8 * t : 8 * t + 8]


def fill(ext, c, body, xlo, xhi, low, high):
    zero4 = jnp.zeros((4, 128), F32)
    ext[rows_of(c, 0, 4), :] = zero4
    ext[rows_of(c, 4, 4), :] = xlo * low
    ext[rows_of(c, 8, CX), :] = body
    ext[rows_of(c, 8 + CX, 4), :] = xhi * high
    ext[rows_of(c, 12 + CX, 4), :] = zero4


def inner_kernel(flags, lat, kap, x_odd, x_even, val, var, tiles, value, weight, odd, ext, alpha, u3, u2, u1, kext):
    xlo, xhi = Received(flags, x_odd, x_even, True), Received(flags, x_odd, x_even, False)
    for c in range(BLOCKS):
        fill(ext, c, lat[:, lanes(c)], xlo[c], xhi[c], flags[0:1, :], flags[1:2, :])
    kappa_rows(kext, kap, xlo, xhi)
    spread_kappa(alpha, kext[0:TALL, :] - CENTRE, BLOCKS, 0)

    def run(src, depth, step, scale, store, at=0, count=TALL):
        order = [(c, max(c - 1, 0), min(c + 1, BLOCKS - 1)) for c in range(depth, BLOCKS - depth)]
        get = lambda c, shift: src[rows_of(c, shift, count), :]
        xi = lambda c: ext[rows_of(c, at, count), :]
        diag = lambda c: alpha[rows_of(c, at, count), :]
        sweep(get, xi, diag, order, COEFFS[step], scale, store, at, count)

    run(ext, 0, 3, COEFFS[4], keep_rows(u3, flags))
    run(u3, 1, 2, 1.0, keep_rows(u2, flags))
    run(u2, 1, 1, 1.0, keep_rows(u1, flags))
    run(u1, 2, 0, 1.0, lambda c, new: into_tiles(tiles, c, new), 8, CX)

    def column(row):
        pieces = [jnp.transpose(jnp.broadcast_to(row[i : i + 1, :], (128, 128))) for i in range(OBS // 128)]
        return jnp.concatenate(pieces, axis=0)

    value[...] = column(val[0:2, :])
    odd[...] = column(val[2:4, :])
    weight[...] = 1.0 / column(var[0:2, :])


def rim_kernel(
    flags, cell_vmem, y_odd, y_even, value, weight, odd, ext, alpha, u3, u2, u1, held,
    tiles, stat, cell, sem, ext_out, alpha_out, v3, v2, v1, kext, pbuf,
):
    fetch = pltpu.make_async_copy(cell_vmem, cell, sem)
    fetch.start()
    low, high = flags[0:1, :], flags[1:2, :]
    kext[...] = jnp.zeros((128, 128), F32)
    is_odd = jnp.broadcast_to(flags[4:5, :], (CX + 8, 128)) > 0.5
    is_odd = jnp.concatenate([is_odd, is_odd], axis=1)
    sides = ((y_even, y_odd), (y_odd, y_even))
    for side, (lower, upper) in enumerate(sides):
        for i in range(HALO):
            r = CX if i < 2 else CX + 7
            at = slice(r, r + 1), lanes(i % 2)
            row = side * HALO + i
            kext[row : row + 1, :] = jnp.where(is_odd[0:1, 0:128], lower[at], upper[at])
    shifted = jnp.transpose(kext[...])[0:TALL, :] - CENTRE
    for side, (lower, upper) in enumerate(sides):
        msg = jnp.where(is_odd, lower[...], upper[...])
        flag = flags[2 + side : 3 + side, :]
        half = (lax.broadcasted_iota(jnp.int32, (TALL, 128), 1) >= MEMBERS).astype(jnp.int32)
        for p in (-2, -1):
            i = p + 2 if side == 0 else -1 - p
            halo = msg[CX : CX + 4, lanes(i)], msg[CX + 4 : CX + 8, lanes(i)]
            fill(ext_out, p + 2, msg[0:CX, lanes(i)] * flag, *halo, low * flag, high * flag)
            alpha_out[rows_of(p + 2), :] = jnp.take_along_axis(shifted, half + (side * HALO + 2 * i), axis=1)

        def local(p):
            return p if side == 0 else BLOCKS - 1 - p

        def run(near, far, mine, first, last, step, scale, store, at=0, count=TALL):
            def pick(p, here, there, ours, start):
                return here[rows_of(p + 2, start, count), :] if p in ours else there[rows_of(local(p), start, count), :]

            get = lambda p, shift: pick(p, near, far, mine, shift)
            xi = lambda p: pick(p, ext_out, ext, (-2, -1), at)
            diag = lambda p: pick(p, alpha_out, alpha, (-2, -1), at)
            order = [(p, max(p - 1, -2), p + 1) for p in range(first, last + 1)]
            if side == 1:
                order = [(p, b, a) for p, a, b in order]
            sweep(get, xi, diag, order, COEFFS[step], scale, store, at, count)

        def keep(dst):
            plain = keep_rows(dst, flags)
            return lambda p, new: plain(p + 2, new * flag if p < 0 else new)

        run(ext_out, ext, (-2, -1), -2, 0, 3, COEFFS[4], keep(v3))
        run(v3, u3, (-2, -1, 0), -1, 0, 2, 1.0, keep(v2))
        run(v2, u2, (-2, -1, 0), -1, 1, 1, 1.0, keep(v1))
        run(v1, u1, (-2, -1, 0, 1), 0, 1, 0, 1.0, lambda p, new: into_tiles(tiles, local(p), new), 8, CX)

    fetch.wait()
    for j in range(OBS):
        pbuf[j : j + 1, :] = tiles[pl.ds(cell[j], 1), :]
    both = pbuf[...]
    lane = lax.broadcasted_iota(jnp.int32, (OBS, 128), 1)
    member = lane < MEMBERS
    predicted = jnp.where(odd[...] > 0.5, pltpu.roll(both, 64, 1), both)
    predicted = jnp.where(member, predicted, 0.0)
    mean = jnp.sum(predicted, axis=1, keepdims=True) * (1.0 / MEMBERS)
    spread = jnp.where(member, predicted - mean, jnp.where(lane == MEMBERS, value[...] - mean, 0.0))
    full = lax.dot_general(
        spread * weight[...],
        spread,
        (((0,), (0,)), ((), ())),
        precision=lax.Precision.HIGHEST,
        preferred_element_type=F32,
    )
    lane = lax.broadcasted_iota(jnp.int32, (HALF, 128), 1)
    row = lax.broadcasted_iota(jnp.int32, (HALF, 128), 0)
    first, second = full[0:HALF], full[HALF:MEMBERS]
    packed = jnp.where(lane >= row, first, pltpu.roll(second, 96, 1))
    folded = jnp.where(lane[0:16] < MEMBERS, packed[0:16], pltpu.roll(packed[16:32], 64, 1))
    diagonal = jnp.sum(jnp.where(lane == row + 96, pltpu.roll(second, 64, 1), 0.0), axis=0, keepdims=True)
    last = jnp.where(lane[0:1] < 96, full[MEMBERS : MEMBERS + 1], diagonal)
    stat[0 : STAT - 1, :] = folded
    stat[STAT - 1 : STAT, :] = last


def eliminate(aug):
    size = 8
    row = lax.broadcasted_iota(jnp.int32, (size, 128), 0)
    for start in range(0, MEMBERS, size):
        columns = [jnp.broadcast_to(aug[:, k : k + 1], (MEMBERS, 128)) for k in range(start, start + size)]
        block = [column[start : start + size] for column in columns]
        pivot_rows = aug[start : start + size]
        for i in range(size):
            here = row == i
            inverse = 1.0 / block[i][i : i + 1]

            def clear(a):
                scaled = a[i : i + 1] * inverse
                return jnp.where(here, scaled, a - block[i] * scaled)

            block = block[: i + 1] + [clear(a) for a in block[i + 1 :]]
            pivot_rows = clear(pivot_rows)
        pieces = []
        for at in range(0, MEMBERS, size):
            if at == start:
                pieces.append(pivot_rows)
                continue
            terms = [column[at : at + size] * pivot_rows[i : i + 1] for i, column in enumerate(columns)]
            while len(terms) > 1:
                terms = [a + b for a, b in zip(terms[0::2], terms[1::2])]
            pieces.append(aug[at : at + size] - terms[0])
        aug = jnp.concatenate(pieces, axis=0)
    return aug


def split(a):
    hi = a.astype(jnp.bfloat16)
    return hi, (a - hi.astype(F32)).astype(jnp.bfloat16)


def solve_kernel(parts, tiles, weights_out, prior_hbm, total, sem):
    copy = pltpu.make_async_copy(tiles, prior_hbm, sem)
    copy.start()
    for i in range(STAT):
        row = parts[0, i]
        for d in range(1, parts.shape[0]):
            row = row + parts[d, i]
        total[i : i + 1, :] = row
    folded, last = total[0:16, :], total[16:17, :]
    packed = jnp.concatenate([folded, pltpu.roll(folded, 64, 1)], axis=0)
    tall = jnp.concatenate([packed, jnp.zeros((32, 128), F32), jnp.broadcast_to(last, (64, 128))], axis=0)
    turned = jnp.transpose(tall)
    lane = lax.broadcasted_iota(jnp.int32, (HALF, 128), 1)
    row = lax.broadcasted_iota(jnp.int32, (HALF, 128), 0)
    first = jnp.where(lane >= row, packed, turned[0:HALF])
    corner = jnp.where(lane < row + HALF, pltpu.roll(packed, 32, 1), pltpu.roll(turned[0:HALF], 32, 1))
    corner = jnp.where(lane == row + HALF, pltpu.roll(last, 64, 1), corner)
    second = jnp.where(lane < HALF, turned[HALF:MEMBERS], corner)
    gram = jnp.concatenate([first, second], axis=0)

    shape = (MEMBERS, 128)
    row = lax.broadcasted_iota(jnp.int32, shape, 0)
    lane = lax.broadcasted_iota(jnp.int32, shape, 1)
    eye = row == lane
    low = lane < MEMBERS
    square = jnp.where(lane[0:1] == MEMBERS, last, 0.0) * float(MEMBERS)
    trace = jnp.sum(jnp.where(eye, gram, 0.0), axis=0, keepdims=True)
    misfit = jnp.sum(square + trace, axis=1, keepdims=True)
    inflation = 1.0 + misfit / float(MEMBERS * (MEMBERS - 1))
    shift = (MEMBERS - 1) * inflation
    right = turned[0:MEMBERS] - pltpu.roll(gram, 64, 1)
    aug = eliminate(jnp.where(low, gram + jnp.where(eye, shift, 0.0), right))
    gain = aug - jnp.sum(aug, axis=0, keepdims=True) * (1.0 / MEMBERS)
    weights = jnp.concatenate(
        [jnp.where(low, pltpu.roll(gain, 64, 1), 0.0), jnp.where(low, 0.0, gain)], axis=0
    )

    w_hi, w_lo = split(weights)
    weights_out[0:128, 0:128] = w_hi
    weights_out[0:128, 128:256] = w_lo
    weights_out[128:256, 0:128] = w_hi
    weights_out[128:256, 128:256] = jnp.zeros((128, 128), jnp.bfloat16)
    copy.wait()


def update_kernel(lat, weights, out_hbm, out, sems):
    both = weights[...]
    copies = []
    for t in range(CX // 8):
        at = slice(t * 256, (t + 1) * 256)
        x = lat[at, :]
        product = jnp.dot(jnp.concatenate(split(x), axis=1), both, preferred_element_type=F32)
        out[at, :] = x + (product[:, 0:128] + product[:, 128:256])
        copies.append(pltpu.make_async_copy(out.at[at, :], out_hbm.at[at, :], sems.at[t]))
        copies[-1].start()
    for copy in copies:
        copy.wait()


def pairs(axis, first):
    count_x, count_y = lax.axis_size("gx"), lax.axis_size("gy")
    count = count_x if axis == "gx" else count_y
    moves = []
    for x in range(count_x):
        for y in range(count_y):
            at = x if axis == "gx" else y
            to = at + 1 if (at - first) % 2 == 0 else at - 1
            if not 0 <= to < count:
                target = (x, y ^ 1) if axis == "gx" else (x ^ 1, y)
            else:
                target = (to, y) if axis == "gx" else (x, to)
            moves.append((x * count_y + y, target[0] * count_y + target[1]))
    return moves


def exchange(block, axis, first):
    return lax.ppermute(block, ("gx", "gy"), pairs(axis, first))


def arr(*shape):
    return jax.ShapeDtypeStruct(shape, F32)


def buf(*shape):
    return pltpu.VMEM(shape, F32)


def params(mib):
    return pltpu.CompilerParams(vmem_limit_bytes=mib << 20)


def cost(flops, moved):
    return pl.CostEstimate(flops=flops, bytes_accessed=moved, transcendentals=0)


def to_tiles(a):
    return a.reshape(CX // 8, 8, BLOCKS, 128).transpose(0, 2, 1, 3).reshape(CX * BLOCKS, 128)


def from_tiles(a):
    return a.reshape(CX // 8, BLOCKS, 8, 128).transpose(0, 2, 1, 3).reshape(CX, WIDTH)


def per_device(latent, kappa, obs_cell, obs_value, obs_var):
    gx, gy = lax.axis_index("gx"), lax.axis_index("gy")
    last_x, last_y = lax.axis_size("gx") - 1, lax.axis_size("gy") - 1
    states = [gx > 0, gx < last_x, gy > 0, gy < last_y, gy % 2 == 1, gx % 2 == 1]
    flags = jnp.broadcast_to(jnp.stack(states + states[:2]).astype(F32)[:, None], (8, 128))
    odd = (obs_cell & 1).astype(F32)
    obs_x, obs_y = obs_cell >> 6, obs_cell & (CY - 1)
    obs_row = (obs_x & 56) * BLOCKS + (obs_y >> 1) * 8 + (obs_x & 7)
    val = jnp.concatenate([obs_value.reshape(2, 128), odd.reshape(2, 128)], axis=0)
    var = obs_var.reshape(2, 128)
    vmem, anywhere = pl.BlockSpec(memory_space=VMEM), pl.BlockSpec(memory_space=pl.ANY)
    hbm = pl.BlockSpec(memory_space=pltpu.MemorySpace.HBM)

    def part(shape, *at):
        return pl.BlockSpec(shape, lambda i: at)

    to_odd, to_even, kappa = pl.pallas_call(
        rows_kernel,
        out_shape=(arr(HALO, WIDTH + 128),) * 2 + (arr(CX, CY),),
        in_specs=[hbm, hbm],
        out_specs=(vmem,) * 3,
        scratch_shapes=[pltpu.SemaphoreType.DMA((3,))],
        compiler_params=params(4),
        name="rows",
    )(*(pltpu.with_memory_space_constraint(a, pltpu.MemorySpace.HBM) for a in (latent, kappa)))
    x_odd = exchange(to_odd, "gx", 1)
    x_even = exchange(to_even, "gx", 0)

    whole = part((HALO, WIDTH + 128), 0, 0)
    to_odd, to_even = pl.pallas_call(
        cols_kernel,
        grid=(1,),
        out_shape=(arr(CX + 8, EDGE),) * 2,
        in_specs=[part((8, 128), 0, 0), part((CX, EDGE), 0, 0), part((CX, EDGE), 0, WIDTH // EDGE - 1), part((CX, CY), 0, 0), whole, whole],
        out_specs=(part((CX + 8, EDGE), 0, 0),) * 2,
        scratch_shapes=[buf(128, 128)],
        compiler_params=params(4),
        name="cols",
    )(flags, latent, latent, kappa, x_odd, x_even)
    y_odd = exchange(to_odd, "gy", 1)
    y_even = exchange(to_even, "gy", 0)

    field = arr(BLOCKS * TALL + 2 * PAD, 128)
    tiles, *rest = pl.pallas_call(
        inner_kernel,
        out_shape=(arr(CX * BLOCKS, 128),) + (arr(OBS, 128),) * 3 + (field,) * 5,
        in_specs=[vmem] * 7,
        out_specs=(vmem,) * 9,
        scratch_shapes=[buf(128, 128)],
        compiler_params=params(12),
        cost_estimate=cost(20_000_000, 12_000_000),
        name="inner",
    )(flags, latent, kappa, x_odd, x_even, val, var)

    tiles, stat = pl.pallas_call(
        rim_kernel,
        out_shape=(arr(CX * BLOCKS, 128), arr(STAT, 128)),
        in_specs=[vmem, anywhere] + [vmem] * 11,
        out_specs=(vmem, vmem),
        scratch_shapes=[pltpu.SMEM((OBS,), jnp.int32), pltpu.SemaphoreType.DMA]
        + [stencil_buf(4)] * 5
        + [buf(128, 128), buf(OBS, 128)],
        input_output_aliases={12: 0},
        compiler_params=params(12),
        name="rim",
    )(flags, obs_row, y_odd, y_even, *rest, tiles)

    stat = stat[:, None, :]
    stat = stat + exchange(stat, "gx", 0)
    count = lax.axis_size("gx")
    groups = [list(range(i, count, 2)) for i in range(2)]
    parts = jnp.broadcast_to(stat[None], (count // 2,) + stat.shape)
    parts = lax.all_to_all(parts, "gx", 0, 0, axis_index_groups=groups)
    stat = jnp.sum(parts, axis=0)
    width = lax.axis_size("gy")
    parts = lax.all_to_all(jnp.broadcast_to(stat[None], (width,) + stat.shape), "gy", 0, 0)

    weights, prior = pl.pallas_call(
        solve_kernel,
        out_shape=(jax.ShapeDtypeStruct((256, 256), jnp.bfloat16), arr(CX * BLOCKS, 128)),
        in_specs=[vmem] * 2,
        out_specs=(vmem, anywhere),
        scratch_shapes=[buf(24, 128), pltpu.SemaphoreType.DMA],
        compiler_params=params(12),
        name="solve",
    )(parts, tiles)
    latent_new = pl.pallas_call(
        update_kernel,
        out_shape=arr(CX * BLOCKS, 128),
        in_specs=[vmem] * 2,
        out_specs=anywhere,
        scratch_shapes=[buf(CX * BLOCKS, 128), pltpu.SemaphoreType.DMA((CX // 8,))],
        compiler_params=params(12),
        name="update",
    )(to_tiles(latent), weights)
    return (from_tiles(latent_new), from_tiles(prior))


def solution(mesh):
    placed = (P("gx", "gy"), P("gx", "gy"), P(("gx", "gy")), P(("gx", "gy")), P(("gx", "gy")))
    return jax.shard_map(
        per_device,
        mesh=mesh,
        in_specs=placed,
        out_specs=(P("gx", "gy"), P("gx", "gy")),
        check_vma=False,
    )
```

```python
import jax
import jax.numpy as jnp
import numpy as np
from jax import lax
from jax.experimental import pallas as pl
from jax.experimental.pallas import tpu as pltpu
from jax.sharding import PartitionSpec as P

MEMBERS = 64
SWEEPS = 4
LOWER_EDGE = 0.25
UPPER_EDGE = 12.0
HALO = SWEEPS
CX = 64
CY = 64
OBS = 256
TALL = CX + 16
WIDTH = CY * MEMBERS
BLOCKS = WIDTH // 128
EDGE = HALO * MEMBERS
STAT = 17
HALF = MEMBERS // 2
VMEM = pltpu.MemorySpace.VMEM
SMEM = pltpu.MemorySpace.SMEM
F32 = jnp.float32


def power_coeffs():
    angles = np.pi * (np.arange(64) + 0.5) / 64.0
    centre, half = 0.5 * (UPPER_EDGE + LOWER_EDGE), 0.5 * (UPPER_EDGE - LOWER_EDGE)
    nodes = centre + half * np.cos(angles)
    cheb = [2.0 / 64.0 * np.sum(np.cos(k * angles) / nodes) for k in range(SWEEPS + 1)]
    cheb[0] *= 0.5
    mono = np.polynomial.chebyshev.cheb2poly(cheb)
    return [float(v / half**k) for k, v in enumerate(mono)]


COEFFS = power_coeffs()
CENTRE = 0.5 * (UPPER_EDGE + LOWER_EDGE) - 4.0


PAD = 8


def lanes(c):
    return slice(c * 128, (c + 1) * 128)


def stencil_buf(blocks):
    return pltpu.VMEM((blocks * TALL + 2 * PAD, 128), F32)


def rows_of(c, first=0, count=TALL):
    at = PAD + c * TALL + first
    return slice(at, at + count)


def sweep(get, xi, alpha, order, coeff, scale, store, at=0, count=TALL):
    low_half = lax.broadcasted_iota(jnp.int32, (count, 128), 1) < MEMBERS
    turned = {}

    def turn(c):
        if c not in turned:
            turned[c] = pltpu.roll(get(c, at), 64, 1)
        return turned[c]

    for c, lower, upper in order:
        beside = turn(c) + jnp.where(low_half, turn(lower), turn(upper))
        beside = beside + (get(c, at - 1) + get(c, at + 1))
        applied = alpha(c) * get(c, at) - beside
        if scale != 1.0:
            applied = applied * scale
        store(c, coeff * xi(c) + applied)


def spread_kappa(alpha, shifted, count, start):
    upper = (lax.broadcasted_iota(jnp.int32, (TALL, 128), 1) >= MEMBERS).astype(jnp.int32)
    for c in range(count):
        alpha[rows_of(c), :] = jnp.take_along_axis(shifted, upper + (2 * c + start), axis=1)


def rows_kernel(lat_hbm, kap_hbm, to_odd, to_even, kap, sems):
    is_odd = lax.rem(lax.axis_index("gx"), 2) == 1
    fetch = pltpu.make_async_copy(kap_hbm, kap, sems.at[0])
    fetch.start()

    def copies(low, high):
        return (
            pltpu.make_async_copy(lat_hbm.at[0:HALO, :], low.at[:, 0:WIDTH], sems.at[1]),
            pltpu.make_async_copy(lat_hbm.at[CX - HALO : CX, :], high.at[:, 0:WIDTH], sems.at[2]),
        )

    @pl.when(is_odd)
    def _():
        for copy in copies(to_even, to_odd):
            copy.start()

    @pl.when(jnp.logical_not(is_odd))
    def _():
        for copy in copies(to_odd, to_even):
            copy.start()

    fetch.wait()
    blank = jnp.zeros((HALO, 128 - CY), F32)
    low = jnp.concatenate([kap[0:HALO, :], blank], axis=1)
    high = jnp.concatenate([kap[CX - HALO : CX, :], blank], axis=1)
    to_odd[:, WIDTH:] = jnp.where(is_odd, high, low)
    to_even[:, WIDTH:] = jnp.where(is_odd, low, high)
    for copy in copies(to_odd, to_even):
        copy.wait()


class Received:
    def __init__(self, flags, x_odd, x_even, below):
        self.is_odd = jnp.broadcast_to(flags[5:6, :], (HALO, 128)) > 0.5
        self.odd_has, self.even_has = (x_even, x_odd) if below else (x_odd, x_even)

    def __getitem__(self, c):
        return jnp.where(self.is_odd, self.odd_has[:, lanes(c)], self.even_has[:, lanes(c)])


def kappa_rows(dst, kap, xlo, xhi):
    dst[...] = jnp.zeros(dst.shape, F32)
    dst[8 : 8 + CX, 0:CY] = kap[...]
    dst[4:8, :] = xlo[BLOCKS]
    dst[8 + CX : 12 + CX, :] = xhi[BLOCKS]


def cols_kernel(flags, first, last, kap, x_odd, x_even, to_odd, to_even, kext):
    xlo, xhi = Received(flags, x_odd, x_even, True), Received(flags, x_odd, x_even, False)
    kappa_rows(kext, kap, xlo, xhi)
    turned = jnp.transpose(kext[...])
    is_odd = jnp.broadcast_to(flags[4:5, :], (8, 128)) > 0.5
    far = BLOCKS - 2
    for dst, swap in ((to_odd, False), (to_even, True)):

        def pick(low, high):
            low, high = (high, low) if swap else (low, high)
            return jnp.where(is_odd[0 : low.shape[0]], high, low)

        for i in range(2):
            for r in range(0, CX, 8):
                dst[r : r + 8, lanes(i)] = pick(first[r : r + 8, lanes(i)], last[r : r + 8, lanes(i)])
            dst[CX : CX + 4, lanes(i)] = pick(xlo[i], xlo[far + i])
            dst[CX + 4 : CX + 8, lanes(i)] = pick(xhi[i], xhi[far + i])
        columns = pick(turned[0:HALO, :], turned[CY - HALO : CY, :])
        for i in range(HALO):
            r = CX if i < 2 else CX + 7
            dst[r : r + 1, lanes(i % 2)] = columns[i : i + 1]


def keep_rows(dst, flags):
    def store(c, new):
        dst[rows_of(c, 0, 8), :] = new[0:8] * flags[0:1, :]
        dst[rows_of(c, 8, CX), :] = new[8 : 8 + CX]
        dst[rows_of(c, 8 + CX, 8), :] = new[8 + CX : TALL] * flags[1:2, :]

    return store


def into_tiles(tiles, c, new):
    for t in range(CX // 8):
        at = (t * BLOCKS + c) * 8
        tiles[at : at + 8, :] = new[8 * t : 8 * t + 8]


def fill(ext, c, body, xlo, xhi, low, high):
    zero4 = jnp.zeros((4, 128), F32)
    ext[rows_of(c, 0, 4), :] = zero4
    ext[rows_of(c, 4, 4), :] = xlo * low
    ext[rows_of(c, 8, CX), :] = body
    ext[rows_of(c, 8 + CX, 4), :] = xhi * high
    ext[rows_of(c, 12 + CX, 4), :] = zero4


def inner_kernel(flags, lat, kap, x_odd, x_even, val, var, tiles, value, weight, odd, ext, alpha, u3, u2, u1, kext):
    xlo, xhi = Received(flags, x_odd, x_even, True), Received(flags, x_odd, x_even, False)
    for c in range(BLOCKS):
        fill(ext, c, lat[:, lanes(c)], xlo[c], xhi[c], flags[0:1, :], flags[1:2, :])
    kappa_rows(kext, kap, xlo, xhi)
    spread_kappa(alpha, kext[0:TALL, :] - CENTRE, BLOCKS, 0)

    def run(src, depth, step, scale, store, at=0, count=TALL):
        order = [(c, max(c - 1, 0), min(c + 1, BLOCKS - 1)) for c in range(depth, BLOCKS - depth)]
        get = lambda c, shift: src[rows_of(c, shift, count), :]
        xi = lambda c: ext[rows_of(c, at, count), :]
        diag = lambda c: alpha[rows_of(c, at, count), :]
        sweep(get, xi, diag, order, COEFFS[step], scale, store, at, count)

    run(ext, 0, 3, COEFFS[4], keep_rows(u3, flags))
    run(u3, 1, 2, 1.0, keep_rows(u2, flags))
    run(u2, 1, 1, 1.0, keep_rows(u1, flags))
    run(u1, 2, 0, 1.0, lambda c, new: into_tiles(tiles, c, new), 8, CX)

    def column(row):
        pieces = [jnp.transpose(jnp.broadcast_to(row[i : i + 1, :], (128, 128))) for i in range(OBS // 128)]
        return jnp.concatenate(pieces, axis=0)

    value[...] = column(val[0:2, :])
    odd[...] = column(val[2:4, :])
    weight[...] = 1.0 / column(var[0:2, :])


def rim_kernel(
    flags, cell_vmem, y_odd, y_even, value, weight, odd, ext, alpha, u3, u2, u1, held,
    tiles, stat, cell, sem, ext_out, alpha_out, v3, v2, v1, kext, pbuf,
):
    fetch = pltpu.make_async_copy(cell_vmem, cell, sem)
    fetch.start()
    low, high = flags[0:1, :], flags[1:2, :]
    kext[...] = jnp.zeros((128, 128), F32)
    is_odd = jnp.broadcast_to(flags[4:5, :], (CX + 8, 128)) > 0.5
    is_odd = jnp.concatenate([is_odd, is_odd], axis=1)
    for side in range(2):
        lower, upper = (y_even, y_odd) if side == 0 else (y_odd, y_even)
        msg = jnp.where(is_odd, lower[...], upper[...])
        flag = flags[2 + side : 3 + side, :]
        for i in range(HALO):
            r = CX if i < 2 else CX + 7
            kext[i : i + 1, :] = msg[r : r + 1, lanes(i % 2)]
        shifted = jnp.transpose(kext[...])[0:TALL, :] - CENTRE
        upper = (lax.broadcasted_iota(jnp.int32, (TALL, 128), 1) >= MEMBERS).astype(jnp.int32)
        for p in (-2, -1):
            i = p + 2 if side == 0 else -1 - p
            halo = msg[CX : CX + 4, lanes(i)], msg[CX + 4 : CX + 8, lanes(i)]
            fill(ext_out, p + 2, msg[0:CX, lanes(i)] * flag, *halo, low * flag, high * flag)
            alpha_out[rows_of(p + 2), :] = jnp.take_along_axis(shifted, upper + 2 * i, axis=1)

        def local(p):
            return p if side == 0 else BLOCKS - 1 - p

        def run(near, far, mine, first, last, step, scale, store, at=0, count=TALL):
            def pick(p, here, there, ours, start):
                return here[rows_of(p + 2, start, count), :] if p in ours else there[rows_of(local(p), start, count), :]

            get = lambda p, shift: pick(p, near, far, mine, shift)
            xi = lambda p: pick(p, ext_out, ext, (-2, -1), at)
            diag = lambda p: pick(p, alpha_out, alpha, (-2, -1), at)
            order = [(p, max(p - 1, -2), p + 1) for p in range(first, last + 1)]
            if side == 1:
                order = [(p, b, a) for p, a, b in order]
            sweep(get, xi, diag, order, COEFFS[step], scale, store, at, count)

        def keep(dst):
            plain = keep_rows(dst, flags)
            return lambda p, new: plain(p + 2, new * flag if p < 0 else new)

        run(ext_out, ext, (-2, -1), -2, 0, 3, COEFFS[4], keep(v3))
        run(v3, u3, (-2, -1, 0), -1, 0, 2, 1.0, keep(v2))
        run(v2, u2, (-2, -1, 0), -1, 1, 1, 1.0, keep(v1))
        run(v1, u1, (-2, -1, 0, 1), 0, 1, 0, 1.0, lambda p, new: into_tiles(tiles, local(p), new), 8, CX)

    fetch.wait()
    for j in range(OBS):
        pbuf[j : j + 1, :] = tiles[pl.ds(cell[j], 1), :]
    both = pbuf[...]
    lane = lax.broadcasted_iota(jnp.int32, (OBS, 128), 1)
    member = lane < MEMBERS
    predicted = jnp.where(odd[...] > 0.5, pltpu.roll(both, 64, 1), both)
    predicted = jnp.where(member, predicted, 0.0)
    mean = jnp.sum(predicted, axis=1, keepdims=True) * (1.0 / MEMBERS)
    spread = jnp.where(member, predicted - mean, jnp.where(lane == MEMBERS, value[...] - mean, 0.0))
    full = lax.dot_general(
        spread * weight[...],
        spread,
        (((0,), (0,)), ((), ())),
        precision=lax.Precision.HIGHEST,
        preferred_element_type=F32,
    )
    lane = lax.broadcasted_iota(jnp.int32, (HALF, 128), 1)
    row = lax.broadcasted_iota(jnp.int32, (HALF, 128), 0)
    first, second = full[0:HALF], full[HALF:MEMBERS]
    packed = jnp.where(lane >= row, first, pltpu.roll(second, 96, 1))
    folded = jnp.where(lane[0:16] < MEMBERS, packed[0:16], pltpu.roll(packed[16:32], 64, 1))
    diagonal = jnp.sum(jnp.where(lane == row + 96, pltpu.roll(second, 64, 1), 0.0), axis=0, keepdims=True)
    last = jnp.where(lane[0:1] < 96, full[MEMBERS : MEMBERS + 1], diagonal)
    stat[0 : STAT - 1, :] = folded
    stat[STAT - 1 : STAT, :] = last


def eliminate(aug):
    size = 8
    row = lax.broadcasted_iota(jnp.int32, (size, 128), 0)
    for start in range(0, MEMBERS, size):
        columns = [jnp.broadcast_to(aug[:, k : k + 1], (MEMBERS, 128)) for k in range(start, start + size)]
        block = [column[start : start + size] for column in columns]
        pivot_rows = aug[start : start + size]
        for i in range(0, size, 2):
            c0, c1 = block[i], block[i + 1]
            a, b, c, d = c0[i : i + 1], c1[i : i + 1], c0[i + 1 : i + 2], c1[i + 1 : i + 2]
            inverse = 1.0 / (a * d - b * c)

            def clear(m):
                m0, m1 = m[i : i + 1], m[i + 1 : i + 2]
                n0, n1 = (d * m0 - b * m1) * inverse, (a * m1 - c * m0) * inverse
                rest = m - (c0 * n0 + c1 * n1)
                return jnp.where(row == i, n0, jnp.where(row == i + 1, n1, rest))

            block = block[: i + 2] + [clear(m) for m in block[i + 2 :]]
            pivot_rows = clear(pivot_rows)
        pieces = []
        for at in range(0, MEMBERS, size):
            if at == start:
                pieces.append(pivot_rows)
                continue
            terms = [column[at : at + size] * pivot_rows[i : i + 1] for i, column in enumerate(columns)]
            while len(terms) > 1:
                terms = [a + b for a, b in zip(terms[0::2], terms[1::2])]
            pieces.append(aug[at : at + size] - terms[0])
        aug = jnp.concatenate(pieces, axis=0)
    return aug


def split(a):
    hi = a.astype(jnp.bfloat16)
    return hi, (a - hi.astype(F32)).astype(jnp.bfloat16)


def solve_kernel(parts, tiles, weights_out, prior_hbm, total, sem):
    copy = pltpu.make_async_copy(tiles, prior_hbm, sem)
    copy.start()
    for i in range(STAT):
        row = parts[0, i]
        for d in range(1, parts.shape[0]):
            row = row + parts[d, i]
        total[i : i + 1, :] = row
    folded, last = total[0:16, :], total[16:17, :]
    packed = jnp.concatenate([folded, pltpu.roll(folded, 64, 1)], axis=0)
    tall = jnp.concatenate([packed, jnp.zeros((32, 128), F32), jnp.broadcast_to(last, (64, 128))], axis=0)
    turned = jnp.transpose(tall)
    lane = lax.broadcasted_iota(jnp.int32, (HALF, 128), 1)
    row = lax.broadcasted_iota(jnp.int32, (HALF, 128), 0)
    first = jnp.where(lane >= row, packed, turned[0:HALF])
    corner = jnp.where(lane < row + HALF, pltpu.roll(packed, 32, 1), pltpu.roll(turned[0:HALF], 32, 1))
    corner = jnp.where(lane == row + HALF, pltpu.roll(last, 64, 1), corner)
    second = jnp.where(lane < HALF, turned[HALF:MEMBERS], corner)
    gram = jnp.concatenate([first, second], axis=0)

    shape = (MEMBERS, 128)
    row = lax.broadcasted_iota(jnp.int32, shape, 0)
    lane = lax.broadcasted_iota(jnp.int32, shape, 1)
    eye = row == lane
    low = lane < MEMBERS
    square = jnp.where(lane[0:1] == MEMBERS, last, 0.0) * float(MEMBERS)
    trace = jnp.sum(jnp.where(eye, gram, 0.0), axis=0, keepdims=True)
    misfit = jnp.sum(square + trace, axis=1, keepdims=True)
    inflation = 1.0 + misfit / float(MEMBERS * (MEMBERS - 1))
    shift = (MEMBERS - 1) * inflation
    right = turned[0:MEMBERS] - pltpu.roll(gram, 64, 1)
    aug = eliminate(jnp.where(low, gram + jnp.where(eye, shift, 0.0), right))
    gain = aug - jnp.sum(aug, axis=0, keepdims=True) * (1.0 / MEMBERS)
    weights = jnp.concatenate(
        [jnp.where(low, pltpu.roll(gain, 64, 1), 0.0), jnp.where(low, 0.0, gain)], axis=0
    )

    w_hi, w_lo = split(weights)
    weights_out[0:128, 0:128] = w_hi
    weights_out[0:128, 128:256] = w_lo
    weights_out[128:256, 0:128] = w_hi
    weights_out[128:256, 128:256] = jnp.zeros((128, 128), jnp.bfloat16)
    copy.wait()


def update_kernel(lat, weights, out_hbm, out, sems):
    both = weights[...]
    copies = []
    for t in range(CX // 8):
        at = slice(t * 256, (t + 1) * 256)
        x = lat[at, :]
        product = jnp.dot(jnp.concatenate(split(x), axis=1), both, preferred_element_type=F32)
        out[at, :] = x + (product[:, 0:128] + product[:, 128:256])
        copies.append(pltpu.make_async_copy(out.at[at, :], out_hbm.at[at, :], sems.at[t]))
        copies[-1].start()
    for copy in copies:
        copy.wait()


def pairs(axis, first):
    count_x, count_y = lax.axis_size("gx"), lax.axis_size("gy")
    count = count_x if axis == "gx" else count_y
    moves = []
    for x in range(count_x):
        for y in range(count_y):
            at = x if axis == "gx" else y
            to = at + 1 if (at - first) % 2 == 0 else at - 1
            if not 0 <= to < count:
                target = (x, y ^ 1) if axis == "gx" else (x ^ 1, y)
            else:
                target = (to, y) if axis == "gx" else (x, to)
            moves.append((x * count_y + y, target[0] * count_y + target[1]))
    return moves


def exchange(block, axis, first):
    return lax.ppermute(block, ("gx", "gy"), pairs(axis, first))


def arr(*shape):
    return jax.ShapeDtypeStruct(shape, F32)


def buf(*shape):
    return pltpu.VMEM(shape, F32)


def params(mib):
    return pltpu.CompilerParams(vmem_limit_bytes=mib << 20)


def cost(flops, moved):
    return pl.CostEstimate(flops=flops, bytes_accessed=moved, transcendentals=0)


def to_tiles(a):
    return a.reshape(CX // 8, 8, BLOCKS, 128).transpose(0, 2, 1, 3).reshape(CX * BLOCKS, 128)


def from_tiles(a):
    return a.reshape(CX // 8, BLOCKS, 8, 128).transpose(0, 2, 1, 3).reshape(CX, WIDTH)


def per_device(latent, kappa, obs_cell, obs_value, obs_var):
    gx, gy = lax.axis_index("gx"), lax.axis_index("gy")
    last_x, last_y = lax.axis_size("gx") - 1, lax.axis_size("gy") - 1
    states = [gx > 0, gx < last_x, gy > 0, gy < last_y, gy % 2 == 1, gx % 2 == 1]
    flags = jnp.broadcast_to(jnp.stack(states + states[:2]).astype(F32)[:, None], (8, 128))
    odd = (obs_cell & 1).astype(F32)
    obs_x, obs_y = obs_cell >> 6, obs_cell & (CY - 1)
    obs_row = (obs_x & 56) * BLOCKS + (obs_y >> 1) * 8 + (obs_x & 7)
    val = jnp.concatenate([obs_value.reshape(2, 128), odd.reshape(2, 128)], axis=0)
    var = obs_var.reshape(2, 128)
    vmem, anywhere = pl.BlockSpec(memory_space=VMEM), pl.BlockSpec(memory_space=pl.ANY)
    hbm = pl.BlockSpec(memory_space=pltpu.MemorySpace.HBM)

    def part(shape, *at):
        return pl.BlockSpec(shape, lambda i: at)

    to_odd, to_even, kappa = pl.pallas_call(
        rows_kernel,
        out_shape=(arr(HALO, WIDTH + 128),) * 2 + (arr(CX, CY),),
        in_specs=[hbm, hbm],
        out_specs=(vmem,) * 3,
        scratch_shapes=[pltpu.SemaphoreType.DMA((3,))],
        compiler_params=params(4),
        name="rows",
    )(*(pltpu.with_memory_space_constraint(a, pltpu.MemorySpace.HBM) for a in (latent, kappa)))
    x_odd = exchange(to_odd, "gx", 1)
    x_even = exchange(to_even, "gx", 0)

    whole = part((HALO, WIDTH + 128), 0, 0)
    to_odd, to_even = pl.pallas_call(
        cols_kernel,
        grid=(1,),
        out_shape=(arr(CX + 8, EDGE),) * 2,
        in_specs=[part((8, 128), 0, 0), part((CX, EDGE), 0, 0), part((CX, EDGE), 0, WIDTH // EDGE - 1), part((CX, CY), 0, 0), whole, whole],
        out_specs=(part((CX + 8, EDGE), 0, 0),) * 2,
        scratch_shapes=[buf(128, 128)],
        compiler_params=params(4),
        name="cols",
    )(flags, latent, latent, kappa, x_odd, x_even)
    y_odd = exchange(to_odd, "gy", 1)
    y_even = exchange(to_even, "gy", 0)

    field = arr(BLOCKS * TALL + 2 * PAD, 128)
    tiles, *rest = pl.pallas_call(
        inner_kernel,
        out_shape=(arr(CX * BLOCKS, 128),) + (arr(OBS, 128),) * 3 + (field,) * 5,
        in_specs=[vmem] * 7,
        out_specs=(vmem,) * 9,
        scratch_shapes=[buf(128, 128)],
        compiler_params=params(12),
        cost_estimate=cost(20_000_000, 12_000_000),
        name="inner",
    )(flags, latent, kappa, x_odd, x_even, val, var)

    tiles, stat = pl.pallas_call(
        rim_kernel,
        out_shape=(arr(CX * BLOCKS, 128), arr(STAT, 128)),
        in_specs=[vmem, anywhere] + [vmem] * 11,
        out_specs=(vmem, vmem),
        scratch_shapes=[pltpu.SMEM((OBS,), jnp.int32), pltpu.SemaphoreType.DMA]
        + [stencil_buf(4)] * 5
        + [buf(128, 128), buf(OBS, 128)],
        input_output_aliases={12: 0},
        compiler_params=params(12),
        name="rim",
    )(flags, obs_row, y_odd, y_even, *rest, tiles)

    stat = stat[:, None, :]
    stat = stat + exchange(stat, "gx", 0)
    count = lax.axis_size("gx")
    groups = [list(range(i, count, 2)) for i in range(2)]
    parts = jnp.broadcast_to(stat[None], (count // 2,) + stat.shape)
    parts = lax.all_to_all(parts, "gx", 0, 0, axis_index_groups=groups)
    stat = jnp.sum(parts, axis=0)
    width = lax.axis_size("gy")
    parts = lax.all_to_all(jnp.broadcast_to(stat[None], (width,) + stat.shape), "gy", 0, 0)

    weights, prior = pl.pallas_call(
        solve_kernel,
        out_shape=(jax.ShapeDtypeStruct((256, 256), jnp.bfloat16), arr(CX * BLOCKS, 128)),
        in_specs=[vmem] * 2,
        out_specs=(vmem, anywhere),
        scratch_shapes=[buf(24, 128), pltpu.SemaphoreType.DMA],
        compiler_params=params(12),
        name="solve",
    )(parts, tiles)
    latent_new = pl.pallas_call(
        update_kernel,
        out_shape=arr(CX * BLOCKS, 128),
        in_specs=[vmem] * 2,
        out_specs=anywhere,
        scratch_shapes=[buf(CX * BLOCKS, 128), pltpu.SemaphoreType.DMA((CX // 8,))],
        compiler_params=params(12),
        name="update",
    )(to_tiles(latent), weights)
    return (from_tiles(latent_new), from_tiles(prior))


def solution(mesh):
    placed = (P("gx", "gy"), P("gx", "gy"), P(("gx", "gy")), P(("gx", "gy")), P(("gx", "gy")))
    return jax.shard_map(
        per_device,
        mesh=mesh,
        in_specs=placed,
        out_specs=(P("gx", "gy"), P("gx", "gy")),
        check_vma=False,
    )
```

```python
import jax
import jax.numpy as jnp
import numpy as np
from jax import lax
from jax.experimental import pallas as pl
from jax.experimental.pallas import tpu as pltpu
from jax.sharding import PartitionSpec as P

MEMBERS = 64
SWEEPS = 4
LOWER_EDGE = 0.25
UPPER_EDGE = 12.0
HALO = SWEEPS
CX = 64
CY = 64
OBS = 256
TALL = CX + 16
WIDTH = CY * MEMBERS
BLOCKS = WIDTH // 128
EDGE = HALO * MEMBERS
STAT = 17
HALF = MEMBERS // 2
VMEM = pltpu.MemorySpace.VMEM
SMEM = pltpu.MemorySpace.SMEM
F32 = jnp.float32


def power_coeffs():
    angles = np.pi * (np.arange(64) + 0.5) / 64.0
    centre, half = 0.5 * (UPPER_EDGE + LOWER_EDGE), 0.5 * (UPPER_EDGE - LOWER_EDGE)
    nodes = centre + half * np.cos(angles)
    cheb = [2.0 / 64.0 * np.sum(np.cos(k * angles) / nodes) for k in range(SWEEPS + 1)]
    cheb[0] *= 0.5
    mono = np.polynomial.chebyshev.cheb2poly(cheb)
    return [float(v / half**k) for k, v in enumerate(mono)]


COEFFS = power_coeffs()
CENTRE = 0.5 * (UPPER_EDGE + LOWER_EDGE) - 4.0


PAD = 8


def lanes(c):
    return slice(c * 128, (c + 1) * 128)


def stencil_buf(blocks):
    return pltpu.VMEM((blocks * TALL + 2 * PAD, 128), F32)


def rows_of(c, first=0, count=TALL):
    at = PAD + c * TALL + first
    return slice(at, at + count)


def sweep(get, xi, alpha, order, coeff, scale, store, at=0, count=TALL):
    low_half = lax.broadcasted_iota(jnp.int32, (count, 128), 1) < MEMBERS
    turned = {}

    def turn(c):
        if c not in turned:
            turned[c] = pltpu.roll(get(c, at), 64, 1)
        return turned[c]

    for c, lower, upper in order:
        beside = turn(c) + jnp.where(low_half, turn(lower), turn(upper))
        beside = beside + (get(c, at - 1) + get(c, at + 1))
        applied = alpha(c) * get(c, at) - beside
        if scale != 1.0:
            applied = applied * scale
        store(c, coeff * xi(c) + applied)


def spread_kappa(alpha, shifted, count, start):
    upper = (lax.broadcasted_iota(jnp.int32, (TALL, 128), 1) >= MEMBERS).astype(jnp.int32)
    for c in range(count):
        alpha[rows_of(c), :] = jnp.take_along_axis(shifted, upper + (2 * c + start), axis=1)


def rows_kernel(lat_hbm, kap_hbm, to_odd, to_even, kap, sems):
    is_odd = lax.rem(lax.axis_index("gx"), 2) == 1
    fetch = pltpu.make_async_copy(kap_hbm, kap, sems.at[0])
    fetch.start()

    def copies(low, high):
        return (
            pltpu.make_async_copy(lat_hbm.at[0:HALO, :], low.at[:, 0:WIDTH], sems.at[1]),
            pltpu.make_async_copy(lat_hbm.at[CX - HALO : CX, :], high.at[:, 0:WIDTH], sems.at[2]),
        )

    @pl.when(is_odd)
    def _():
        for copy in copies(to_even, to_odd):
            copy.start()

    @pl.when(jnp.logical_not(is_odd))
    def _():
        for copy in copies(to_odd, to_even):
            copy.start()

    fetch.wait()
    blank = jnp.zeros((HALO, 128 - CY), F32)
    low = jnp.concatenate([kap[0:HALO, :], blank], axis=1)
    high = jnp.concatenate([kap[CX - HALO : CX, :], blank], axis=1)
    to_odd[:, WIDTH:] = jnp.where(is_odd, high, low)
    to_even[:, WIDTH:] = jnp.where(is_odd, low, high)
    for copy in copies(to_odd, to_even):
        copy.wait()


class Received:
    def __init__(self, flags, x_odd, x_even, below):
        self.is_odd = jnp.broadcast_to(flags[5:6, :], (HALO, 128)) > 0.5
        self.odd_has, self.even_has = (x_even, x_odd) if below else (x_odd, x_even)

    def __getitem__(self, c):
        return jnp.where(self.is_odd, self.odd_has[:, lanes(c)], self.even_has[:, lanes(c)])


def kappa_rows(dst, kap, xlo, xhi):
    dst[...] = jnp.zeros(dst.shape, F32)
    dst[8 : 8 + CX, 0:CY] = kap[...]
    dst[4:8, :] = xlo[BLOCKS]
    dst[8 + CX : 12 + CX, :] = xhi[BLOCKS]


def cols_kernel(flags, first, last, kap, x_odd, x_even, to_odd, to_even, kext):
    xlo, xhi = Received(flags, x_odd, x_even, True), Received(flags, x_odd, x_even, False)
    kappa_rows(kext, kap, xlo, xhi)
    turned = jnp.transpose(kext[...])
    is_odd = jnp.broadcast_to(flags[4:5, :], (8, 128)) > 0.5
    far = BLOCKS - 2
    for dst, swap in ((to_odd, False), (to_even, True)):

        def pick(low, high):
            low, high = (high, low) if swap else (low, high)
            return jnp.where(is_odd[0 : low.shape[0]], high, low)

        for i in range(2):
            for r in range(0, CX, 8):
                dst[r : r + 8, lanes(i)] = pick(first[r : r + 8, lanes(i)], last[r : r + 8, lanes(i)])
            dst[CX : CX + 4, lanes(i)] = pick(xlo[i], xlo[far + i])
            dst[CX + 4 : CX + 8, lanes(i)] = pick(xhi[i], xhi[far + i])
        columns = pick(turned[0:HALO, :], turned[CY - HALO : CY, :])
        for i in range(HALO):
            r = CX if i < 2 else CX + 7
            dst[r : r + 1, lanes(i % 2)] = columns[i : i + 1]


def keep_rows(dst, flags):
    def store(c, new):
        dst[rows_of(c, 0, 8), :] = new[0:8] * flags[0:1, :]
        dst[rows_of(c, 8, CX), :] = new[8 : 8 + CX]
        dst[rows_of(c, 8 + CX, 8), :] = new[8 + CX : TALL] * flags[1:2, :]

    return store


def into_tiles(tiles, c, new):
    for t in range(CX // 8):
        at = (t * BLOCKS + c) * 8
        tiles[at : at + 8, :] = new[8 * t : 8 * t + 8]


def fill(ext, c, body, xlo, xhi, low, high):
    zero4 = jnp.zeros((4, 128), F32)
    ext[rows_of(c, 0, 4), :] = zero4
    ext[rows_of(c, 4, 4), :] = xlo * low
    ext[rows_of(c, 8, CX), :] = body
    ext[rows_of(c, 8 + CX, 4), :] = xhi * high
    ext[rows_of(c, 12 + CX, 4), :] = zero4


def inner_kernel(flags, lat, kap, x_odd, x_even, val, var, tiles, value, weight, odd, ext, alpha, u3, u2, u1, kext):
    xlo, xhi = Received(flags, x_odd, x_even, True), Received(flags, x_odd, x_even, False)
    for c in range(BLOCKS):
        fill(ext, c, lat[:, lanes(c)], xlo[c], xhi[c], flags[0:1, :], flags[1:2, :])
    kappa_rows(kext, kap, xlo, xhi)
    spread_kappa(alpha, kext[0:TALL, :] - CENTRE, BLOCKS, 0)

    def run(src, depth, step, scale, store, at=0, count=TALL):
        order = [(c, max(c - 1, 0), min(c + 1, BLOCKS - 1)) for c in range(depth, BLOCKS - depth)]
        get = lambda c, shift: src[rows_of(c, shift, count), :]
        xi = lambda c: ext[rows_of(c, at, count), :]
        diag = lambda c: alpha[rows_of(c, at, count), :]
        sweep(get, xi, diag, order, COEFFS[step], scale, store, at, count)

    run(ext, 0, 3, COEFFS[4], keep_rows(u3, flags))
    run(u3, 1, 2, 1.0, keep_rows(u2, flags))
    run(u2, 1, 1, 1.0, keep_rows(u1, flags))
    run(u1, 2, 0, 1.0, lambda c, new: into_tiles(tiles, c, new), 8, CX)

    def column(row):
        pieces = [jnp.transpose(jnp.broadcast_to(row[i : i + 1, :], (128, 128))) for i in range(OBS // 128)]
        return jnp.concatenate(pieces, axis=0)

    value[...] = column(val[0:2, :])
    odd[...] = column(val[2:4, :])
    weight[...] = 1.0 / column(var[0:2, :])


def rim_kernel(
    flags, cell_vmem, y_odd, y_even, value, weight, odd, ext, alpha, u3, u2, u1, held,
    tiles, stat, cell, sem, ext_out, alpha_out, v3, v2, v1, kext, pbuf,
):
    fetch = pltpu.make_async_copy(cell_vmem, cell, sem)
    fetch.start()
    low, high = flags[0:1, :], flags[1:2, :]
    kext[...] = jnp.zeros((128, 128), F32)
    is_odd = jnp.broadcast_to(flags[4:5, :], (CX + 8, 128)) > 0.5
    is_odd = jnp.concatenate([is_odd, is_odd], axis=1)
    sides = ((y_even, y_odd), (y_odd, y_even))
    for side, (lower, upper) in enumerate(sides):
        for i in range(HALO):
            r = CX if i < 2 else CX + 7
            at = slice(r, r + 1), lanes(i % 2)
            row = side * HALO + i
            kext[row : row + 1, :] = jnp.where(is_odd[0:1, 0:128], lower[at], upper[at])
    shifted = jnp.transpose(kext[...])[0:TALL, :] - CENTRE
    for side, (lower, upper) in enumerate(sides):
        msg = jnp.where(is_odd, lower[...], upper[...])
        flag = flags[2 + side : 3 + side, :]
        half = (lax.broadcasted_iota(jnp.int32, (TALL, 128), 1) >= MEMBERS).astype(jnp.int32)
        for p in (-2, -1):
            i = p + 2 if side == 0 else -1 - p
            halo = msg[CX : CX + 4, lanes(i)], msg[CX + 4 : CX + 8, lanes(i)]
            fill(ext_out, p + 2, msg[0:CX, lanes(i)] * flag, *halo, low * flag, high * flag)
            alpha_out[rows_of(p + 2), :] = jnp.take_along_axis(shifted, half + (side * HALO + 2 * i), axis=1)

        def local(p):
            return p if side == 0 else BLOCKS - 1 - p

        def run(near, far, mine, first, last, step, scale, store, at=0, count=TALL):
            def pick(p, here, there, ours, start):
                return here[rows_of(p + 2, start, count), :] if p in ours else there[rows_of(local(p), start, count), :]

            get = lambda p, shift: pick(p, near, far, mine, shift)
            xi = lambda p: pick(p, ext_out, ext, (-2, -1), at)
            diag = lambda p: pick(p, alpha_out, alpha, (-2, -1), at)
            order = [(p, max(p - 1, -2), p + 1) for p in range(first, last + 1)]
            if side == 1:
                order = [(p, b, a) for p, a, b in order]
            sweep(get, xi, diag, order, COEFFS[step], scale, store, at, count)

        def keep(dst):
            plain = keep_rows(dst, flags)
            return lambda p, new: plain(p + 2, new * flag if p < 0 else new)

        run(ext_out, ext, (-2, -1), -2, 0, 3, COEFFS[4], keep(v3))
        run(v3, u3, (-2, -1, 0), -1, 0, 2, 1.0, keep(v2))
        run(v2, u2, (-2, -1, 0), -1, 1, 1, 1.0, keep(v1))
        run(v1, u1, (-2, -1, 0, 1), 0, 1, 0, 1.0, lambda p, new: into_tiles(tiles, local(p), new), 8, CX)

    fetch.wait()
    for j in range(OBS):
        pbuf[j : j + 1, :] = tiles[pl.ds(cell[j], 1), :]
    both = pbuf[...]
    lane = lax.broadcasted_iota(jnp.int32, (OBS, 128), 1)
    member = lane < MEMBERS
    predicted = jnp.where(odd[...] > 0.5, pltpu.roll(both, 64, 1), both)
    predicted = jnp.where(member, predicted, 0.0)
    mean = jnp.sum(predicted, axis=1, keepdims=True) * (1.0 / MEMBERS)
    spread = jnp.where(member, predicted - mean, jnp.where(lane == MEMBERS, value[...] - mean, 0.0))
    full = lax.dot_general(
        spread * weight[...],
        spread,
        (((0,), (0,)), ((), ())),
        precision=lax.Precision.HIGHEST,
        preferred_element_type=F32,
    )
    lane = lax.broadcasted_iota(jnp.int32, (HALF, 128), 1)
    row = lax.broadcasted_iota(jnp.int32, (HALF, 128), 0)
    first, second = full[0:HALF], full[HALF:MEMBERS]
    packed = jnp.where(lane >= row, first, pltpu.roll(second, 96, 1))
    folded = jnp.where(lane[0:16] < MEMBERS, packed[0:16], pltpu.roll(packed[16:32], 64, 1))
    diagonal = jnp.sum(jnp.where(lane == row + 96, pltpu.roll(second, 64, 1), 0.0), axis=0, keepdims=True)
    last = jnp.where(lane[0:1] < 96, full[MEMBERS : MEMBERS + 1], diagonal)
    stat[0 : STAT - 1, :] = folded
    stat[STAT - 1 : STAT, :] = last


def eliminate(aug):
    size = 8
    row = lax.broadcasted_iota(jnp.int32, (size, 128), 0)
    for start in range(0, MEMBERS, size):
        columns = [jnp.broadcast_to(aug[:, k : k + 1], (MEMBERS, 128)) for k in range(start, start + size)]
        block = [column[start : start + size] for column in columns]
        pivot_rows = aug[start : start + size]
        for i in range(0, size, 2):
            c0, c1 = block[i], block[i + 1]
            a, b, c, d = c0[i : i + 1], c1[i : i + 1], c0[i + 1 : i + 2], c1[i + 1 : i + 2]
            inverse = 1.0 / (a * d - b * c)

            def clear(m):
                m0, m1 = m[i : i + 1], m[i + 1 : i + 2]
                n0, n1 = (d * m0 - b * m1) * inverse, (a * m1 - c * m0) * inverse
                rest = m - (c0 * n0 + c1 * n1)
                return jnp.where(row == i, n0, jnp.where(row == i + 1, n1, rest))

            block = block[: i + 2] + [clear(m) for m in block[i + 2 :]]
            pivot_rows = clear(pivot_rows)
        pieces = []
        for at in range(0, MEMBERS, size):
            if at == start:
                pieces.append(pivot_rows)
                continue
            terms = [column[at : at + size] * pivot_rows[i : i + 1] for i, column in enumerate(columns)]
            while len(terms) > 1:
                terms = [a + b for a, b in zip(terms[0::2], terms[1::2])]
            pieces.append(aug[at : at + size] - terms[0])
        aug = jnp.concatenate(pieces, axis=0)
    return aug


def split(a):
    hi = a.astype(jnp.bfloat16)
    return hi, (a - hi.astype(F32)).astype(jnp.bfloat16)


def solve_kernel(parts, tiles, weights_out, prior_hbm, total, sem):
    copy = pltpu.make_async_copy(tiles, prior_hbm, sem)
    copy.start()
    for i in range(STAT):
        row = parts[0, i]
        for d in range(1, parts.shape[0]):
            row = row + parts[d, i]
        total[i : i + 1, :] = row
    folded, last = total[0:16, :], total[16:17, :]
    packed = jnp.concatenate([folded, pltpu.roll(folded, 64, 1)], axis=0)
    tall = jnp.concatenate([packed, jnp.zeros((32, 128), F32), jnp.broadcast_to(last, (64, 128))], axis=0)
    turned = jnp.transpose(tall)
    lane = lax.broadcasted_iota(jnp.int32, (HALF, 128), 1)
    row = lax.broadcasted_iota(jnp.int32, (HALF, 128), 0)
    first = jnp.where(lane >= row, packed, turned[0:HALF])
    corner = jnp.where(lane < row + HALF, pltpu.roll(packed, 32, 1), pltpu.roll(turned[0:HALF], 32, 1))
    corner = jnp.where(lane == row + HALF, pltpu.roll(last, 64, 1), corner)
    second = jnp.where(lane < HALF, turned[HALF:MEMBERS], corner)
    gram = jnp.concatenate([first, second], axis=0)

    shape = (MEMBERS, 128)
    row = lax.broadcasted_iota(jnp.int32, shape, 0)
    lane = lax.broadcasted_iota(jnp.int32, shape, 1)
    eye = row == lane
    low = lane < MEMBERS
    square = jnp.where(lane[0:1] == MEMBERS, last, 0.0) * float(MEMBERS)
    trace = jnp.sum(jnp.where(eye, gram, 0.0), axis=0, keepdims=True)
    misfit = jnp.sum(square + trace, axis=1, keepdims=True)
    inflation = 1.0 + misfit / float(MEMBERS * (MEMBERS - 1))
    shift = (MEMBERS - 1) * inflation
    right = turned[0:MEMBERS] - pltpu.roll(gram, 64, 1)
    aug = eliminate(jnp.where(low, gram + jnp.where(eye, shift, 0.0), right))
    gain = aug - jnp.sum(aug, axis=0, keepdims=True) * (1.0 / MEMBERS)
    weights = jnp.concatenate(
        [jnp.where(low, pltpu.roll(gain, 64, 1), 0.0), jnp.where(low, 0.0, gain)], axis=0
    )

    w_hi, w_lo = split(weights)
    weights_out[0:128, 0:128] = w_hi
    weights_out[0:128, 128:256] = w_lo
    weights_out[128:256, 0:128] = w_hi
    weights_out[128:256, 128:256] = jnp.zeros((128, 128), jnp.bfloat16)
    copy.wait()


def update_kernel(lat, weights, out_hbm, out, sems):
    both = weights[...]
    copies = []
    for t in range(CX // 8):
        at = slice(t * 256, (t + 1) * 256)
        x = lat[at, :]
        product = jnp.dot(jnp.concatenate(split(x), axis=1), both, preferred_element_type=F32)
        out[at, :] = x + (product[:, 0:128] + product[:, 128:256])
        copies.append(pltpu.make_async_copy(out.at[at, :], out_hbm.at[at, :], sems.at[t]))
        copies[-1].start()
    for copy in copies:
        copy.wait()


def pairs(axis, first):
    count_x, count_y = lax.axis_size("gx"), lax.axis_size("gy")
    count = count_x if axis == "gx" else count_y
    moves = []
    for x in range(count_x):
        for y in range(count_y):
            at = x if axis == "gx" else y
            to = at + 1 if (at - first) % 2 == 0 else at - 1
            if not 0 <= to < count:
                target = (x, y ^ 1) if axis == "gx" else (x ^ 1, y)
            else:
                target = (to, y) if axis == "gx" else (x, to)
            moves.append((x * count_y + y, target[0] * count_y + target[1]))
    return moves


def exchange(block, axis, first):
    return lax.ppermute(block, ("gx", "gy"), pairs(axis, first))


def arr(*shape):
    return jax.ShapeDtypeStruct(shape, F32)


def buf(*shape):
    return pltpu.VMEM(shape, F32)


def params(mib):
    return pltpu.CompilerParams(vmem_limit_bytes=mib << 20)


def cost(flops, moved):
    return pl.CostEstimate(flops=flops, bytes_accessed=moved, transcendentals=0)


def to_tiles(a):
    return a.reshape(CX // 8, 8, BLOCKS, 128).transpose(0, 2, 1, 3).reshape(CX * BLOCKS, 128)


def from_tiles(a):
    return a.reshape(CX // 8, BLOCKS, 8, 128).transpose(0, 2, 1, 3).reshape(CX, WIDTH)


def per_device(latent, kappa, obs_cell, obs_value, obs_var):
    gx, gy = lax.axis_index("gx"), lax.axis_index("gy")
    last_x, last_y = lax.axis_size("gx") - 1, lax.axis_size("gy") - 1
    states = [gx > 0, gx < last_x, gy > 0, gy < last_y, gy % 2 == 1, gx % 2 == 1]
    flags = jnp.broadcast_to(jnp.stack(states + states[:2]).astype(F32)[:, None], (8, 128))
    odd = (obs_cell & 1).astype(F32)
    obs_x, obs_y = obs_cell >> 6, obs_cell & (CY - 1)
    obs_row = (obs_x & 56) * BLOCKS + (obs_y >> 1) * 8 + (obs_x & 7)
    val = jnp.concatenate([obs_value.reshape(2, 128), odd.reshape(2, 128)], axis=0)
    var = obs_var.reshape(2, 128)
    vmem, anywhere = pl.BlockSpec(memory_space=VMEM), pl.BlockSpec(memory_space=pl.ANY)
    hbm = pl.BlockSpec(memory_space=pltpu.MemorySpace.HBM)

    def part(shape, *at):
        return pl.BlockSpec(shape, lambda i: at)

    to_odd, to_even, kappa = pl.pallas_call(
        rows_kernel,
        out_shape=(arr(HALO, WIDTH + 128),) * 2 + (arr(CX, CY),),
        in_specs=[hbm, hbm],
        out_specs=(vmem,) * 3,
        scratch_shapes=[pltpu.SemaphoreType.DMA((3,))],
        compiler_params=params(4),
        name="rows",
    )(*(pltpu.with_memory_space_constraint(a, pltpu.MemorySpace.HBM) for a in (latent, kappa)))
    x_odd = exchange(to_odd, "gx", 1)
    x_even = exchange(to_even, "gx", 0)

    whole = part((HALO, WIDTH + 128), 0, 0)
    to_odd, to_even = pl.pallas_call(
        cols_kernel,
        grid=(1,),
        out_shape=(arr(CX + 8, EDGE),) * 2,
        in_specs=[part((8, 128), 0, 0), part((CX, EDGE), 0, 0), part((CX, EDGE), 0, WIDTH // EDGE - 1), part((CX, CY), 0, 0), whole, whole],
        out_specs=(part((CX + 8, EDGE), 0, 0),) * 2,
        scratch_shapes=[buf(128, 128)],
        compiler_params=params(4),
        name="cols",
    )(flags, latent, latent, kappa, x_odd, x_even)
    y_odd = exchange(to_odd, "gy", 1)
    y_even = exchange(to_even, "gy", 0)

    field = arr(BLOCKS * TALL + 2 * PAD, 128)
    tiles, *rest = pl.pallas_call(
        inner_kernel,
        out_shape=(arr(CX * BLOCKS, 128),) + (arr(OBS, 128),) * 3 + (field,) * 5,
        in_specs=[vmem] * 7,
        out_specs=(vmem,) * 9,
        scratch_shapes=[buf(128, 128)],
        compiler_params=params(12),
        cost_estimate=cost(20_000_000, 12_000_000),
        name="inner",
    )(flags, latent, kappa, x_odd, x_even, val, var)

    tiles, stat = pl.pallas_call(
        rim_kernel,
        out_shape=(arr(CX * BLOCKS, 128), arr(STAT, 128)),
        in_specs=[vmem, anywhere] + [vmem] * 11,
        out_specs=(vmem, vmem),
        scratch_shapes=[pltpu.SMEM((OBS,), jnp.int32), pltpu.SemaphoreType.DMA]
        + [stencil_buf(4)] * 5
        + [buf(128, 128), buf(OBS, 128)],
        input_output_aliases={12: 0},
        compiler_params=params(12),
        name="rim",
    )(flags, obs_row, y_odd, y_even, *rest, tiles)

    stat = stat[:, None, :]
    stat = stat + exchange(stat, "gx", 0)
    count = lax.axis_size("gx")
    groups = [list(range(i, count, 2)) for i in range(2)]
    parts = jnp.broadcast_to(stat[None], (count // 2,) + stat.shape)
    parts = lax.all_to_all(parts, "gx", 0, 0, axis_index_groups=groups)
    stat = jnp.sum(parts, axis=0)
    width = lax.axis_size("gy")
    parts = lax.all_to_all(jnp.broadcast_to(stat[None], (width,) + stat.shape), "gy", 0, 0)

    weights, prior = pl.pallas_call(
        solve_kernel,
        out_shape=(jax.ShapeDtypeStruct((256, 256), jnp.bfloat16), arr(CX * BLOCKS, 128)),
        in_specs=[vmem] * 2,
        out_specs=(vmem, anywhere),
        scratch_shapes=[buf(24, 128), pltpu.SemaphoreType.DMA],
        compiler_params=params(12),
        name="solve",
    )(parts, tiles)
    latent_new = pl.pallas_call(
        update_kernel,
        out_shape=arr(CX * BLOCKS, 128),
        in_specs=[vmem] * 2,
        out_specs=anywhere,
        scratch_shapes=[buf(CX * BLOCKS, 128), pltpu.SemaphoreType.DMA((CX // 8,))],
        compiler_params=params(12),
        name="update",
    )(to_tiles(latent), weights)
    return (from_tiles(latent_new), from_tiles(prior))


def solution(mesh):
    placed = (P("gx", "gy"), P("gx", "gy"), P(("gx", "gy")), P(("gx", "gy")), P(("gx", "gy")))
    return jax.shard_map(
        per_device,
        mesh=mesh,
        in_specs=placed,
        out_specs=(P("gx", "gy"), P("gx", "gy")),
        check_vma=False,
    )
```
